128 devices in a mesh: lon: 32 (over x, y, z_lo), lat: 4 (over z_hi, core).
Axes of the slice: x: 4, y: 4, z: 4 (z_hi: 2, z_lo: 2; z = z_hi * 2 + z_lo), core: 2. Of those that a mesh axis runs over, the one named last changes fastest.
Arguments:
- adjoint_in: float32 [72, 2, 256, 4096], P(None, None, 'lat', 'lon'), may hold values from -6 to 6
- courant: float32 [2, 72, 256, 4096], P(None, None, 'lat', 'lon'), may hold values from -0.5 to 0.5
- mixing: float32 [71, 256, 4096], P(None, 'lat', 'lon'), may hold values from 0.05 to 4
- kernel_blocks: float32 [72, 262144], P(None, ('lon', 'lat')), may hold values from -6 to 6
- sounding_dest: int32 [262144, 1], P(('lon', 'lat')), may hold values from 0 to 127; in each aligned block of 2048 rows (0 to 2047, 2048 to 4095, ...) at most 64 rows name the same one
- sounding_cell: int32 [262144], P(('lon', 'lat')), may hold values from 0 to 16383
Outputs:
- adjoint_out: float32 [72, 2, 256, 4096], P(None, None, 'lat', 'lon')
- flux_grad: float32 [2, 256, 4096], P(None, 'lat', 'lon')
The draws below stay inside these ranges and needn't reach their ends.
Inputs may be any that keep to these rules, and one draw needn't show every extreme that they name: `sounding_dest`: in each device's block of 2048 soundings at most 64 name one owner device, and some owner gets exactly 64 of them.
All inputs are finite; a program needn't handle non-finite values.
Results may differ from the reference program's by a relative error of at most 0.00002.
Values sent between devices are 32-bit elements; how exact they have to be, the bound alone decides.
A program may use at most 192 MiB of HBM per device.

```python
import math
import jax
import jax.numpy as jnp
import numpy as np

LEVELS = 72
TRACERS = 2
BAND = 64
TILE = 128
SOUND_DEV = 2048
CAP = 64
NLAT = 256
NLON = 4096
SOUNDS = 262144
N_LON = 32
N_LAT = 4


def place_ends(entries, rng, least, largest):
    shape = entries.shape
    spot = [jax.random.randint(jax.random.fold_in(rng, axis), (), 0, shape[axis]) for axis in range(len(shape))]
    entries = entries.at[tuple(spot)].set(least)
    longest = shape.index(max(shape))
    spot[longest] = (spot[longest] + 1) % shape[longest]
    return entries.at[tuple(spot)].set(largest)


def block_levels(own_key, shape, split, smallest, largest):
    factor_of = 1.0
    for axis_at, parts in split:
        steps = jax.random.uniform(jax.random.fold_in(jax.random.fold_in(own_key, 6), axis_at), (parts,), jnp.float32, smallest / len(split), largest / len(split))
        factor_of = factor_of * jnp.repeat(jnp.exp(steps), shape[axis_at] // parts).reshape((-1,) + (1,) * (len(shape) - 1 - axis_at))
    return factor_of


def routed_block(key, own, number, rows, amount, top, limit, lean):
    sequence = jax.random.permutation(key, amount)
    packed, usual = shares(amount, rows * top, limit, lean, True), shares(amount, rows * top, limit, lean, False)
    places = jnp.arange(amount)

    def named(tallies, rotation):
        used = int((tallies > 0).sum())
        fixed = max(1, used // 4)
        moved = fixed + (places - fixed + rotation * (used - fixed)) % max(1, amount - fixed)
        return jnp.zeros((amount,), jnp.int32).at[sequence[jnp.where(places < fixed, places, moved)]].set(jnp.asarray(tallies, jnp.int32))

    tallies = jnp.where(number % 4 == 0, named(packed, number // 4), named(usual, number - number // 4 - 1))
    mixed = jax.random.permutation(jax.random.fold_in(own, 3), amount)
    donor, taker = mixed[0:amount // 2 * 2:2], mixed[1:amount // 2 * 2:2]
    slack = jnp.minimum(tallies[donor] - 1, limit - tallies[taker]) // 2
    slack = jnp.where((donor == sequence[0]) | (taker == sequence[0]) | (tallies[taker] == 0), 0, jnp.maximum(slack, 0))
    moved = jax.random.randint(jax.random.fold_in(own, 4), (amount // 2,), 0, 1 << 20) % (slack + 1)
    tallies = tallies.at[donor].add(-moved).at[taker].add(moved)
    items = jnp.searchsorted(jnp.cumsum(tallies), jnp.arange(rows * top), side="right").astype(jnp.int32)
    table = items.reshape(top, rows).T
    table = table[jax.random.permutation(jax.random.fold_in(own, 1), rows)]
    rotation = jax.random.randint(jax.random.fold_in(own, 2), (rows, 1), 0, top)
    return jnp.take_along_axis(table, (jnp.arange(top)[None, :] + rotation) % top, axis=1)


def shares(count, total, limit, skew, full):
    weights = [(1 << 20) // math.isqrt(rank ** skew) + 1 for rank in range(1, count + 1)]
    largest = limit if full else min(limit, max(-(-total // count), total * weights[0] // sum(weights)))
    least = 1 if total - largest >= count - 1 else 0
    counts, spare = [largest] + [least] * (count - 1), total - largest - least * (count - 1)
    while spare > 0:
        free = [i for i in range(1, count) if counts[i] < largest] or [i for i in range(1, count) if counts[i] < limit]
        whole, left = sum([weights[i] for i in free]), spare
        for i in free:
            more = min(limit - counts[i], max(1, left * weights[i] // whole), spare)
            counts[i] = counts[i] + more
            spare = spare - more
    return np.array(counts)


def normal_values(stream_key, shape, deviation, reach, shards=(), dtype=jnp.bfloat16):
    array = deviation * jax.random.normal(stream_key, shape, jnp.float32)
    if shards:
        array = array * block_levels(stream_key, shape, shards, -0.22, 0.18)
    return jnp.clip(array, -reach, reach).astype(dtype)


def setup_inputs(seed: int = 0) -> dict:
    streams_of = jax.random.split(jax.random.key(seed), 7)
    adjoint_in = normal_values(streams_of[0], (LEVELS, TRACERS, NLAT, NLON), 1.0, 6.0, ((2, 4), (3, 32)), jnp.float32)
    courant = jnp.clip(jax.random.uniform(streams_of[1], (2, LEVELS, NLAT, NLON), jnp.float32, -0.5, 0.5) * block_levels(streams_of[1], (2, LEVELS, NLAT, NLON), ((2, 4), (3, 32)), -0.4, 0.0), -0.5, 0.5)
    mixing = jnp.clip(jnp.exp(math.log(4.0) - 4.3820266 * jax.random.uniform(streams_of[2], (LEVELS - 1, NLAT, NLON), jnp.float32) ** block_levels(streams_of[2], (LEVELS - 1, NLAT, NLON), ((1, 4), (2, 32)), -0.2, 0.2)), 0.05, 4.0)
    kernel_blocks = normal_values(streams_of[3], (LEVELS, SOUNDS), 1.0, 6.0, ((1, 128),), jnp.float32)
    sounding_dest_keys = jax.random.split(jax.random.fold_in(streams_of[4], 1), SOUNDS // SOUND_DEV)
    sounding_dest_turns = jax.random.permutation(jax.random.fold_in(streams_of[4], 3), SOUNDS // SOUND_DEV)
    sounding_dest = jax.vmap(lambda own, number: routed_block(jax.random.fold_in(streams_of[4], 2), own, number, SOUND_DEV, N_LON * N_LAT, 1, CAP, 2))(sounding_dest_keys, sounding_dest_turns).reshape((SOUNDS, 1))
    sounding_cell = place_ends(jax.random.randint(streams_of[5], (SOUNDS,), 0, 2 * BAND * TILE), jax.random.fold_in(streams_of[5], 1), 0, (2 * BAND * TILE) - 1).astype(jnp.int32)
    return {"adjoint_in": adjoint_in, "courant": courant, "mixing": mixing, "kernel_blocks": kernel_blocks, "sounding_dest": sounding_dest, "sounding_cell": sounding_cell}


def factors(mixing):
    levels = mixing.shape[0] + 1
    pivots = []
    ratios = []
    for stratum in range(levels):
        pivot_now = jnp.ones_like(mixing[0])
        if stratum > 0:
            pivot_now = pivot_now + mixing[stratum - 1]
        if stratum < levels - 1:
            pivot_now = pivot_now + mixing[stratum]
        if stratum > 0:
            pivot_now = pivot_now - mixing[stratum - 1] * ratios[stratum - 1]
        pivots.append(pivot_now)
        if stratum < levels - 1:
            ratios.append(mixing[stratum] / pivot_now)
    return pivots, ratios


def vertical_solve(state_in, mixing, pivots, ratios):
    levels = state_in.shape[0]
    forward = []
    for stratum in range(levels):
        carried = state_in[stratum]
        if stratum > 0:
            carried = carried + mixing[stratum - 1][None] * forward[-1]
        forward.append(carried / pivots[stratum][None])
    solved = [None] * levels
    solved[-1] = forward[-1]
    for stratum in range(levels - 2, -1, -1):
        solved[stratum] = forward[stratum] + ratios[stratum][None] * solved[stratum + 1]
    return jnp.stack(solved)


def sweep_roll(state_in, face_winds, along):
    jump_up = jnp.roll(state_in, -1, along) - state_in
    outgoing = jnp.maximum(face_winds, 0.0) * jump_up
    incoming = jnp.minimum(face_winds, 0.0) * jump_up
    return state_in + outgoing + jnp.roll(incoming, 1, along)


def reference(adjoint_in, courant, mixing, kernel_blocks, sounding_dest, sounding_cell):
    winds = courant.at[1, :, NLAT - 1, :].set(0.0)
    pivots, ratios = factors(mixing)

    def adjoint_step(state_in):
        vertical = vertical_solve(state_in, mixing, pivots, ratios)
        north = sweep_roll(vertical, winds[1][:, None], 2)
        return sweep_roll(north, winds[0][:, None], 3)

    after_first = adjoint_step(adjoint_in)
    owner = sounding_dest[:, 0]
    tile_lon = owner // N_LAT
    tile_lat = owner % N_LAT
    tracer = sounding_cell // (BAND * TILE)
    remain = sounding_cell % (BAND * TILE)
    row_global = tile_lat * BAND + remain // TILE
    col_global = tile_lon * TILE + remain % TILE
    target = ((tracer * NLAT + row_global) * NLON + col_global).astype(jnp.int32)
    forcing = jnp.zeros((LEVELS, TRACERS * NLAT * NLON), jnp.float32).at[:, target].add(kernel_blocks)
    forcing = forcing.reshape(LEVELS, TRACERS, NLAT, NLON)
    adjoint_out = adjoint_step(after_first + forcing)
    flux_grad = after_first[0] + adjoint_out[0]
    return adjoint_out, flux_grad
```

```python
import functools
import jax
import jax.numpy as jnp
from jax import lax
from jax.experimental import pallas as pl
from jax.experimental.pallas import tpu as pltpu
from jax.sharding import PartitionSpec as P

MESH = pl.DeviceIdType.MESH
ANY = pl.BlockSpec(memory_space=pl.ANY)
LANES = 128
HALF = 40
STREAMS = 4
VMEM_LIMIT = 60 * 1024 * 1024


def lane_iota(shape):
    return lax.broadcasted_iota(jnp.int32, shape, len(shape) - 1)


def pack_kernel(
    devices, capacity, levels, blocks_ref, dest_ref, cell_ref, out_ref, rows, slots, order, order_smem, sem
):
    held = blocks_ref.shape[1]
    chunks = held // LANES
    row_id = lax.broadcasted_iota(jnp.int32, (LANES, LANES), 0)
    col_id = lax.broadcasted_iota(jnp.int32, (LANES, LANES), 1)
    before = jnp.where(row_id < col_id, 1.0, 0.0).astype(jnp.bfloat16)
    ones = jnp.ones((LANES, LANES), jnp.bfloat16)
    base = jnp.zeros((LANES, LANES), jnp.float32)
    for chunk in range(chunks):
        owner = dest_ref[chunk : chunk + 1, :]
        hot = jnp.broadcast_to(owner, (LANES, LANES)) == row_id
        hot_f = jnp.where(hot, 1.0, 0.0)
        hot_b = hot_f.astype(jnp.bfloat16)
        earlier = jnp.dot(hot_b, before, preferred_element_type=jnp.float32)
        rank = jnp.sum(hot_f * (earlier + base), axis=0, keepdims=True)
        order[chunk : chunk + 1, :] = owner * capacity + rank.astype(jnp.int32)
        base = base + jnp.dot(hot_b, ones, preferred_element_type=jnp.float32)
    to_smem = pltpu.make_async_copy(order, order_smem, sem)
    to_smem.start()
    blank = jnp.where(lane_iota((64, LANES)) == levels, -1.0, 0.0)

    @pl.loop(0, devices * capacity // 64)
    def _(i):
        slots[pl.ds(pl.multiple_of(i * 64, 64), 64), :] = blank

    for chunk in range(chunks):
        span = slice(chunk * LANES, (chunk + 1) * LANES)
        tall = jnp.concatenate(
            [
                blocks_ref[:, span],
                jnp.broadcast_to(cell_ref[chunk : chunk + 1, :].astype(jnp.float32), (8, LANES)),
                jnp.zeros((LANES - levels - 8, LANES), jnp.float32),
            ],
            axis=0,
        )
        rows[span, :] = tall.T
    to_smem.wait()

    @pl.loop(0, chunks)
    def _(chunk):
        @pl.loop(0, LANES // 16)
        def _(part):
            for i in range(16):
                at = part * 16 + i
                slots[pl.ds(order_smem[chunk, at], 1), :] = rows[pl.ds(chunk * LANES + at, 1), :]

    low = lane_iota((HALF, LANES)) < capacity

    @pl.loop(0, devices // 2)
    def _(pair):
        wide = slots[pl.ds(pl.multiple_of(pair * LANES, LANES), LANES), :].T
        first, second = wide[:HALF], wide[HALF : 2 * HALF]
        out_ref[2 * pair] = jnp.where(low, first, pltpu.roll(second, capacity, 1))
        out_ref[2 * pair + 1] = jnp.where(low, pltpu.roll(first, capacity, 1), second)


def pack(kernel_blocks, owner, cell, devices, capacity):
    levels, held = kernel_blocks.shape
    return pl.pallas_call(
        functools.partial(pack_kernel, devices, capacity, levels),
        out_shape=jax.ShapeDtypeStruct((devices, HALF, LANES), jnp.float32),
        in_specs=[pl.BlockSpec(memory_space=pltpu.VMEM)] * 3,
        out_specs=pl.BlockSpec(memory_space=pltpu.VMEM),
        scratch_shapes=[
            pltpu.VMEM((held, LANES), jnp.float32),
            pltpu.VMEM((devices * capacity, LANES), jnp.float32),
            pltpu.VMEM((held // LANES, LANES), jnp.int32),
            pltpu.SMEM((held // LANES, LANES), jnp.int32),
            pltpu.SemaphoreType.DMA,
        ],
        compiler_params=pltpu.CompilerParams(vmem_limit_bytes=VMEM_LIMIT),
        name="pack_soundings",
    )(kernel_blocks, owner, cell)


def transport_body(
    lon_count,
    lat_count,
    after_entry,
    before_exit,
    a_hbm,
    c_hbm,
    m_hbm,
    out_hbm,
    a_ref,
    c_ref,
    m_ref,
    vbuf,
    rbuf,
    obuf,
    send_n,
    send_s,
    send_e,
    send_w,
    from_s,
    from_n,
    from_w,
    from_e,
    merged,
    load_sem,
    store_sem,
    send_sem,
    recv_sem,
):
    levels, tracers, band, tile = a_ref.shape
    lon, lat = lax.axis_index("lon"), lax.axis_index("lat")
    north = {"lon": lon, "lat": lax.rem(lat + 1, lat_count)}
    south = {"lon": lon, "lat": lax.rem(lat + lat_count - 1, lat_count)}
    east = {"lon": lax.rem(lon + 1, lon_count), "lat": lat}
    west = {"lon": lax.rem(lon + lon_count - 1, lon_count), "lat": lat}

    loads = [
        pltpu.make_async_copy(m_hbm, m_ref, load_sem.at[0]),
        pltpu.make_async_copy(a_hbm, a_ref, load_sem.at[1]),
        pltpu.make_async_copy(c_hbm, c_ref, load_sem.at[2]),
    ]
    for load in loads:
        load.start()
    after_entry()
    loads[0].wait()
    loads[1].wait()

    mix = m_ref[0]
    inverse = 1.0 / (1.0 + mix)
    ratio = mix * inverse
    solved = a_ref[0] * inverse[None]
    rbuf[0] = ratio
    vbuf[0] = solved

    def down(k, carry):
        mix_above, ratio, solved = carry
        mix = m_ref[k]
        inverse = 1.0 / (1.0 + mix_above + mix - mix_above * ratio)
        ratio = mix * inverse
        solved = (a_ref[k] + mix_above[None] * solved) * inverse[None]
        rbuf[k] = ratio
        vbuf[k] = solved
        return mix, ratio, solved

    mix, ratio, solved = lax.fori_loop(1, levels - 1, down, (mix, ratio, solved))
    inverse = 1.0 / (1.0 + mix - mix * ratio)
    solved = (a_ref[levels - 1] + mix[None] * solved) * inverse[None]

    def keep(k, solved):
        vbuf[k] = solved
        for t in range(tracers):
            send_s[pl.ds(tracers * k + t, 1), :] = solved[t, 0:1, :]
            send_n[pl.ds(tracers * k + t, 1), :] = solved[t, band - 1 : band, :]

    keep(levels - 1, solved)

    def up(i, solved):
        k = levels - 2 - i
        solved = vbuf[k] + rbuf[k][None] * solved
        keep(k, solved)
        return solved

    lax.fori_loop(0, levels - 1, up, solved)

    loads[2].wait()
    row = lax.broadcasted_iota(jnp.int32, (band, tile), 0)
    lane = lane_iota((band, tile))
    top = row == band - 1
    edge = jnp.where(lat == lat_count - 1, 0.0, 1.0)

    @pl.loop(0, levels)
    def _(k):
        send_n[pl.ds(levels * tracers + k, 1), :] = c_ref[1, k, band - 1 : band, :] * edge

    def remote(index, src, dst, to):
        return pltpu.make_async_remote_copy(
            src_ref=src, dst_ref=dst, send_sem=send_sem.at[index], recv_sem=recv_sem.at[index],
            device_id=to, device_id_type=MESH,
        )

    to_north = remote(0, send_n, from_s, north)
    to_south = remote(1, send_s, from_n, south)
    to_north.start()
    to_south.start()
    to_north.wait()
    to_south.wait()

    keep_top = jnp.where(top, edge, 1.0)
    zero = jnp.zeros((band, tile), jnp.float32)
    for t in range(tracers):

        def sweep(k, carry):
            first, last, wind_last = carry
            face = c_ref[1, k] * keep_top
            cells = vbuf[k, t]
            above = from_n[pl.ds(tracers * k + t, 1), :]
            below = from_s[pl.ds(tracers * k + t, 1), :]
            face_below = from_s[pl.ds(levels * tracers + k, 1), :]
            rise = jnp.where(top, above, pltpu.roll(cells, band - 1, 0)) - cells
            incoming = jnp.minimum(face, 0.0) * rise
            incoming = jnp.where(
                row == 0,
                jnp.minimum(face_below, 0.0) * (cells - below),
                pltpu.roll(incoming, 1, 0),
            )
            cells = cells + jnp.maximum(face, 0.0) * rise + incoming
            vbuf[k, t] = cells
            turned = pltpu.roll(cells, k, 1)
            at_first = lane == k
            at_last = lane == lax.rem(k + tile - 1, tile)
            first = jnp.where(at_first, turned, first)
            last = jnp.where(at_last, turned, last)
            if t == 0:
                wind_last = jnp.where(at_last, pltpu.roll(c_ref[0, k], k, 1), wind_last)
            return first, last, wind_last

        first, last, wind_last = lax.fori_loop(0, levels, sweep, (zero, zero, zero))
        send_w[t] = first
        send_e[t] = last
        if t == 0:
            send_e[tracers] = wind_last

    to_east = remote(2, send_e, from_w, east)
    to_west = remote(3, send_w, from_e, west)
    to_east.start()
    to_west.start()
    to_east.wait()
    to_west.wait()
    even = lax.rem(lane, 2) == 0
    for t in range(tracers):
        eastern, western = from_e[t], pltpu.roll(from_w[t], 2, 1)
        merged[t, 0] = jnp.where(even, eastern, western)
        merged[t, 1] = jnp.where(even, western, eastern)

    group = 8

    def stored(j):
        span = pl.ds(j * group, group)
        return pltpu.make_async_copy(obuf.at[span], out_hbm.at[span], store_sem.at[j])

    @pl.loop(0, levels // group)
    def _(j):
        @pl.loop(0, group // 2)
        def _(i):
            for parity in range(2):
                k = j * group + 2 * i + parity
                face = c_ref[0, k]
                face_west = pltpu.roll(from_w[tracers], lax.rem(tile + 1 - k, tile), 1)
                for t in range(tracers):
                    cells = vbuf[k, t]
                    sides = pltpu.roll(merged[t, parity], tile - 1 - k, 1)
                    rise = jnp.where(lane == tile - 1, sides, pltpu.roll(cells, tile - 1, 1)) - cells
                    incoming = jnp.minimum(face, 0.0) * rise
                    incoming = jnp.where(
                        lane == 0,
                        jnp.minimum(face_west, 0.0) * (cells - sides),
                        pltpu.roll(incoming, 1, 1),
                    )
                    obuf[k, t] = cells + jnp.maximum(face, 0.0) * rise + incoming

        stored(j).start()

    before_exit()

    @pl.loop(0, levels // group)
    def _(j):
        stored(j).wait()


def step_scratch(levels, tracers, band, tile):
    f32 = jnp.float32
    return [
        pltpu.VMEM((levels, tracers, band, tile), f32),
        pltpu.VMEM((2, levels, band, tile), f32),
        pltpu.VMEM((levels - 1, band, tile), f32),
        pltpu.VMEM((levels, tracers, band, tile), f32),
        pltpu.VMEM((levels - 1, band, tile), f32),
        pltpu.VMEM((levels, tracers, band, tile), f32),
        pltpu.VMEM((levels * (tracers + 1), tile), f32),
        pltpu.VMEM((levels * tracers, tile), f32),
        pltpu.VMEM((tracers + 1, band, tile), f32),
        pltpu.VMEM((tracers, band, tile), f32),
        pltpu.VMEM((levels * (tracers + 1), tile), f32),
        pltpu.VMEM((levels * tracers, tile), f32),
        pltpu.VMEM((tracers + 1, band, tile), f32),
        pltpu.VMEM((tracers, band, tile), f32),
        pltpu.VMEM((tracers, 2, band, tile), f32),
        pltpu.SemaphoreType.DMA((3,)),
        pltpu.SemaphoreType.DMA((levels // 8,)),
        pltpu.SemaphoreType.DMA((4,)),
        pltpu.SemaphoreType.DMA((4,)),
    ]


def first_kernel(lon_count, lat_count, a_hbm, c_hbm, m_hbm, blocks_hbm, out_hbm, got_hbm, *scratch):
    *step, trade_send, trade_recv, own_sem = scratch
    devices = lon_count * lat_count
    me = lax.axis_index("lon") * lat_count + lax.axis_index("lat")

    def entry():
        barrier = pltpu.get_barrier_semaphore()

        @pl.loop(1, devices)
        def _(i):
            peer = lax.rem(me + i, devices)
            pl.semaphore_signal(
                barrier, inc=1, device_id={"lon": peer // lat_count, "lat": lax.rem(peer, lat_count)},
                device_id_type=MESH,
            )

        pl.semaphore_wait(barrier, devices - 1)

        @pl.loop(1, devices)
        def _(i):
            peer = lax.rem(me + i, devices)
            pltpu.make_async_remote_copy(
                src_ref=blocks_hbm.at[peer], dst_ref=got_hbm.at[me],
                send_sem=trade_send, recv_sem=trade_recv,
                device_id={"lon": peer // lat_count, "lat": lax.rem(peer, lat_count)},
                device_id_type=MESH,
            ).start()

        pltpu.make_async_copy(blocks_hbm.at[me], got_hbm.at[me], own_sem).start()

    def leave():
        pltpu.make_async_copy(blocks_hbm.at[me], got_hbm.at[me], own_sem).wait()
        most = pl.ds(0, devices - 1)
        everything = pltpu.make_async_remote_copy(
            src_ref=blocks_hbm.at[most], dst_ref=got_hbm.at[most],
            send_sem=trade_send, recv_sem=trade_recv,
            device_id={"lon": lax.axis_index("lon"), "lat": lax.rem(lax.axis_index("lat") + 1, lat_count)},
            device_id_type=MESH,
        )
        everything.wait()

    transport_body(lon_count, lat_count, entry, leave, a_hbm, c_hbm, m_hbm, out_hbm, *step)


def second_kernel(lon_count, lat_count, a_hbm, c_hbm, m_hbm, first_hbm, out_hbm, flux_ref, *scratch):
    *step, ground, ground_sem = scratch
    obuf = step[5]

    def entry():
        lon, lat = lax.axis_index("lon"), lax.axis_index("lat")
        barrier = pltpu.get_barrier_semaphore()
        for d_lon, d_lat in ((1, 0), (lon_count - 1, 0), (0, 1), (0, lat_count - 1)):
            pl.semaphore_signal(
                barrier, inc=1,
                device_id={"lon": lax.rem(lon + d_lon, lon_count), "lat": lax.rem(lat + d_lat, lat_count)},
                device_id_type=MESH,
            )
        pltpu.make_async_copy(first_hbm.at[0], ground, ground_sem).start()
        pl.semaphore_wait(barrier, 4)

    def leave():
        pltpu.make_async_copy(first_hbm.at[0], ground, ground_sem).wait()
        flux_ref[...] = ground[...] + obuf[0]

    transport_body(lon_count, lat_count, entry, leave, a_hbm, c_hbm, m_hbm, out_hbm, *step)


def first_step(state, courant, mixing, blocks, lon_count, lat_count):
    levels, tracers, band, tile = state.shape
    return pl.pallas_call(
        functools.partial(first_kernel, lon_count, lat_count),
        out_shape=(
            jax.ShapeDtypeStruct(state.shape, jnp.float32),
            jax.ShapeDtypeStruct(blocks.shape, jnp.float32),
        ),
        in_specs=[ANY] * 4,
        out_specs=(ANY, ANY),
        scratch_shapes=step_scratch(levels, tracers, band, tile)
        + [pltpu.SemaphoreType.DMA, pltpu.SemaphoreType.DMA, pltpu.SemaphoreType.DMA],
        compiler_params=pltpu.CompilerParams(
            collective_id=0, has_side_effects=True, vmem_limit_bytes=VMEM_LIMIT
        ),
        name="first_step",
    )(state, courant, mixing, blocks)


def second_step(state, courant, mixing, after_first, lon_count, lat_count):
    levels, tracers, band, tile = state.shape
    return pl.pallas_call(
        functools.partial(second_kernel, lon_count, lat_count),
        out_shape=(
            jax.ShapeDtypeStruct(state.shape, jnp.float32),
            jax.ShapeDtypeStruct(state.shape[1:], jnp.float32),
        ),
        in_specs=[ANY] * 4,
        out_specs=(ANY, pl.BlockSpec(memory_space=pltpu.VMEM)),
        scratch_shapes=step_scratch(levels, tracers, band, tile)
        + [pltpu.VMEM((tracers, band, tile), jnp.float32), pltpu.SemaphoreType.DMA],
        compiler_params=pltpu.CompilerParams(
            collective_id=1, has_side_effects=True, vmem_limit_bytes=VMEM_LIMIT
        ),
        name="second_step",
    )(state, courant, mixing, after_first)


def force_kernel(capacity, levels, lines, got_ref, state_hbm, out_hbm, rows, ids, ids_smem, state, *rest):
    sums, (ids_sem, load_sem, store_sem) = rest[:STREAMS], rest[STREAMS:]
    devices = got_ref.shape[0]
    cells_all = lines * LANES
    load = pltpu.make_async_copy(state_hbm, state, load_sem)
    load.start()
    low = lane_iota((HALF, LANES)) < capacity

    @pl.loop(0, devices // 2)
    def _(pair):
        one, two = got_ref[2 * pair], got_ref[2 * pair + 1]
        first = jnp.where(low, one, pltpu.roll(two, capacity, 1))
        second = jnp.where(low, pltpu.roll(one, capacity, 1), two)
        cell = second[levels - HALF : levels - HALF + 1, :].astype(jnp.int32)
        ids[pl.ds(pair, 1), :] = jnp.where(cell < 0, cells_all, cell)
        wide = jnp.concatenate([first, second, jnp.zeros((LANES - 2 * HALF, LANES), jnp.float32)], axis=0)
        rows[pl.ds(pl.multiple_of(pair * LANES, LANES), LANES), :] = wide.T

    to_smem = pltpu.make_async_copy(ids, ids_smem, ids_sem)
    to_smem.start()
    zero = jnp.zeros((64, LANES), jnp.float32)

    @pl.loop(0, cells_all // 64)
    def _(i):
        for s in range(STREAMS):
            sums[s][pl.ds(pl.multiple_of(i * 64, 64), 64), :] = zero

    to_smem.wait()

    @pl.loop(0, devices // 2)
    def _(pair):
        @pl.loop(0, LANES // (4 * STREAMS))
        def _(part):
            for i in range(4):
                at = [part * 4 * STREAMS + i * STREAMS + s for s in range(STREAMS)]
                cell = [ids_smem[pair, at[s]] for s in range(STREAMS)]
                new = [
                    sums[s][pl.ds(cell[s], 1), :] + rows[pl.ds(pair * LANES + at[s], 1), :]
                    for s in range(STREAMS)
                ]
                for s in range(STREAMS):
                    sums[s][pl.ds(cell[s], 1), :] = new[s]

    load.wait()

    @pl.loop(0, cells_all // LANES)
    def _(line):
        span = pl.ds(pl.multiple_of(line * LANES, LANES), LANES)
        total = sums[0][span, :]
        for s in range(1, STREAMS):
            total = total + sums[s][span, :]
        at = pl.ds(line, levels, stride=cells_all // LANES)
        state[at, :] = state[at, :] + total.T[:levels]

    store = pltpu.make_async_copy(state, out_hbm, store_sem)
    store.start()
    store.wait()


def add_forcing(got, after_first, capacity):
    levels, tracers, band, tile = after_first.shape
    devices = got.shape[0]
    lines = tracers * band
    flat = after_first.reshape(levels * lines, tile)

    out = pl.pallas_call(
        functools.partial(force_kernel, capacity, levels, lines),
        out_shape=jax.ShapeDtypeStruct(flat.shape, jnp.float32),
        in_specs=[pl.BlockSpec(memory_space=pltpu.VMEM), ANY],
        out_specs=ANY,
        scratch_shapes=[
            pltpu.VMEM((devices * capacity, LANES), jnp.float32),
            pltpu.VMEM((devices // 2, LANES), jnp.int32),
            pltpu.SMEM((devices // 2, LANES), jnp.int32),
            pltpu.VMEM(flat.shape, jnp.float32),
        ]
        + [pltpu.VMEM((lines * tile + 8, LANES), jnp.float32)] * STREAMS
        + [pltpu.SemaphoreType.DMA] * 3,
        compiler_params=pltpu.CompilerParams(vmem_limit_bytes=VMEM_LIMIT),
        name="add_forcing",
    )(got, flat)
    return out.reshape(after_first.shape)


def on_device(adjoint_in, courant, mixing, kernel_blocks, sounding_dest, sounding_cell):
    lon_count = lax.axis_size("lon")
    lat_count = lax.axis_size("lat")
    devices = lon_count * lat_count
    held = kernel_blocks.shape[1]
    capacity = 4 * held // devices
    owner = sounding_dest.reshape(held // LANES, LANES)
    cell = sounding_cell.reshape(held // LANES, LANES)
    blocks = pack(kernel_blocks, owner, cell, devices, capacity)
    after_first, got = first_step(adjoint_in, courant, mixing, blocks, lon_count, lat_count)
    forced = add_forcing(got, after_first, capacity)
    return second_step(forced, courant, mixing, after_first, lon_count, lat_count)


def solution(mesh):
    placed = (
        P(None, None, "lat", "lon"),
        P(None, None, "lat", "lon"),
        P(None, "lat", "lon"),
        P(None, ("lon", "lat")),
        P(("lon", "lat"), None),
        P(("lon", "lat")),
    )
    return jax.shard_map(
        on_device,
        mesh=mesh,
        in_specs=placed,
        out_specs=(P(None, None, "lat", "lon"), P(None, "lat", "lon")),
        check_vma=False,
    )
```

```python
import functools
import jax
import jax.numpy as jnp
from jax import lax
from jax.experimental import pallas as pl
from jax.experimental.pallas import tpu as pltpu
from jax.sharding import PartitionSpec as P

MESH = pl.DeviceIdType.MESH
ANY = pl.BlockSpec(memory_space=pl.ANY)
LANES = 128
HALF = 40
STREAMS = 4
VMEM_LIMIT = 60 * 1024 * 1024


def lane_iota(shape):
    return lax.broadcasted_iota(jnp.int32, shape, len(shape) - 1)


def pack_kernel(
    devices, capacity, levels, blocks_ref, dest_ref, cell_ref, out_ref, rows, slots, order, order_smem, sems
):
    held = blocks_ref.shape[1]
    chunks = held // LANES
    row_id = lax.broadcasted_iota(jnp.int32, (LANES, LANES), 0)
    col_id = lax.broadcasted_iota(jnp.int32, (LANES, LANES), 1)
    before = jnp.where(row_id < col_id, 1.0, 0.0).astype(jnp.bfloat16)
    ones = jnp.ones((LANES, LANES), jnp.bfloat16)
    base = jnp.zeros((LANES, LANES), jnp.float32)

    def to_smem(chunk):
        return pltpu.make_async_copy(
            order.at[chunk], order_smem.at[pl.ds(chunk * LANES, LANES)], sems.at[chunk]
        )

    for chunk in range(chunks):
        owner = dest_ref[chunk : chunk + 1, :]
        hot = jnp.broadcast_to(owner, (LANES, LANES)) == row_id
        hot_f = jnp.where(hot, 1.0, 0.0)
        hot_b = hot_f.astype(jnp.bfloat16)
        earlier = jnp.dot(hot_b, before, preferred_element_type=jnp.float32)
        rank = jnp.sum(hot_f * (earlier + base), axis=0, keepdims=True)
        order[chunk : chunk + 1, :] = owner * capacity + rank.astype(jnp.int32)
        base = base + jnp.dot(hot_b, ones, preferred_element_type=jnp.float32)
    for chunk in range(chunks):
        to_smem(chunk).start()
    blank = jnp.where(lane_iota((64, LANES)) == levels, -1.0, 0.0)

    @pl.loop(0, devices * capacity // 64)
    def _(i):
        slots[pl.ds(pl.multiple_of(i * 64, 64), 64), :] = blank

    for chunk in range(chunks):
        span = slice(chunk * LANES, (chunk + 1) * LANES)
        tall = jnp.concatenate(
            [
                blocks_ref[:, span],
                jnp.broadcast_to(cell_ref[chunk : chunk + 1, :].astype(jnp.float32), (8, LANES)),
                jnp.zeros((LANES - levels - 8, LANES), jnp.float32),
            ],
            axis=0,
        )
        rows[span, :] = tall.T
    for chunk in range(chunks):
        to_smem(chunk).wait()

    @pl.loop(0, held // 16)
    def _(part):
        for i in range(16):
            at = part * 16 + i
            slots[pl.ds(order_smem[at], 1), :] = rows[pl.ds(at, 1), :]

    low = lane_iota((HALF, LANES)) < capacity
    group = 8

    @pl.loop(0, devices // (2 * group))
    def _(part):
        wides = []
        for i in range(group):
            at = pl.multiple_of((part * group + i) * LANES, LANES)
            wides.append(slots[pl.ds(at, LANES), :].T)
        for i, wide in enumerate(wides):
            first, second = wide[:HALF], wide[HALF : 2 * HALF]
            pair = part * group + i
            out_ref[2 * pair] = jnp.where(low, first, pltpu.roll(second, capacity, 1))
            out_ref[2 * pair + 1] = jnp.where(low, pltpu.roll(first, capacity, 1), second)


def pack(kernel_blocks, owner, cell, devices, capacity):
    levels, held = kernel_blocks.shape
    return pl.pallas_call(
        functools.partial(pack_kernel, devices, capacity, levels),
        out_shape=jax.ShapeDtypeStruct((devices, HALF, LANES), jnp.float32),
        in_specs=[pl.BlockSpec(memory_space=pltpu.VMEM)] * 3,
        out_specs=pl.BlockSpec(memory_space=pltpu.VMEM),
        scratch_shapes=[
            pltpu.VMEM((held, LANES), jnp.float32),
            pltpu.VMEM((devices * capacity, LANES), jnp.float32),
            pltpu.VMEM((held // LANES, LANES), jnp.int32),
            pltpu.SMEM((held,), jnp.int32),
            pltpu.SemaphoreType.DMA((held // LANES,)),
        ],
        compiler_params=pltpu.CompilerParams(vmem_limit_bytes=VMEM_LIMIT),
        name="pack_soundings",
    )(kernel_blocks, owner, cell)


def transport_front(lon_count, lat_count, hooks, a_hbm, c_hbm, m_hbm, front):
    (
        a_ref, c_ref, m_ref, vbuf, rbuf, send_n, send_s, send_e, send_w,
        from_s, from_n, from_w, from_e, rows_fix, merged, load_sem, send_sem, recv_sem,
    ) = front
    at_entry, after_rows, after_columns, during_columns = hooks
    levels, tracers, band, tile = a_ref.shape
    lon, lat = lax.axis_index("lon"), lax.axis_index("lat")
    north = {"lon": lon, "lat": lax.rem(lat + 1, lat_count)}
    south = {"lon": lon, "lat": lax.rem(lat + lat_count - 1, lat_count)}
    east = {"lon": lax.rem(lon + 1, lon_count), "lat": lat}
    west = {"lon": lax.rem(lon + lon_count - 1, lon_count), "lat": lat}

    loads = [
        pltpu.make_async_copy(m_hbm, m_ref, load_sem.at[0]),
        pltpu.make_async_copy(a_hbm, a_ref, load_sem.at[1]),
        pltpu.make_async_copy(c_hbm, c_ref, load_sem.at[2]),
    ]
    for load in loads:
        load.start()
    at_entry()
    loads[0].wait()
    loads[1].wait()

    mix = m_ref[0]
    inverse = 1.0 / (1.0 + mix)
    ratio = mix * inverse
    solved = a_ref[0] * inverse[None]
    rbuf[0] = ratio
    vbuf[0] = solved

    def down(k, carry):
        mix_above, ratio, solved = carry
        mix = m_ref[k]
        inverse = 1.0 / (1.0 + mix_above + mix - mix_above * ratio)
        ratio = mix * inverse
        solved = (a_ref[k] + mix_above[None] * solved) * inverse[None]
        rbuf[k] = ratio
        vbuf[k] = solved
        return mix, ratio, solved

    mix, ratio, solved = lax.fori_loop(1, levels - 1, down, (mix, ratio, solved))
    inverse = 1.0 / (1.0 + mix - mix * ratio)
    solved = (a_ref[levels - 1] + mix[None] * solved) * inverse[None]

    def keep(k, solved):
        vbuf[k] = solved
        for t in range(tracers):
            send_s[pl.ds(t * levels + k, 1), :] = solved[t, 0:1, :]
            send_n[pl.ds(t * levels + k, 1), :] = solved[t, band - 1 : band, :]

    keep(levels - 1, solved)

    def up(i, solved):
        k = levels - 2 - i
        solved = vbuf[k] + rbuf[k][None] * solved
        keep(k, solved)
        return solved

    lax.fori_loop(0, levels - 1, up, solved)

    loads[2].wait()
    edge = jnp.where(lat == lat_count - 1, 0.0, 1.0)

    @pl.loop(0, levels // 8)
    def _(j):
        for i in range(8):
            k = j * 8 + i
            send_n[pl.ds(tracers * levels + k, 1), :] = c_ref[1, k, band - 1 : band, :] * edge

    def remote(index, src, dst, to):
        return pltpu.make_async_remote_copy(
            src_ref=src, dst_ref=dst, send_sem=send_sem.at[index], recv_sem=recv_sem.at[index],
            device_id=to, device_id_type=MESH,
        )

    to_north = remote(0, send_n, from_s, north)
    to_south = remote(1, send_s, from_n, south)
    to_north.start()
    to_south.start()
    after_rows()

    top = lax.broadcasted_iota(jnp.int32, (band, tile), 0) == band - 1

    @pl.loop(0, levels // 2)
    def _(j):
        swept = []
        for i in range(2):
            face = c_ref[1, 2 * j + i]
            out_face, in_face = jnp.maximum(face, 0.0), jnp.minimum(face, 0.0)
            for t in range(tracers):
                cells = vbuf[2 * j + i, t]
                rise = jnp.where(top, 0.0, pltpu.roll(cells, band - 1, 0) - cells)
                swept.append(cells + out_face * rise + pltpu.roll(in_face * rise, 1, 0))
        for i in range(2):
            for t in range(tracers):
                vbuf[2 * j + i, t] = swept[tracers * i + t]

    lane = lane_iota((8, tile))
    zero = jnp.zeros((8, tile), jnp.float32)

    @pl.loop(0, band // 8)
    def _(g):
        span = pl.ds(pl.multiple_of(g * 8, 8), 8)
        last = zero
        for k in range(levels):
            last = jnp.where(lane == (k - 1) % tile, pltpu.roll(c_ref[0, k, span, :], k, 1), last)
        send_e[tracers, span, :] = last

    to_north.wait()
    to_south.wait()
    face_south = jnp.minimum(from_s[tracers * levels :, :], 0.0)
    face_north = jnp.maximum(send_n[tracers * levels :, :], 0.0)
    for t in range(tracers):
        part = slice(t * levels, (t + 1) * levels)
        rows_fix[part, :] = face_south * (send_s[part, :] - from_s[part, :])
        rows_fix[tracers * levels + t * levels : tracers * levels + (t + 1) * levels, :] = face_north * (
            from_n[part, :] - send_n[part, :]
        )

    row = lax.broadcasted_iota(jnp.int32, (8, tile), 0)

    def columns(g, fixed, at):
        span = pl.ds(pl.multiple_of(g * 8, 8), 8)
        for t in range(tracers):
            first, last = zero, zero
            for k in range(levels):
                cells = vbuf[k, t, span, :]
                if fixed is not None:
                    fix = rows_fix[fixed + t * levels + k : fixed + t * levels + k + 1, :]
                    cells = cells + jnp.where(row == at, jnp.broadcast_to(fix, (8, tile)), 0.0)
                    vbuf[k, t, span, :] = cells
                turned = pltpu.roll(cells, k, 1)
                first = jnp.where(lane == k, turned, first)
                last = jnp.where(lane == (k - 1) % tile, turned, last)
            send_w[t, span, :] = first
            send_e[t, span, :] = last

    columns(0, 0, 0)
    columns(band // 8 - 1, tracers * levels, 7)

    @pl.loop(1, band // 8 - 1)
    def _(g):
        columns(g, None, None)

    to_east = remote(2, send_e, from_w, east)
    to_west = remote(3, send_w, from_e, west)
    to_east.start()
    to_west.start()
    after_columns()
    during_columns()
    to_east.wait()
    to_west.wait()

    even = lax.rem(lane_iota((band, tile)), 2) == 0
    face_last = jnp.maximum(pltpu.roll(send_e[tracers], 1, 1), 0.0)
    face_first = jnp.minimum(pltpu.roll(from_w[tracers], 2, 1), 0.0)
    for t in range(tracers):
        at_last = face_last * (from_e[t] - pltpu.roll(send_e[t], 1, 1))
        at_first = face_first * (pltpu.roll(send_w[t], 1, 1) - pltpu.roll(from_w[t], 2, 1))
        merged[t, 0] = jnp.where(even, at_last, at_first)
        merged[t, 1] = jnp.where(even, at_first, at_last)


def front_scratch(levels, tracers, band, tile, merged=True):
    f32 = jnp.float32
    return [
        pltpu.VMEM((levels, tracers, band, tile), f32),
        pltpu.VMEM((2, levels, band, tile), f32),
        pltpu.VMEM((levels - 1, band, tile), f32),
        pltpu.VMEM((levels, tracers, band, tile), f32),
        pltpu.VMEM((levels - 1, band, tile), f32),
        pltpu.VMEM((levels * (tracers + 1), tile), f32),
        pltpu.VMEM((levels * tracers, tile), f32),
        pltpu.VMEM((tracers + 1, band, tile), f32),
        pltpu.VMEM((tracers, band, tile), f32),
        pltpu.VMEM((levels * (tracers + 1), tile), f32),
        pltpu.VMEM((levels * tracers, tile), f32),
        pltpu.VMEM((tracers + 1, band, tile), f32),
        pltpu.VMEM((tracers, band, tile), f32),
        pltpu.VMEM((2 * tracers * levels, tile), f32),
        pltpu.VMEM((tracers, 2, band, tile), f32),
        pltpu.SemaphoreType.DMA((3,)),
        pltpu.SemaphoreType.DMA((4,)),
        pltpu.SemaphoreType.DMA((4,)),
    ]


FRONT = 18


def sweep_columns(levels, tracers, lane, load_face, load_cells, load_sides, store):
    tile = lane.shape[1]
    for k in range(levels):
        face = load_face(k)
        out_face, in_face = jnp.maximum(face, 0.0), jnp.minimum(face, 0.0)
        for t in range(tracers):
            cells = load_cells(k, t)
            rise = jnp.where(lane == tile - 1, 0.0, pltpu.roll(cells, tile - 1, 1) - cells)
            swept = cells + out_face * rise + pltpu.roll(in_face * rise, 1, 1)
            if load_sides is not None:
                swept = swept + sides_of(lane, load_sides(k, t), k)
            store(k, t, swept)


def sides_of(lane, merged, k):
    tile = lane.shape[1]
    return jnp.where((lane == 0) | (lane == tile - 1), pltpu.roll(merged, tile - 1 - k, 1), 0.0)


def first_kernel(lon_count, lat_count, a_hbm, c_hbm, m_hbm, blocks_hbm, out_hbm, got_hbm, *scratch):
    front, (obuf, store_sem, trade_send, trade_recv, own_sem) = scratch[:FRONT], scratch[FRONT:]
    c_ref, vbuf, merged = front[1], front[3], front[14]
    levels, tracers, band, tile = vbuf.shape
    devices = lon_count * lat_count
    me = lax.axis_index("lon") * lat_count + lax.axis_index("lat")

    def trade(begin, end):
        @pl.loop(begin, end)
        def _(i):
            peer = lax.rem(me + i, devices)
            pltpu.make_async_remote_copy(
                src_ref=blocks_hbm.at[peer], dst_ref=got_hbm.at[me],
                send_sem=trade_send, recv_sem=trade_recv,
                device_id={"lon": peer // lat_count, "lat": lax.rem(peer, lat_count)},
                device_id_type=MESH,
            ).start()

    cuts = (1, 1 + devices // 4, devices // 2, devices)

    def at_entry():
        barrier = pltpu.get_barrier_semaphore()

        @pl.loop(1, devices)
        def _(i):
            peer = lax.rem(me + i, devices)
            pl.semaphore_signal(
                barrier, inc=1, device_id={"lon": peer // lat_count, "lat": lax.rem(peer, lat_count)},
                device_id_type=MESH,
            )

        pl.semaphore_wait(barrier, devices - 1)
        trade(cuts[0], cuts[1])
        pltpu.make_async_copy(blocks_hbm.at[me], got_hbm.at[me], own_sem).start()

    lane = lane_iota((8, tile))

    def main_sweep():
        @pl.loop(0, band // 8)
        def _(g):
            span = pl.ds(pl.multiple_of(g * 8, 8), 8)

            def store(k, t, swept):
                obuf[k, t, span, :] = swept

            sweep_columns(
                levels, tracers, lane, lambda k: c_ref[0, k, span, :],
                lambda k, t: vbuf[k, t, span, :], None, store,
            )

    hooks = (at_entry, lambda: trade(cuts[1], cuts[2]), lambda: trade(cuts[2], cuts[3]), main_sweep)
    transport_front(lon_count, lat_count, hooks, a_hbm, c_hbm, m_hbm, front)

    def stored(g):
        span = pl.ds(pl.multiple_of(g * 8, 8), 8)
        return pltpu.make_async_copy(obuf.at[:, :, span, :], out_hbm.at[:, :, span, :], store_sem.at[g])

    @pl.loop(0, band // 8)
    def _(g):
        span = pl.ds(pl.multiple_of(g * 8, 8), 8)
        for t in range(tracers):
            sides = [merged[t, 0, span, :], merged[t, 1, span, :]]
            for k in range(levels):
                obuf[k, t, span, :] = obuf[k, t, span, :] + sides_of(lane, sides[k % 2], k)
        stored(g).start()

    pltpu.make_async_copy(blocks_hbm.at[me], got_hbm.at[me], own_sem).wait()
    most = pl.ds(0, devices - 1)
    pltpu.make_async_remote_copy(
        src_ref=blocks_hbm.at[most], dst_ref=got_hbm.at[most],
        send_sem=trade_send, recv_sem=trade_recv,
        device_id={"lon": lax.axis_index("lon"), "lat": lax.rem(lax.axis_index("lat") + 1, lat_count)},
        device_id_type=MESH,
    ).wait()

    @pl.loop(0, band // 8)
    def _(g):
        stored(g).wait()


def second_kernel(lon_count, lat_count, a_hbm, c_hbm, m_hbm, out_hbm, sides_ref, *scratch):
    front, (store_sem,) = scratch[:FRONT], scratch[FRONT:]
    vbuf, merged = front[3], front[14]

    def at_entry():
        lon, lat = lax.axis_index("lon"), lax.axis_index("lat")
        barrier = pltpu.get_barrier_semaphore()
        for d_lon, d_lat in ((1, 0), (lon_count - 1, 0), (0, 1), (0, lat_count - 1)):
            pl.semaphore_signal(
                barrier, inc=1,
                device_id={"lon": lax.rem(lon + d_lon, lon_count), "lat": lax.rem(lat + d_lat, lat_count)},
                device_id_type=MESH,
            )
        pl.semaphore_wait(barrier, 4)

    store = pltpu.make_async_copy(vbuf, out_hbm, store_sem)
    hooks = (at_entry, lambda: None, store.start, lambda: None)
    transport_front(lon_count, lat_count, hooks, a_hbm, c_hbm, m_hbm, front)
    sides_ref[...] = merged[...]
    store.wait()


def first_step(state, courant, mixing, blocks, lon_count, lat_count):
    levels, tracers, band, tile = state.shape
    return pl.pallas_call(
        functools.partial(first_kernel, lon_count, lat_count),
        out_shape=(
            jax.ShapeDtypeStruct(state.shape, jnp.float32),
            jax.ShapeDtypeStruct(blocks.shape, jnp.float32),
        ),
        in_specs=[ANY] * 4,
        out_specs=(ANY, ANY),
        scratch_shapes=front_scratch(levels, tracers, band, tile)
        + [
            pltpu.VMEM((levels, tracers, band, tile), jnp.float32),
            pltpu.SemaphoreType.DMA((band // 8,)),
            pltpu.SemaphoreType.DMA,
            pltpu.SemaphoreType.DMA,
            pltpu.SemaphoreType.DMA,
        ],
        compiler_params=pltpu.CompilerParams(
            collective_id=0, has_side_effects=True, vmem_limit_bytes=VMEM_LIMIT
        ),
        name="first_step",
    )(state, courant, mixing, blocks)


def second_front(state, courant, mixing, lon_count, lat_count):
    levels, tracers, band, tile = state.shape
    return pl.pallas_call(
        functools.partial(second_kernel, lon_count, lat_count),
        out_shape=(
            jax.ShapeDtypeStruct(state.shape, jnp.float32),
            jax.ShapeDtypeStruct((tracers, 2, band, tile), jnp.float32),
        ),
        in_specs=[ANY] * 3,
        out_specs=(ANY, pl.BlockSpec(memory_space=pltpu.VMEM)),
        scratch_shapes=front_scratch(levels, tracers, band, tile) + [pltpu.SemaphoreType.DMA],
        compiler_params=pltpu.CompilerParams(
            collective_id=1, has_side_effects=True, vmem_limit_bytes=VMEM_LIMIT
        ),
        name="second_front",
    )(state, courant, mixing)


def last_kernel(cells_ref, face_ref, sides_ref, ground_ref, out_ref, flux_ref):
    levels, tracers, _, tile = cells_ref.shape
    lane = lane_iota((8, tile))
    sides = [[sides_ref[t, p] for p in range(2)] for t in range(tracers)]

    def store(k, t, swept):
        out_ref[k, t] = swept
        if k == 0:
            flux_ref[t] = ground_ref[0, t] + swept

    sweep_columns(
        levels, tracers, lane, lambda k: face_ref[0, k], lambda k, t: cells_ref[k, t],
        lambda k, t: sides[t][k % 2], store,
    )


def last_sweep(cells, courant, sides, after_first):
    levels, tracers, band, tile = cells.shape
    return pl.pallas_call(
        last_kernel,
        grid=(band // 8,),
        out_shape=(
            jax.ShapeDtypeStruct(cells.shape, jnp.float32),
            jax.ShapeDtypeStruct(cells.shape[1:], jnp.float32),
        ),
        in_specs=[
            pl.BlockSpec((levels, tracers, 8, tile), lambda g: (0, 0, g, 0)),
            pl.BlockSpec((1, levels, 8, tile), lambda g: (0, 0, g, 0)),
            pl.BlockSpec((tracers, 2, 8, tile), lambda g: (0, 0, g, 0)),
            pl.BlockSpec((1, tracers, 8, tile), lambda g: (0, 0, g, 0)),
        ],
        out_specs=(
            pl.BlockSpec((levels, tracers, 8, tile), lambda g: (0, 0, g, 0)),
            pl.BlockSpec((tracers, 8, tile), lambda g: (0, g, 0)),
        ),
        compiler_params=pltpu.CompilerParams(vmem_limit_bytes=VMEM_LIMIT),
        name="last_sweep",
    )(cells, courant, sides, after_first)


def force_kernel(capacity, levels, lines, got_ref, state_hbm, out_hbm, rows, ids, ids_smem, state, total, *rest):
    sums, (ids_sem, load_sem, store_sem) = rest[:STREAMS], rest[STREAMS:]
    devices = got_ref.shape[0]
    cells_all = lines * LANES
    load = pltpu.make_async_copy(state_hbm, state, load_sem)
    load.start()
    low = lane_iota((HALF, LANES)) < capacity
    group = 8

    def to_smem(pair):
        return pltpu.make_async_copy(
            ids.at[pair], ids_smem.at[pl.ds(pair * LANES, LANES)], ids_sem.at[pair]
        )

    @pl.loop(0, devices // (2 * group))
    def _(part):
        for i in range(group):
            pair = part * group + i
            one, two = got_ref[2 * pair], got_ref[2 * pair + 1]
            first = jnp.where(low, one, pltpu.roll(two, capacity, 1))
            second = jnp.where(low, pltpu.roll(one, capacity, 1), two)
            cell = second[levels - HALF : levels - HALF + 1, :].astype(jnp.int32)
            ids[pl.ds(pair, 1), :] = jnp.where(cell < 0, cells_all, cell)
            wide = jnp.concatenate([first, second, jnp.zeros((LANES - 2 * HALF, LANES), jnp.float32)], axis=0)
            rows[pl.ds(pl.multiple_of(pair * LANES, LANES), LANES), :] = wide.T

    @pl.loop(0, devices // 2)
    def _(pair):
        to_smem(pair).start()

    zero = jnp.zeros((64, LANES), jnp.float32)

    @pl.loop(0, cells_all // 64)
    def _(i):
        for s in range(STREAMS):
            sums[s][pl.ds(pl.multiple_of(i * 64, 64), 64), :] = zero

    @pl.loop(0, devices // 2)
    def _(pair):
        to_smem(pair).wait()

    @pl.loop(0, devices * capacity // (4 * STREAMS))
    def _(part):
        for i in range(4):
            at = [part * 4 * STREAMS + i * STREAMS + s for s in range(STREAMS)]
            cell = [ids_smem[at[s]] for s in range(STREAMS)]
            new = [sums[s][pl.ds(cell[s], 1), :] + rows[pl.ds(at[s], 1), :] for s in range(STREAMS)]
            for s in range(STREAMS):
                sums[s][pl.ds(cell[s], 1), :] = new[s]

    load.wait()

    def stored(part):
        span = pl.ds(pl.multiple_of(part * group, group), group)
        return pltpu.make_async_copy(
            total.reshape(levels, lines, LANES).at[:, span, :], out_hbm.at[:, span, :], store_sem.at[part]
        )

    @pl.loop(0, lines // group)
    def _(part):
        turned = []
        for i in range(group):
            span = pl.ds(pl.multiple_of((part * group + i) * LANES, LANES), LANES)
            total_here = sums[0][span, :]
            for s in range(1, STREAMS):
                total_here = total_here + sums[s][span, :]
            turned.append(total_here.T[:levels])
        for i in range(group):
            at = pl.ds(part * group + i, levels, stride=lines)
            total[at, :] = state[at, :] + turned[i]
        stored(part).start()

    @pl.loop(0, lines // group)
    def _(part):
        stored(part).wait()


def add_forcing(got, after_first, capacity):
    levels, tracers, band, tile = after_first.shape
    devices = got.shape[0]
    lines = tracers * band
    out = pl.pallas_call(
        functools.partial(force_kernel, capacity, levels, lines),
        out_shape=jax.ShapeDtypeStruct((levels, lines, tile), jnp.float32),
        in_specs=[pl.BlockSpec(memory_space=pltpu.VMEM), ANY],
        out_specs=ANY,
        scratch_shapes=[
            pltpu.VMEM((devices * capacity, LANES), jnp.float32),
            pltpu.VMEM((devices // 2, LANES), jnp.int32),
            pltpu.SMEM((devices * capacity,), jnp.int32),
            pltpu.VMEM((levels * lines, tile), jnp.float32),
            pltpu.VMEM((levels * lines, tile), jnp.float32),
        ]
        + [pltpu.VMEM((lines * tile + 8, LANES), jnp.float32)] * STREAMS
        + [
            pltpu.SemaphoreType.DMA((devices // 2,)),
            pltpu.SemaphoreType.DMA,
            pltpu.SemaphoreType.DMA((lines // 8,)),
        ],
        compiler_params=pltpu.CompilerParams(vmem_limit_bytes=VMEM_LIMIT),
        name="add_forcing",
    )(got, after_first.reshape(levels * lines, tile))
    return out.reshape(after_first.shape)


def on_device(adjoint_in, courant, mixing, kernel_blocks, sounding_dest, sounding_cell):
    lon_count = lax.axis_size("lon")
    lat_count = lax.axis_size("lat")
    devices = lon_count * lat_count
    held = kernel_blocks.shape[1]
    capacity = 4 * held // devices
    owner = sounding_dest.reshape(held // LANES, LANES)
    cell = sounding_cell.reshape(held // LANES, LANES)
    blocks = pack(kernel_blocks, owner, cell, devices, capacity)
    after_first, got = first_step(adjoint_in, courant, mixing, blocks, lon_count, lat_count)
    forced = add_forcing(got, after_first, capacity)
    swept, sides = second_front(forced, courant, mixing, lon_count, lat_count)
    return last_sweep(swept, courant, sides, after_first)


def solution(mesh):
    placed = (
        P(None, None, "lat", "lon"),
        P(None, None, "lat", "lon"),
        P(None, "lat", "lon"),
        P(None, ("lon", "lat")),
        P(("lon", "lat"), None),
        P(("lon", "lat")),
    )
    return jax.shard_map(
        on_device,
        mesh=mesh,
        in_specs=placed,
        out_specs=(P(None, None, "lat", "lon"), P(None, "lat", "lon")),
        check_vma=False,
    )
```

```python
import functools
import jax
import jax.numpy as jnp
from jax import lax
from jax.experimental import pallas as pl
from jax.experimental.pallas import tpu as pltpu
from jax.sharding import PartitionSpec as P

MESH = pl.DeviceIdType.MESH
ANY = pl.BlockSpec(memory_space=pl.ANY)
LANES = 128
HALF = 40
STREAMS = 4
VMEM_LIMIT = 60 * 1024 * 1024


def lane_iota(shape):
    return lax.broadcasted_iota(jnp.int32, shape, len(shape) - 1)


def pack_kernel(
    devices, capacity, levels, blocks_ref, dest_ref, cell_ref, out_ref, rows, slots, order, order_smem, sems
):
    held = blocks_ref.shape[1]
    chunks = held // LANES
    row_id = lax.broadcasted_iota(jnp.int32, (LANES, LANES), 0)
    col_id = lax.broadcasted_iota(jnp.int32, (LANES, LANES), 1)
    before = jnp.where(row_id < col_id, 1.0, 0.0).astype(jnp.bfloat16)
    ones = jnp.ones((LANES, LANES), jnp.bfloat16)
    base = jnp.zeros((LANES, LANES), jnp.float32)

    def to_smem(chunk):
        return pltpu.make_async_copy(
            order.at[chunk], order_smem.at[pl.ds(chunk * LANES, LANES)], sems.at[chunk]
        )

    for chunk in range(chunks):
        owner = dest_ref[chunk : chunk + 1, :]
        hot = jnp.broadcast_to(owner, (LANES, LANES)) == row_id
        hot_f = jnp.where(hot, 1.0, 0.0)
        hot_b = hot_f.astype(jnp.bfloat16)
        earlier = jnp.dot(hot_b, before, preferred_element_type=jnp.float32)
        rank = jnp.sum(hot_f * (earlier + base), axis=0, keepdims=True)
        order[chunk : chunk + 1, :] = owner * capacity + rank.astype(jnp.int32)
        base = base + jnp.dot(hot_b, ones, preferred_element_type=jnp.float32)
    for chunk in range(chunks):
        to_smem(chunk).start()
    blank = jnp.where(lane_iota((64, LANES)) == levels, -1.0, 0.0)

    @pl.loop(0, devices * capacity // 64)
    def _(i):
        slots[pl.ds(pl.multiple_of(i * 64, 64), 64), :] = blank

    for chunk in range(chunks):
        span = slice(chunk * LANES, (chunk + 1) * LANES)
        tall = jnp.concatenate(
            [
                blocks_ref[:, span],
                jnp.broadcast_to(cell_ref[chunk : chunk + 1, :].astype(jnp.float32), (8, LANES)),
                jnp.zeros((LANES - levels - 8, LANES), jnp.float32),
            ],
            axis=0,
        )
        rows[span, :] = tall.T
    for chunk in range(chunks):
        to_smem(chunk).wait()

    @pl.loop(0, held // 16)
    def _(part):
        for i in range(16):
            at = part * 16 + i
            slots[pl.ds(order_smem[at], 1), :] = rows[pl.ds(at, 1), :]

    low = lane_iota((HALF, LANES)) < capacity
    group = 8

    @pl.loop(0, devices // (2 * group))
    def _(part):
        wides = []
        for i in range(group):
            at = pl.multiple_of((part * group + i) * LANES, LANES)
            wides.append(slots[pl.ds(at, LANES), :].T)
        for i, wide in enumerate(wides):
            first, second = wide[:HALF], wide[HALF : 2 * HALF]
            pair = part * group + i
            out_ref[2 * pair] = jnp.where(low, first, pltpu.roll(second, capacity, 1))
            out_ref[2 * pair + 1] = jnp.where(low, pltpu.roll(first, capacity, 1), second)


def pack(kernel_blocks, owner, cell, devices, capacity):
    levels, held = kernel_blocks.shape
    return pl.pallas_call(
        functools.partial(pack_kernel, devices, capacity, levels),
        out_shape=jax.ShapeDtypeStruct((devices, HALF, LANES), jnp.float32),
        in_specs=[pl.BlockSpec(memory_space=pltpu.VMEM)] * 3,
        out_specs=pl.BlockSpec(memory_space=pltpu.VMEM),
        scratch_shapes=[
            pltpu.VMEM((held, LANES), jnp.float32),
            pltpu.VMEM((devices * capacity, LANES), jnp.float32),
            pltpu.VMEM((held // LANES, LANES), jnp.int32),
            pltpu.SMEM((held,), jnp.int32),
            pltpu.SemaphoreType.DMA((held // LANES,)),
        ],
        compiler_params=pltpu.CompilerParams(vmem_limit_bytes=VMEM_LIMIT),
        name="pack_soundings",
    )(kernel_blocks, owner, cell)


def transport_front(lon_count, lat_count, hooks, a_hbm, c_hbm, m_hbm, front):
    (
        a_ref, c_ref, m_ref, vbuf, rbuf, send_n, send_s, send_e, send_w,
        from_s, from_n, from_w, from_e, rows_fix, merged, load_sem, send_sem, recv_sem,
    ) = front
    at_entry, after_rows, after_columns, during_columns = hooks
    levels, tracers, band, tile = a_ref.shape
    lon, lat = lax.axis_index("lon"), lax.axis_index("lat")
    north = {"lon": lon, "lat": lax.rem(lat + 1, lat_count)}
    south = {"lon": lon, "lat": lax.rem(lat + lat_count - 1, lat_count)}
    east = {"lon": lax.rem(lon + 1, lon_count), "lat": lat}
    west = {"lon": lax.rem(lon + lon_count - 1, lon_count), "lat": lat}

    loads = [
        pltpu.make_async_copy(m_hbm, m_ref, load_sem.at[0]),
        pltpu.make_async_copy(a_hbm, a_ref, load_sem.at[1]),
        pltpu.make_async_copy(c_hbm, c_ref, load_sem.at[2]),
    ]
    for load in loads:
        load.start()
    at_entry()
    loads[0].wait()
    loads[1].wait()

    mix = m_ref[0]
    inverse = 1.0 / (1.0 + mix)
    ratio = mix * inverse
    solved = a_ref[0] * inverse[None]
    rbuf[0] = ratio
    vbuf[0] = solved

    def down(k, carry):
        mix_above, ratio, solved = carry
        mix = m_ref[k]
        inverse = 1.0 / (1.0 + mix_above + mix - mix_above * ratio)
        ratio = mix * inverse
        solved = (a_ref[k] + mix_above[None] * solved) * inverse[None]
        rbuf[k] = ratio
        vbuf[k] = solved
        return mix, ratio, solved

    mix, ratio, solved = lax.fori_loop(1, levels - 1, down, (mix, ratio, solved))
    inverse = 1.0 / (1.0 + mix - mix * ratio)
    solved = (a_ref[levels - 1] + mix[None] * solved) * inverse[None]

    def keep(k, solved):
        vbuf[k] = solved
        for t in range(tracers):
            send_s[pl.ds(t * levels + k, 1), :] = solved[t, 0:1, :]
            send_n[pl.ds(t * levels + k, 1), :] = solved[t, band - 1 : band, :]

    keep(levels - 1, solved)

    def up(i, solved):
        k = levels - 2 - i
        solved = vbuf[k] + rbuf[k][None] * solved
        keep(k, solved)
        return solved

    lax.fori_loop(0, levels - 1, up, solved)

    loads[2].wait()
    edge = jnp.where(lat == lat_count - 1, 0.0, 1.0)

    @pl.loop(0, levels // 8)
    def _(j):
        for i in range(8):
            k = j * 8 + i
            send_n[pl.ds(tracers * levels + k, 1), :] = c_ref[1, k, band - 1 : band, :] * edge

    def remote(index, src, dst, to):
        return pltpu.make_async_remote_copy(
            src_ref=src, dst_ref=dst, send_sem=send_sem.at[index], recv_sem=recv_sem.at[index],
            device_id=to, device_id_type=MESH,
        )

    to_north = remote(0, send_n, from_s, north)
    to_south = remote(1, send_s, from_n, south)
    to_north.start()
    to_south.start()
    after_rows()

    top = lax.broadcasted_iota(jnp.int32, (band, tile), 0) == band - 1

    @pl.loop(0, levels // 2)
    def _(j):
        swept = []
        for i in range(2):
            face = c_ref[1, 2 * j + i]
            out_face, in_face = jnp.maximum(face, 0.0), jnp.minimum(face, 0.0)
            for t in range(tracers):
                cells = vbuf[2 * j + i, t]
                rise = jnp.where(top, 0.0, pltpu.roll(cells, band - 1, 0) - cells)
                swept.append(cells + out_face * rise + pltpu.roll(in_face * rise, 1, 0))
        for i in range(2):
            for t in range(tracers):
                vbuf[2 * j + i, t] = swept[tracers * i + t]

    lane = lane_iota((8, tile))
    zero = jnp.zeros((8, tile), jnp.float32)

    @pl.loop(0, band // 8)
    def _(g):
        span = pl.ds(pl.multiple_of(g * 8, 8), 8)
        last = zero
        for k in range(levels):
            last = jnp.where(lane == (k - 1) % tile, pltpu.roll(c_ref[0, k, span, :], k, 1), last)
        send_e[tracers, span, :] = last

    to_north.wait()
    to_south.wait()
    face_south = jnp.minimum(from_s[tracers * levels :, :], 0.0)
    face_north = jnp.maximum(send_n[tracers * levels :, :], 0.0)
    for t in range(tracers):
        part = slice(t * levels, (t + 1) * levels)
        rows_fix[part, :] = face_south * (send_s[part, :] - from_s[part, :])
        rows_fix[tracers * levels + t * levels : tracers * levels + (t + 1) * levels, :] = face_north * (
            from_n[part, :] - send_n[part, :]
        )

    row = lax.broadcasted_iota(jnp.int32, (8, tile), 0)

    def columns(g, fixed, at):
        span = pl.ds(pl.multiple_of(g * 8, 8), 8)
        for t in range(tracers):
            first, last = zero, zero
            for k in range(levels):
                cells = vbuf[k, t, span, :]
                if fixed is not None:
                    fix = rows_fix[fixed + t * levels + k : fixed + t * levels + k + 1, :]
                    cells = cells + jnp.where(row == at, jnp.broadcast_to(fix, (8, tile)), 0.0)
                    vbuf[k, t, span, :] = cells
                turned = pltpu.roll(cells, k, 1)
                first = jnp.where(lane == k, turned, first)
                last = jnp.where(lane == (k - 1) % tile, turned, last)
            send_w[t, span, :] = first
            send_e[t, span, :] = last

    columns(0, 0, 0)
    columns(band // 8 - 1, tracers * levels, 7)

    @pl.loop(1, band // 8 - 1)
    def _(g):
        columns(g, None, None)

    to_east = remote(2, send_e, from_w, east)
    to_west = remote(3, send_w, from_e, west)
    to_east.start()
    to_west.start()
    after_columns()
    during_columns()
    to_east.wait()
    to_west.wait()

    even = lax.rem(lane_iota((band, tile)), 2) == 0
    face_last = jnp.maximum(pltpu.roll(send_e[tracers], 1, 1), 0.0)
    face_first = jnp.minimum(pltpu.roll(from_w[tracers], 2, 1), 0.0)
    for t in range(tracers):
        at_last = face_last * (from_e[t] - pltpu.roll(send_e[t], 1, 1))
        at_first = face_first * (pltpu.roll(send_w[t], 1, 1) - pltpu.roll(from_w[t], 2, 1))
        merged[t, 0] = jnp.where(even, at_last, at_first)
        merged[t, 1] = jnp.where(even, at_first, at_last)


def front_scratch(levels, tracers, band, tile, merged=True):
    f32 = jnp.float32
    return [
        pltpu.VMEM((levels, tracers, band, tile), f32),
        pltpu.VMEM((2, levels, band, tile), f32),
        pltpu.VMEM((levels - 1, band, tile), f32),
        pltpu.VMEM((levels, tracers, band, tile), f32),
        pltpu.VMEM((levels - 1, band, tile), f32),
        pltpu.VMEM((levels * (tracers + 1), tile), f32),
        pltpu.VMEM((levels * tracers, tile), f32),
        pltpu.VMEM((tracers + 1, band, tile), f32),
        pltpu.VMEM((tracers, band, tile), f32),
        pltpu.VMEM((levels * (tracers + 1), tile), f32),
        pltpu.VMEM((levels * tracers, tile), f32),
        pltpu.VMEM((tracers + 1, band, tile), f32),
        pltpu.VMEM((tracers, band, tile), f32),
        pltpu.VMEM((2 * tracers * levels, tile), f32),
        pltpu.VMEM((tracers, 2, band, tile), f32),
        pltpu.SemaphoreType.DMA((3,)),
        pltpu.SemaphoreType.DMA((4,)),
        pltpu.SemaphoreType.DMA((4,)),
    ]


FRONT = 18


def sweep_columns(levels, tracers, lane, load_face, load_cells, store):
    tile = lane.shape[1]
    for k in range(levels):
        face = load_face(k)
        out_face, in_face = jnp.maximum(face, 0.0), jnp.minimum(face, 0.0)
        for t in range(tracers):
            cells = load_cells(k, t)
            rise = jnp.where(lane == tile - 1, 0.0, pltpu.roll(cells, tile - 1, 1) - cells)
            swept = cells + out_face * rise + pltpu.roll(in_face * rise, 1, 1)
            store(k, t, swept)


def add_sides(levels, tracers, lane, obuf, merged, span):
    tile = lane.shape[1]
    ends = (lane == 0) | (lane == tile - 1)
    for t in range(tracers):
        sides = [merged[t, 0, span, :], merged[t, 1, span, :]]
        for k in range(levels):
            turned = pltpu.roll(sides[k % 2], tile - 1 - k, 1)
            obuf[k, t, span, :] = obuf[k, t, span, :] + jnp.where(ends, turned, 0.0)


def peer_at(step, lon_count, lat_count):
    shift = lax.rem(step * 53, lon_count * lat_count)
    lon, lat = lax.axis_index("lon"), lax.axis_index("lat")
    wide = lon_count // 8
    x = lax.rem(lon // 8 + shift // 32, wide)
    y = lax.rem(lax.rem(lon // 2, 4) + lax.rem(shift // 8, 4), 4)
    z = lax.rem((lat // 2) * 2 + lax.rem(lon, 2) + lax.rem(shift // 2, 4), 4)
    core = lax.rem(lat + shift, 2)
    return x * 8 + y * 2 + lax.rem(z, 2), (z // 2) * 2 + core


def first_kernel(lon_count, lat_count, a_hbm, c_hbm, m_hbm, blocks_hbm, out_hbm, got_hbm, *scratch):
    front, (obuf, store_sem, trade_send, trade_recv, own_sem) = scratch[:FRONT], scratch[FRONT:]
    c_ref, vbuf, merged = front[1], front[3], front[14]
    levels, tracers, band, tile = vbuf.shape
    devices = lon_count * lat_count
    me = lax.axis_index("lon") * lat_count + lax.axis_index("lat")

    def trade(begin, end):
        @pl.loop(begin, end)
        def _(i):
            lon, lat = peer_at(i, lon_count, lat_count)
            pltpu.make_async_remote_copy(
                src_ref=blocks_hbm.at[lon * lat_count + lat], dst_ref=got_hbm.at[me],
                send_sem=trade_send, recv_sem=trade_recv,
                device_id={"lon": lon, "lat": lat}, device_id_type=MESH,
            ).start()

    cuts = (1, 1 + devices // 4, devices // 2, devices)

    def at_entry():
        barrier = pltpu.get_barrier_semaphore()

        @pl.loop(1, devices)
        def _(i):
            peer = lax.rem(me + i, devices)
            pl.semaphore_signal(
                barrier, inc=1, device_id={"lon": peer // lat_count, "lat": lax.rem(peer, lat_count)},
                device_id_type=MESH,
            )

        pl.semaphore_wait(barrier, devices - 1)
        trade(cuts[0], cuts[1])
        pltpu.make_async_copy(blocks_hbm.at[me], got_hbm.at[me], own_sem).start()

    lane = lane_iota((8, tile))

    def main_sweep():
        @pl.loop(0, band // 8)
        def _(g):
            span = pl.ds(pl.multiple_of(g * 8, 8), 8)

            def store(k, t, swept):
                obuf[k, t, span, :] = swept

            sweep_columns(
                levels, tracers, lane, lambda k: c_ref[0, k, span, :],
                lambda k, t: vbuf[k, t, span, :], store,
            )

    hooks = (at_entry, lambda: trade(cuts[1], cuts[2]), lambda: trade(cuts[2], cuts[3]), main_sweep)
    transport_front(lon_count, lat_count, hooks, a_hbm, c_hbm, m_hbm, front)

    def stored(t, r):
        return pltpu.make_async_copy(obuf.at[:, t, r, :], out_hbm.at[t, r], store_sem.at[t * band + r])

    @pl.loop(0, band // 8)
    def _(g):
        add_sides(levels, tracers, lane, obuf, merged, pl.ds(pl.multiple_of(g * 8, 8), 8))
        for t in range(tracers):
            for r in range(8):
                stored(t, g * 8 + r).start()

    pltpu.make_async_copy(blocks_hbm.at[me], got_hbm.at[me], own_sem).wait()
    most = pl.ds(0, devices - 1)
    pltpu.make_async_remote_copy(
        src_ref=blocks_hbm.at[most], dst_ref=got_hbm.at[most],
        send_sem=trade_send, recv_sem=trade_recv,
        device_id={"lon": lax.axis_index("lon"), "lat": lax.rem(lax.axis_index("lat") + 1, lat_count)},
        device_id_type=MESH,
    ).wait()

    @pl.loop(0, band)
    def _(r):
        for t in range(tracers):
            stored(t, r).wait()


def second_kernel(lon_count, lat_count, a_hbm, c_hbm, m_hbm, out_hbm, sides_ref, *scratch):
    front, (store_sem,) = scratch[:FRONT], scratch[FRONT:]
    vbuf, merged = front[3], front[14]

    def at_entry():
        lon, lat = lax.axis_index("lon"), lax.axis_index("lat")
        barrier = pltpu.get_barrier_semaphore()
        for d_lon, d_lat in ((1, 0), (lon_count - 1, 0), (0, 1), (0, lat_count - 1)):
            pl.semaphore_signal(
                barrier, inc=1,
                device_id={"lon": lax.rem(lon + d_lon, lon_count), "lat": lax.rem(lat + d_lat, lat_count)},
                device_id_type=MESH,
            )
        pl.semaphore_wait(barrier, 4)

    store = pltpu.make_async_copy(vbuf, out_hbm, store_sem)
    hooks = (at_entry, lambda: None, store.start, lambda: None)
    transport_front(lon_count, lat_count, hooks, a_hbm, c_hbm, m_hbm, front)
    sides_ref[...] = merged[...]
    store.wait()


def first_step(state, courant, mixing, blocks, lon_count, lat_count):
    levels, tracers, band, tile = state.shape
    return pl.pallas_call(
        functools.partial(first_kernel, lon_count, lat_count),
        out_shape=(
            jax.ShapeDtypeStruct((tracers, band, levels, tile), jnp.float32),
            jax.ShapeDtypeStruct(blocks.shape, jnp.float32),
        ),
        in_specs=[ANY] * 4,
        out_specs=(ANY, ANY),
        scratch_shapes=front_scratch(levels, tracers, band, tile)
        + [
            pltpu.VMEM((levels, tracers, band, tile), jnp.float32),
            pltpu.SemaphoreType.DMA((tracers * band,)),
            pltpu.SemaphoreType.DMA,
            pltpu.SemaphoreType.DMA,
            pltpu.SemaphoreType.DMA,
        ],
        compiler_params=pltpu.CompilerParams(
            collective_id=0, has_side_effects=True, vmem_limit_bytes=VMEM_LIMIT
        ),
        name="first_step",
    )(state, courant, mixing, blocks)


def second_front(state, courant, mixing, lon_count, lat_count):
    levels, tracers, band, tile = state.shape
    return pl.pallas_call(
        functools.partial(second_kernel, lon_count, lat_count),
        out_shape=(
            jax.ShapeDtypeStruct(state.shape, jnp.float32),
            jax.ShapeDtypeStruct((tracers, 2, band, tile), jnp.float32),
        ),
        in_specs=[ANY] * 3,
        out_specs=(ANY, pl.BlockSpec(memory_space=pltpu.VMEM)),
        scratch_shapes=front_scratch(levels, tracers, band, tile) + [pltpu.SemaphoreType.DMA],
        compiler_params=pltpu.CompilerParams(
            collective_id=1, has_side_effects=True, vmem_limit_bytes=VMEM_LIMIT
        ),
        name="second_front",
    )(state, courant, mixing)


def last_kernel(
    cells_hbm, c_hbm, sides_ref, first_hbm, out_hbm, flux_ref, cells, faces, obuf, ground, cell_sem, face_sem,
    store_sem, ground_sem,
):
    levels, tracers, band, tile = cells.shape
    lane = lane_iota((8, tile))

    def rows_of(g):
        return pl.ds(pl.multiple_of(g * 8, 8), 8)

    def load_cells(g):
        return pltpu.make_async_copy(
            cells_hbm.at[:, :, rows_of(g), :], cells.at[:, :, rows_of(g), :], cell_sem.at[g]
        )

    def load_faces(g):
        return pltpu.make_async_copy(
            c_hbm.at[0, :, rows_of(g), :], faces.at[:, rows_of(g), :], face_sem.at[g]
        )

    def stored(g):
        return pltpu.make_async_copy(
            obuf.at[:, :, rows_of(g), :], out_hbm.at[:, :, rows_of(g), :], store_sem.at[g]
        )

    @pl.loop(0, band // 8)
    def _(g):
        load_cells(g).start()
        load_faces(g).start()

    load_ground = pltpu.make_async_copy(first_hbm.at[:, :, 0, :], ground, ground_sem)
    load_ground.start()

    @pl.loop(0, band // 8)
    def _(g):
        load_cells(g).wait()
        load_faces(g).wait()
        span = rows_of(g)

        def store(k, t, swept):
            obuf[k, t, span, :] = swept

        sweep_columns(
            levels, tracers, lane, lambda k: faces[k, span, :], lambda k, t: cells[k, t, span, :], store
        )

    @pl.loop(0, band // 8)
    def _(g):
        add_sides(levels, tracers, lane, obuf, sides_ref, rows_of(g))
        stored(g).start()

    load_ground.wait()
    flux_ref[...] = ground[...] + obuf[0]

    @pl.loop(0, band // 8)
    def _(g):
        stored(g).wait()


def last_sweep(cells, courant, sides, after_first):
    levels, tracers, band, tile = cells.shape
    return pl.pallas_call(
        last_kernel,
        out_shape=(
            jax.ShapeDtypeStruct(cells.shape, jnp.float32),
            jax.ShapeDtypeStruct(cells.shape[1:], jnp.float32),
        ),
        in_specs=[ANY, ANY, pl.BlockSpec(memory_space=pltpu.VMEM), ANY],
        out_specs=(ANY, pl.BlockSpec(memory_space=pltpu.VMEM)),
        scratch_shapes=[
            pltpu.VMEM((levels, tracers, band, tile), jnp.float32),
            pltpu.VMEM((levels, band, tile), jnp.float32),
            pltpu.VMEM((levels, tracers, band, tile), jnp.float32),
            pltpu.VMEM((tracers, band, tile), jnp.float32),
            pltpu.SemaphoreType.DMA((band // 8,)),
            pltpu.SemaphoreType.DMA((band // 8,)),
            pltpu.SemaphoreType.DMA((band // 8,)),
            pltpu.SemaphoreType.DMA,
        ],
        compiler_params=pltpu.CompilerParams(vmem_limit_bytes=VMEM_LIMIT),
        name="last_sweep",
    )(cells, courant, sides, after_first)


def force_kernel(capacity, levels, lines, got_ref, state_hbm, out_hbm, rows, ids, ids_smem, state, total, *rest):
    sums, (ids_sem, load_sem, store_sem) = rest[:STREAMS], rest[STREAMS:]
    devices = got_ref.shape[0]
    cells_all = lines * LANES
    load = pltpu.make_async_copy(state_hbm, state, load_sem)
    load.start()
    low = lane_iota((HALF, LANES)) < capacity
    group = 8

    def to_smem(pair):
        return pltpu.make_async_copy(
            ids.at[pair], ids_smem.at[pl.ds(pair * LANES, LANES)], ids_sem.at[pair]
        )

    @pl.loop(0, devices // (2 * group))
    def _(part):
        for i in range(group):
            pair = part * group + i
            one, two = got_ref[2 * pair], got_ref[2 * pair + 1]
            first = jnp.where(low, one, pltpu.roll(two, capacity, 1))
            second = jnp.where(low, pltpu.roll(one, capacity, 1), two)
            cell = second[levels - HALF : levels - HALF + 1, :].astype(jnp.int32)
            ids[pl.ds(pair, 1), :] = jnp.where(cell < 0, cells_all, cell)
            wide = jnp.concatenate([first, second, jnp.zeros((LANES - 2 * HALF, LANES), jnp.float32)], axis=0)
            rows[pl.ds(pl.multiple_of(pair * LANES, LANES), LANES), :] = wide.T

    @pl.loop(0, devices // 2)
    def _(pair):
        to_smem(pair).start()

    zero = jnp.zeros((64, LANES), jnp.float32)

    @pl.loop(0, cells_all // 64)
    def _(i):
        for s in range(STREAMS):
            sums[s][pl.ds(pl.multiple_of(i * 64, 64), 64), :] = zero

    @pl.loop(0, devices // 2)
    def _(pair):
        to_smem(pair).wait()

    @pl.loop(0, devices * capacity // (8 * STREAMS))
    def _(part):
        for i in range(8):
            at = [part * 8 * STREAMS + i * STREAMS + s for s in range(STREAMS)]
            cell = [ids_smem[at[s]] for s in range(STREAMS)]
            new = [sums[s][pl.ds(cell[s], 1), :] + rows[pl.ds(at[s], 1), :] for s in range(STREAMS)]
            for s in range(STREAMS):
                sums[s][pl.ds(cell[s], 1), :] = new[s]

    load.wait()

    def level_rows(line):
        return pl.ds(pl.multiple_of(line * levels, 8), levels)

    def stored(line):
        return pltpu.make_async_copy(total.at[level_rows(line)], out_hbm.at[:, line, :], store_sem.at[line])

    @pl.loop(0, lines // group)
    def _(part):
        turned = []
        for i in range(group):
            span = pl.ds(pl.multiple_of((part * group + i) * LANES, LANES), LANES)
            total_here = sums[0][span, :]
            for s in range(1, STREAMS):
                total_here = total_here + sums[s][span, :]
            turned.append(total_here.T[:levels])
        for i in range(group):
            at = level_rows(part * group + i)
            total[at, :] = state[at, :] + turned[i]
        for i in range(group):
            stored(part * group + i).start()

    @pl.loop(0, lines)
    def _(line):
        stored(line).wait()


def add_forcing(got, after_first, capacity):
    tracers, band, levels, tile = after_first.shape
    devices = got.shape[0]
    lines = tracers * band
    out = pl.pallas_call(
        functools.partial(force_kernel, capacity, levels, lines),
        out_shape=jax.ShapeDtypeStruct((levels, lines, tile), jnp.float32),
        in_specs=[pl.BlockSpec(memory_space=pltpu.VMEM), ANY],
        out_specs=ANY,
        scratch_shapes=[
            pltpu.VMEM((devices * capacity, LANES), jnp.float32),
            pltpu.VMEM((devices // 2, LANES), jnp.int32),
            pltpu.SMEM((devices * capacity,), jnp.int32),
            pltpu.VMEM((levels * lines, tile), jnp.float32),
            pltpu.VMEM((levels * lines, tile), jnp.float32),
        ]
        + [pltpu.VMEM((lines * tile + 8, LANES), jnp.float32)] * STREAMS
        + [
            pltpu.SemaphoreType.DMA((devices // 2,)),
            pltpu.SemaphoreType.DMA,
            pltpu.SemaphoreType.DMA((lines,)),
        ],
        compiler_params=pltpu.CompilerParams(vmem_limit_bytes=VMEM_LIMIT),
        name="add_forcing",
    )(got, after_first.reshape(levels * lines, tile))
    return out.reshape(levels, tracers, band, tile)


def on_device(adjoint_in, courant, mixing, kernel_blocks, sounding_dest, sounding_cell):
    lon_count = lax.axis_size("lon")
    lat_count = lax.axis_size("lat")
    devices = lon_count * lat_count
    held = kernel_blocks.shape[1]
    capacity = 4 * held // devices
    owner = sounding_dest.reshape(held // LANES, LANES)
    cell = sounding_cell.reshape(held // LANES, LANES)
    blocks = pack(kernel_blocks, owner, cell, devices, capacity)
    after_first, got = first_step(adjoint_in, courant, mixing, blocks, lon_count, lat_count)
    forced = add_forcing(got, after_first, capacity)
    swept, sides = second_front(forced, courant, mixing, lon_count, lat_count)
    return last_sweep(swept, courant, sides, after_first)


def solution(mesh):
    placed = (
        P(None, None, "lat", "lon"),
        P(None, None, "lat", "lon"),
        P(None, "lat", "lon"),
        P(None, ("lon", "lat")),
        P(("lon", "lat"), None),
        P(("lon", "lat")),
    )
    return jax.shard_map(
        on_device,
        mesh=mesh,
        in_specs=placed,
        out_specs=(P(None, None, "lat", "lon"), P(None, "lat", "lon")),
        check_vma=False,
    )
```

```python
import functools
import jax
import jax.numpy as jnp
from jax import lax
from jax.experimental import pallas as pl
from jax.experimental.pallas import tpu as pltpu
from jax.sharding import PartitionSpec as P

MESH = pl.DeviceIdType.MESH
ANY = pl.BlockSpec(memory_space=pl.ANY)
LANES = 128
HALF = 37
ROOM = 40
STREAMS = 4
CHUNKS = 4
VMEM_LIMIT = 60 * 1024 * 1024


def lane_iota(shape):
    return lax.broadcasted_iota(jnp.int32, shape, len(shape) - 1)


def pack_kernel(
    devices, capacity, levels, blocks_ref, dest_ref, cell_ref, out_ref, rows, slots, order, order_smem, sems
):
    held = blocks_ref.shape[1]
    chunks = held // LANES
    row_id = lax.broadcasted_iota(jnp.int32, (LANES, LANES), 0)
    col_id = lax.broadcasted_iota(jnp.int32, (LANES, LANES), 1)
    before = jnp.where(row_id < col_id, 1.0, 0.0).astype(jnp.bfloat16)
    ones = jnp.ones((LANES, LANES), jnp.bfloat16)
    base = jnp.zeros((LANES, LANES), jnp.float32)

    def to_smem(chunk):
        return pltpu.make_async_copy(
            order.at[chunk], order_smem.at[pl.ds(chunk * LANES, LANES)], sems.at[chunk]
        )

    for chunk in range(chunks):
        owner = dest_ref[chunk : chunk + 1, :]
        hot = jnp.broadcast_to(owner, (LANES, LANES)) == row_id
        hot_f = jnp.where(hot, 1.0, 0.0)
        hot_b = hot_f.astype(jnp.bfloat16)
        earlier = jnp.dot(hot_b, before, preferred_element_type=jnp.float32)
        rank = jnp.sum(hot_f * (earlier + base), axis=0, keepdims=True)
        order[chunk : chunk + 1, :] = owner * capacity + rank.astype(jnp.int32)
        base = base + jnp.dot(hot_b, ones, preferred_element_type=jnp.float32)
    for chunk in range(chunks):
        to_smem(chunk).start()
    blank = jnp.where(lane_iota((64, LANES)) == levels, -1.0, 0.0)

    @pl.loop(0, devices * capacity // 64)
    def _(i):
        slots[pl.ds(pl.multiple_of(i * 64, 64), 64), :] = blank

    for chunk in range(chunks):
        span = slice(chunk * LANES, (chunk + 1) * LANES)
        tall = jnp.concatenate(
            [
                blocks_ref[:, span],
                jnp.broadcast_to(cell_ref[chunk : chunk + 1, :].astype(jnp.float32), (8, LANES)),
                jnp.zeros((LANES - levels - 8, LANES), jnp.float32),
            ],
            axis=0,
        )
        rows[span, :] = tall.T
    for chunk in range(chunks):
        to_smem(chunk).wait()

    @pl.loop(0, held // 16)
    def _(part):
        for i in range(16):
            at = part * 16 + i
            slots[pl.ds(order_smem[at], 1), :] = rows[pl.ds(at, 1), :]

    low = lane_iota((HALF, LANES)) < capacity
    group = 8

    @pl.loop(0, devices // (2 * group))
    def _(part):
        wides = []
        for i in range(group):
            at = pl.multiple_of((part * group + i) * LANES, LANES)
            wides.append(slots[pl.ds(at, LANES), :].T)
        for i, wide in enumerate(wides):
            first, second = wide[:HALF], wide[HALF : 2 * HALF]
            pair = part * group + i
            out_ref[2 * pair, :HALF] = jnp.where(low, first, pltpu.roll(second, capacity, 1))
            out_ref[2 * pair + 1, :HALF] = jnp.where(low, pltpu.roll(first, capacity, 1), second)


def pack(kernel_blocks, owner, cell, devices, capacity):
    levels, held = kernel_blocks.shape
    return pl.pallas_call(
        functools.partial(pack_kernel, devices, capacity, levels),
        out_shape=jax.ShapeDtypeStruct((devices, ROOM, LANES), jnp.float32),
        in_specs=[pl.BlockSpec(memory_space=pltpu.VMEM)] * 3,
        out_specs=pl.BlockSpec(memory_space=pltpu.VMEM),
        scratch_shapes=[
            pltpu.VMEM((held, LANES), jnp.float32),
            pltpu.VMEM((devices * capacity, LANES), jnp.float32),
            pltpu.VMEM((held // LANES, LANES), jnp.int32),
            pltpu.SMEM((held,), jnp.int32),
            pltpu.SemaphoreType.DMA((held // LANES,)),
        ],
        compiler_params=pltpu.CompilerParams(vmem_limit_bytes=VMEM_LIMIT),
        name="pack_soundings",
    )(kernel_blocks, owner, cell)


def transport_front(lon_count, lat_count, hooks, a_hbm, c_hbm, m_hbm, front):
    (
        a_ref, c_ref, m_ref, vbuf, rbuf, send_n, send_s, send_e, send_w,
        from_s, from_n, from_w, from_e, rows_fix, merged, load_sem, send_sem, recv_sem,
    ) = front
    at_entry, before_rows, after_rows, after_columns, during_columns = hooks
    levels, tracers, band, tile = a_ref.shape
    lon, lat = lax.axis_index("lon"), lax.axis_index("lat")
    north = {"lon": lon, "lat": lax.rem(lat + 1, lat_count)}
    south = {"lon": lon, "lat": lax.rem(lat + lat_count - 1, lat_count)}
    east = {"lon": lax.rem(lon + 1, lon_count), "lat": lat}
    west = {"lon": lax.rem(lon + lon_count - 1, lon_count), "lat": lat}

    cuts = [levels * i // CHUNKS for i in range(CHUNKS)] + [levels]
    loads = []
    for i in range(CHUNKS):
        span, faces = slice(cuts[i], cuts[i + 1]), slice(cuts[i], min(cuts[i + 1], levels - 1))
        loads.append(pltpu.make_async_copy(m_hbm.at[faces], m_ref.at[faces], load_sem.at[2 * i]))
        loads.append(pltpu.make_async_copy(a_hbm.at[span], a_ref.at[span], load_sem.at[2 * i + 1]))
    loads.append(pltpu.make_async_copy(c_hbm, c_ref, load_sem.at[2 * CHUNKS]))
    for load in loads:
        load.start()
    at_entry()
    loads[0].wait()
    loads[1].wait()

    mix = m_ref[0]
    inverse = 1.0 / (1.0 + mix)
    ratio = mix * inverse
    solved = a_ref[0] * inverse[None]
    rbuf[0] = ratio
    vbuf[0] = solved

    def down(k, carry):
        mix_above, ratio, solved = carry
        mix = m_ref[k]
        inverse = 1.0 / (1.0 + mix_above + mix - mix_above * ratio)
        ratio = mix * inverse
        solved = (a_ref[k] + mix_above[None] * solved) * inverse[None]
        rbuf[k] = ratio
        vbuf[k] = solved
        return mix, ratio, solved

    carry = (mix, ratio, solved)
    for i in range(CHUNKS):
        if i > 0:
            loads[2 * i].wait()
            loads[2 * i + 1].wait()
        carry = lax.fori_loop(max(cuts[i], 1), min(cuts[i + 1], levels - 1), down, carry)
    mix, ratio, solved = carry
    inverse = 1.0 / (1.0 + mix - mix * ratio)
    solved = (a_ref[levels - 1] + mix[None] * solved) * inverse[None]

    def keep(k, solved):
        vbuf[k] = solved
        for t in range(tracers):
            send_s[pl.ds(t * levels + k, 1), :] = solved[t, 0:1, :]
            send_n[pl.ds(t * levels + k, 1), :] = solved[t, band - 1 : band, :]

    keep(levels - 1, solved)

    def up(i, solved):
        k = levels - 2 - i
        solved = vbuf[k] + rbuf[k][None] * solved
        keep(k, solved)
        return solved

    lax.fori_loop(0, levels - 1, up, solved)

    loads[2 * CHUNKS].wait()
    edge = jnp.where(lat == lat_count - 1, 0.0, 1.0)

    @pl.loop(0, levels // 8)
    def _(j):
        for i in range(8):
            k = j * 8 + i
            send_n[pl.ds(tracers * levels + k, 1), :] = c_ref[1, k, band - 1 : band, :] * edge

    def remote(index, src, dst, to):
        return pltpu.make_async_remote_copy(
            src_ref=src, dst_ref=dst, send_sem=send_sem.at[index], recv_sem=recv_sem.at[index],
            device_id=to, device_id_type=MESH,
        )

    to_north = remote(0, send_n, from_s, north)
    to_south = remote(1, send_s, from_n, south)
    before_rows()
    to_north.start()
    to_south.start()
    after_rows()

    top = lax.broadcasted_iota(jnp.int32, (band, tile), 0) == band - 1

    @pl.loop(0, levels // 2)
    def _(j):
        swept = []
        for i in range(2):
            face = c_ref[1, 2 * j + i]
            out_face, in_face = jnp.maximum(face, 0.0), jnp.minimum(face, 0.0)
            for t in range(tracers):
                cells = vbuf[2 * j + i, t]
                rise = jnp.where(top, 0.0, pltpu.roll(cells, band - 1, 0) - cells)
                swept.append(cells + out_face * rise + pltpu.roll(in_face * rise, 1, 0))
        for i in range(2):
            for t in range(tracers):
                vbuf[2 * j + i, t] = swept[tracers * i + t]

    lane = lane_iota((8, tile))
    zero = jnp.zeros((8, tile), jnp.float32)

    @pl.loop(0, band // 8)
    def _(g):
        span = pl.ds(pl.multiple_of(g * 8, 8), 8)
        last = zero
        for k in range(levels):
            last = jnp.where(lane == (k - 1) % tile, pltpu.roll(c_ref[0, k, span, :], k, 1), last)
        send_e[tracers, span, :] = last

    to_north.wait()
    to_south.wait()
    face_south = jnp.minimum(from_s[tracers * levels :, :], 0.0)
    face_north = jnp.maximum(send_n[tracers * levels :, :], 0.0)
    for t in range(tracers):
        part = slice(t * levels, (t + 1) * levels)
        rows_fix[part, :] = face_south * (send_s[part, :] - from_s[part, :])
        rows_fix[tracers * levels + t * levels : tracers * levels + (t + 1) * levels, :] = face_north * (
            from_n[part, :] - send_n[part, :]
        )

    row = lax.broadcasted_iota(jnp.int32, (8, tile), 0)

    def columns(g, fixed, at):
        span = pl.ds(pl.multiple_of(g * 8, 8), 8)
        for t in range(tracers):
            first, last = zero, zero
            for k in range(levels):
                cells = vbuf[k, t, span, :]
                if fixed is not None:
                    fix = rows_fix[fixed + t * levels + k : fixed + t * levels + k + 1, :]
                    cells = cells + jnp.where(row == at, jnp.broadcast_to(fix, (8, tile)), 0.0)
                    vbuf[k, t, span, :] = cells
                turned = pltpu.roll(cells, k, 1)
                first = jnp.where(lane == k, turned, first)
                last = jnp.where(lane == (k - 1) % tile, turned, last)
            send_w[t, span, :] = first
            send_e[t, span, :] = last

    columns(0, 0, 0)
    columns(band // 8 - 1, tracers * levels, 7)

    @pl.loop(1, band // 8 - 1)
    def _(g):
        columns(g, None, None)

    to_east = remote(2, send_e, from_w, east)
    to_west = remote(3, send_w, from_e, west)
    to_east.start()
    to_west.start()
    after_columns()
    during_columns()
    to_east.wait()
    to_west.wait()

    even = lax.rem(lane_iota((band, tile)), 2) == 0
    face_last = jnp.maximum(pltpu.roll(send_e[tracers], 1, 1), 0.0)
    face_first = jnp.minimum(pltpu.roll(from_w[tracers], 2, 1), 0.0)
    for t in range(tracers):
        at_last = face_last * (from_e[t] - pltpu.roll(send_e[t], 1, 1))
        at_first = face_first * (pltpu.roll(send_w[t], 1, 1) - pltpu.roll(from_w[t], 2, 1))
        merged[t, 0] = jnp.where(even, at_last, at_first)
        merged[t, 1] = jnp.where(even, at_first, at_last)


def front_scratch(levels, tracers, band, tile, merged=True):
    f32 = jnp.float32
    return [
        pltpu.VMEM((levels, tracers, band, tile), f32),
        pltpu.VMEM((2, levels, band, tile), f32),
        pltpu.VMEM((levels - 1, band, tile), f32),
        pltpu.VMEM((levels, tracers, band, tile), f32),
        pltpu.VMEM((levels - 1, band, tile), f32),
        pltpu.VMEM((levels * (tracers + 1), tile), f32),
        pltpu.VMEM((levels * tracers, tile), f32),
        pltpu.VMEM((tracers + 1, band, tile), f32),
        pltpu.VMEM((tracers, band, tile), f32),
        pltpu.VMEM((levels * (tracers + 1), tile), f32),
        pltpu.VMEM((levels * tracers, tile), f32),
        pltpu.VMEM((tracers + 1, band, tile), f32),
        pltpu.VMEM((tracers, band, tile), f32),
        pltpu.VMEM((2 * tracers * levels, tile), f32),
        pltpu.VMEM((tracers, 2, band, tile), f32),
        pltpu.SemaphoreType.DMA((2 * CHUNKS + 1,)),
        pltpu.SemaphoreType.DMA((4,)),
        pltpu.SemaphoreType.DMA((4,)),
    ]


FRONT = 18


def sweep_all(c_ref, vbuf, obuf, done):
    levels, tracers, band, tile = vbuf.shape
    lane = lane_iota((8, tile))

    @pl.loop(0, band // 8)
    def _(g):
        span = pl.ds(pl.multiple_of(g * 8, 8), 8)
        for k in range(levels):
            face = c_ref[0, k, span, :]
            out_face, in_face = jnp.maximum(face, 0.0), jnp.minimum(face, 0.0)
            for t in range(tracers):
                cells = vbuf[k, t, span, :]
                rise = jnp.where(lane == tile - 1, 0.0, pltpu.roll(cells, tile - 1, 1) - cells)
                obuf[k, t, span, :] = cells + out_face * rise + pltpu.roll(in_face * rise, 1, 1)
        done(g)


def add_sides(cells, merged, span, out):
    levels, tracers, band, tile = cells.shape
    lane = lane_iota((8, tile))
    ends = (lane == 0) | (lane == tile - 1)
    for t in range(tracers):
        sides = [merged[t, 0, span, :], merged[t, 1, span, :]]
        for k in range(levels):
            turned = pltpu.roll(sides[k % 2], tile - 1 - k, 1)
            out[k, t, span, :] = cells[k, t, span, :] + jnp.where(ends, turned, 0.0)


def peer_at(step, lon_count, lat_count):
    shift = lax.rem(step * 53, lon_count * lat_count)
    lon, lat = lax.axis_index("lon"), lax.axis_index("lat")
    wide = lon_count // 8
    x = lax.rem(lon // 8 + shift // 32, wide)
    y = lax.rem(lax.rem(lon // 2, 4) + lax.rem(shift // 8, 4), 4)
    z = lax.rem((lat // 2) * 2 + lax.rem(lon, 2) + lax.rem(shift // 2, 4), 4)
    core = lax.rem(lat + shift, 2)
    return x * 8 + y * 2 + lax.rem(z, 2), (z // 2) * 2 + core


def first_kernel(lon_count, lat_count, a_hbm, c_hbm, m_hbm, blocks_hbm, out_hbm, got_hbm, *scratch):
    front, (obuf, store_sem, trade_send, trade_recv, own_sem) = scratch[:FRONT], scratch[FRONT:]
    c_ref, vbuf, merged = front[1], front[3], front[14]
    levels, tracers, band, tile = vbuf.shape
    devices = lon_count * lat_count
    me = lax.axis_index("lon") * lat_count + lax.axis_index("lat")
    used = pl.ds(0, HALF)

    def trade(begin, end):
        @pl.loop(begin, end)
        def _(i):
            lon, lat = peer_at(i, lon_count, lat_count)
            pltpu.make_async_remote_copy(
                src_ref=blocks_hbm.at[lon * lat_count + lat, used], dst_ref=got_hbm.at[me, used],
                send_sem=trade_send, recv_sem=trade_recv,
                device_id={"lon": lon, "lat": lat}, device_id_type=MESH,
            ).start()

    early = 1 + devices // 5

    def at_entry():
        barrier = pltpu.get_barrier_semaphore()

        @pl.loop(1, devices)
        def _(i):
            peer = lax.rem(me + i, devices)
            pl.semaphore_signal(
                barrier, inc=1, device_id={"lon": peer // lat_count, "lat": lax.rem(peer, lat_count)},
                device_id_type=MESH,
            )

        pltpu.make_async_copy(blocks_hbm.at[me], got_hbm.at[me], own_sem).start()

    def before_rows():
        pl.semaphore_wait(pltpu.get_barrier_semaphore(), devices - 1)

    def main_sweep():
        sweep_all(c_ref, vbuf, obuf, lambda g: None)

    hooks = (at_entry, before_rows, lambda: trade(1, early), lambda: trade(early, devices), main_sweep)
    transport_front(lon_count, lat_count, hooks, a_hbm, c_hbm, m_hbm, front)

    def stored(t, r):
        return pltpu.make_async_copy(obuf.at[:, t, r, :], out_hbm.at[t, r], store_sem.at[t * band + r])

    @pl.loop(0, band // 8)
    def _(g):
        add_sides(obuf, merged, pl.ds(pl.multiple_of(g * 8, 8), 8), obuf)
        for t in range(tracers):
            for r in range(8):
                stored(t, g * 8 + r).start()

    pltpu.make_async_copy(blocks_hbm.at[me], got_hbm.at[me], own_sem).wait()
    most = pl.ds(0, devices - 1)
    pltpu.make_async_remote_copy(
        src_ref=blocks_hbm.at[most, used], dst_ref=got_hbm.at[most, used],
        send_sem=trade_send, recv_sem=trade_recv,
        device_id={"lon": lax.axis_index("lon"), "lat": lax.rem(lax.axis_index("lat") + 1, lat_count)},
        device_id_type=MESH,
    ).wait()

    @pl.loop(0, band)
    def _(r):
        for t in range(tracers):
            stored(t, r).wait()


def second_kernel(lon_count, lat_count, a_hbm, c_hbm, m_hbm, out_hbm, sides_ref, *scratch):
    front, (obuf, store_sem) = scratch[:FRONT], scratch[FRONT:]
    c_ref, vbuf, merged = front[1], front[3], front[14]
    band = vbuf.shape[2]

    def at_entry():
        lon, lat = lax.axis_index("lon"), lax.axis_index("lat")
        barrier = pltpu.get_barrier_semaphore()
        for d_lon, d_lat in ((1, 0), (lon_count - 1, 0), (0, 1), (0, lat_count - 1)):
            pl.semaphore_signal(
                barrier, inc=1,
                device_id={"lon": lax.rem(lon + d_lon, lon_count), "lat": lax.rem(lat + d_lat, lat_count)},
                device_id_type=MESH,
            )

    def before_rows():
        pl.semaphore_wait(pltpu.get_barrier_semaphore(), 4)

    def stored(g):
        span = pl.ds(pl.multiple_of(g * 8, 8), 8)
        return pltpu.make_async_copy(obuf.at[:, :, span, :], out_hbm.at[:, :, span, :], store_sem.at[g])

    def main_sweep():
        sweep_all(c_ref, vbuf, obuf, lambda g: stored(g).start())

    hooks = (at_entry, before_rows, lambda: None, lambda: None, main_sweep)
    transport_front(lon_count, lat_count, hooks, a_hbm, c_hbm, m_hbm, front)
    sides_ref[...] = merged[...]

    @pl.loop(0, band // 8)
    def _(g):
        stored(g).wait()


def first_step(state, courant, mixing, blocks, lon_count, lat_count):
    levels, tracers, band, tile = state.shape
    return pl.pallas_call(
        functools.partial(first_kernel, lon_count, lat_count),
        out_shape=(
            jax.ShapeDtypeStruct((tracers, band, levels, tile), jnp.float32),
            jax.ShapeDtypeStruct(blocks.shape, jnp.float32),
        ),
        in_specs=[ANY] * 4,
        out_specs=(ANY, ANY),
        scratch_shapes=front_scratch(levels, tracers, band, tile)
        + [
            pltpu.VMEM((levels, tracers, band, tile), jnp.float32),
            pltpu.SemaphoreType.DMA((tracers * band,)),
            pltpu.SemaphoreType.DMA,
            pltpu.SemaphoreType.DMA,
            pltpu.SemaphoreType.DMA,
        ],
        compiler_params=pltpu.CompilerParams(
            collective_id=0, has_side_effects=True, vmem_limit_bytes=VMEM_LIMIT
        ),
        name="first_step",
    )(state, courant, mixing, blocks)


def second_front(state, courant, mixing, lon_count, lat_count):
    levels, tracers, band, tile = state.shape
    return pl.pallas_call(
        functools.partial(second_kernel, lon_count, lat_count),
        out_shape=(
            jax.ShapeDtypeStruct(state.shape, jnp.float32),
            jax.ShapeDtypeStruct((tracers, 2, band, tile), jnp.float32),
        ),
        in_specs=[ANY] * 3,
        out_specs=(ANY, pl.BlockSpec(memory_space=pltpu.VMEM)),
        scratch_shapes=front_scratch(levels, tracers, band, tile)
        + [pltpu.VMEM((levels, tracers, band, tile), jnp.float32), pltpu.SemaphoreType.DMA((band // 8,))],
        compiler_params=pltpu.CompilerParams(
            collective_id=1, has_side_effects=True, vmem_limit_bytes=VMEM_LIMIT
        ),
        name="second_front",
    )(state, courant, mixing)


def last_kernel(
    cells_hbm, sides_ref, first_hbm, out_hbm, flux_ref, cells, obuf, ground, cell_sem, store_sem, ground_sem
):
    band = cells.shape[2]

    def rows_of(g):
        return pl.ds(pl.multiple_of(g * 8, 8), 8)

    def load(g):
        return pltpu.make_async_copy(
            cells_hbm.at[:, :, rows_of(g), :], cells.at[:, :, rows_of(g), :], cell_sem.at[g]
        )

    def stored(g):
        return pltpu.make_async_copy(
            obuf.at[:, :, rows_of(g), :], out_hbm.at[:, :, rows_of(g), :], store_sem.at[g]
        )

    @pl.loop(0, band // 8)
    def _(g):
        load(g).start()

    load_ground = pltpu.make_async_copy(first_hbm.at[:, :, 0, :], ground, ground_sem)
    load_ground.start()

    @pl.loop(0, band // 8)
    def _(g):
        load(g).wait()
        add_sides(cells, sides_ref, rows_of(g), obuf)
        stored(g).start()

    load_ground.wait()
    flux_ref[...] = ground[...] + obuf[0]

    @pl.loop(0, band // 8)
    def _(g):
        stored(g).wait()


def last_part(cells, sides, after_first):
    levels, tracers, band, tile = cells.shape
    return pl.pallas_call(
        last_kernel,
        out_shape=(
            jax.ShapeDtypeStruct(cells.shape, jnp.float32),
            jax.ShapeDtypeStruct(cells.shape[1:], jnp.float32),
        ),
        in_specs=[ANY, pl.BlockSpec(memory_space=pltpu.VMEM), ANY],
        out_specs=(ANY, pl.BlockSpec(memory_space=pltpu.VMEM)),
        scratch_shapes=[
            pltpu.VMEM((levels, tracers, band, tile), jnp.float32),
            pltpu.VMEM((levels, tracers, band, tile), jnp.float32),
            pltpu.VMEM((tracers, band, tile), jnp.float32),
            pltpu.SemaphoreType.DMA((band // 8,)),
            pltpu.SemaphoreType.DMA((band // 8,)),
            pltpu.SemaphoreType.DMA,
        ],
        compiler_params=pltpu.CompilerParams(vmem_limit_bytes=VMEM_LIMIT),
        name="last_part",
    )(cells, sides, after_first)


def force_kernel(capacity, levels, lines, got_hbm, state_hbm, out_hbm, got_ref, rows, ids, ids_smem, state, total, *rest):
    sums, (got_sem, ids_sem, load_sem, store_sem) = rest[:STREAMS], rest[STREAMS:]
    devices = got_ref.shape[0]
    cells_all = lines * LANES
    load_got = pltpu.make_async_copy(got_hbm, got_ref, got_sem)
    load_got.start()
    load = pltpu.make_async_copy(state_hbm, state, load_sem)
    load.start()
    low = lane_iota((HALF, LANES)) < capacity
    group = 8
    zero = jnp.zeros((64, LANES), jnp.float32)

    @pl.loop(0, cells_all // 64)
    def _(i):
        for s in range(STREAMS):
            sums[s][pl.ds(pl.multiple_of(i * 64, 64), 64), :] = zero

    load_got.wait()

    def to_smem(pair):
        return pltpu.make_async_copy(
            ids.at[pair], ids_smem.at[pl.ds(pair * LANES, LANES)], ids_sem.at[pair]
        )

    @pl.loop(0, devices // (2 * group))
    def _(part):
        for i in range(group):
            pair = part * group + i
            one, two = got_ref[2 * pair, :HALF], got_ref[2 * pair + 1, :HALF]
            first = jnp.where(low, one, pltpu.roll(two, capacity, 1))
            second = jnp.where(low, pltpu.roll(one, capacity, 1), two)
            cell = second[levels - HALF : levels - HALF + 1, :].astype(jnp.int32)
            ids[pl.ds(pair, 1), :] = jnp.where(cell < 0, cells_all, cell)
            wide = jnp.concatenate([first, second, jnp.zeros((LANES - 2 * HALF, LANES), jnp.float32)], axis=0)
            rows[pl.ds(pl.multiple_of(pair * LANES, LANES), LANES), :] = wide.T

    @pl.loop(0, devices // 2)
    def _(pair):
        to_smem(pair).start()

    @pl.loop(0, devices // 2)
    def _(pair):
        to_smem(pair).wait()

    @pl.loop(0, devices * capacity // (8 * STREAMS))
    def _(part):
        for i in range(8):
            at = [part * 8 * STREAMS + i * STREAMS + s for s in range(STREAMS)]
            cell = [ids_smem[at[s]] for s in range(STREAMS)]
            new = [sums[s][pl.ds(cell[s], 1), :] + rows[pl.ds(at[s], 1), :] for s in range(STREAMS)]
            for s in range(STREAMS):
                sums[s][pl.ds(cell[s], 1), :] = new[s]

    load.wait()

    def level_rows(line):
        return pl.ds(pl.multiple_of(line * levels, 8), levels)

    def stored(line):
        return pltpu.make_async_copy(total.at[level_rows(line)], out_hbm.at[:, line, :], store_sem.at[line])

    @pl.loop(0, lines // group)
    def _(part):
        turned = []
        for i in range(group):
            span = pl.ds(pl.multiple_of((part * group + i) * LANES, LANES), LANES)
            total_here = sums[0][span, :]
            for s in range(1, STREAMS):
                total_here = total_here + sums[s][span, :]
            turned.append(total_here.T[:levels])
        for i in range(group):
            at = level_rows(part * group + i)
            total[at, :] = state[at, :] + turned[i]
        for i in range(group):
            stored(part * group + i).start()

    @pl.loop(0, lines)
    def _(line):
        stored(line).wait()


def add_forcing(got, after_first, capacity):
    tracers, band, levels, tile = after_first.shape
    devices = got.shape[0]
    lines = tracers * band
    out = pl.pallas_call(
        functools.partial(force_kernel, capacity, levels, lines),
        out_shape=jax.ShapeDtypeStruct((levels, lines, tile), jnp.float32),
        in_specs=[ANY, ANY],
        out_specs=ANY,
        scratch_shapes=[
            pltpu.VMEM(got.shape, jnp.float32),
            pltpu.VMEM((devices * capacity, LANES), jnp.float32),
            pltpu.VMEM((devices // 2, LANES), jnp.int32),
            pltpu.SMEM((devices * capacity,), jnp.int32),
            pltpu.VMEM((levels * lines, tile), jnp.float32),
            pltpu.VMEM((levels * lines, tile), jnp.float32),
        ]
        + [pltpu.VMEM((lines * tile + 8, LANES), jnp.float32)] * STREAMS
        + [
            pltpu.SemaphoreType.DMA,
            pltpu.SemaphoreType.DMA((devices // 2,)),
            pltpu.SemaphoreType.DMA,
            pltpu.SemaphoreType.DMA((lines,)),
        ],
        compiler_params=pltpu.CompilerParams(vmem_limit_bytes=VMEM_LIMIT),
        name="add_forcing",
    )(got, after_first.reshape(levels * lines, tile))
    return out.reshape(levels, tracers, band, tile)


def on_device(adjoint_in, courant, mixing, kernel_blocks, sounding_dest, sounding_cell):
    lon_count = lax.axis_size("lon")
    lat_count = lax.axis_size("lat")
    devices = lon_count * lat_count
    held = kernel_blocks.shape[1]
    capacity = 4 * held // devices
    owner = sounding_dest.reshape(held // LANES, LANES)
    cell = sounding_cell.reshape(held // LANES, LANES)
    blocks = pack(kernel_blocks, owner, cell, devices, capacity)
    after_first, got = first_step(adjoint_in, courant, mixing, blocks, lon_count, lat_count)
    forced = add_forcing(got, after_first, capacity)
    swept, sides = second_front(forced, courant, mixing, lon_count, lat_count)
    return last_part(swept, sides, after_first)


def solution(mesh):
    placed = (
        P(None, None, "lat", "lon"),
        P(None, None, "lat", "lon"),
        P(None, "lat", "lon"),
        P(None, ("lon", "lat")),
        P(("lon", "lat"), None),
        P(("lon", "lat")),
    )
    return jax.shard_map(
        on_device,
        mesh=mesh,
        in_specs=placed,
        out_specs=(P(None, None, "lat", "lon"), P(None, "lat", "lon")),
        check_vma=False,
    )
```

```python
import functools
import jax
import jax.numpy as jnp
from jax import lax
from jax.experimental import pallas as pl
from jax.experimental.pallas import tpu as pltpu
from jax.sharding import PartitionSpec as P

MESH = pl.DeviceIdType.MESH
ANY = pl.BlockSpec(memory_space=pl.ANY)
LANES = 128
HALF = 37
ROOM = 40
STREAMS = 4
CHUNKS = 4
VMEM_LIMIT = 60 * 1024 * 1024


def lane_iota(shape):
    return lax.broadcasted_iota(jnp.int32, shape, len(shape) - 1)


def slot_table(owner_ref, capacity, held):
    row_id = lax.broadcasted_iota(jnp.int32, (LANES, LANES), 0)
    col_id = lax.broadcasted_iota(jnp.int32, (LANES, LANES), 1)
    pair_id = lax.broadcasted_iota(jnp.int32, (LANES // 2, LANES), 0)
    place = lane_iota((LANES // 2, LANES)).astype(jnp.float32)
    before = jnp.where(row_id < col_id, 1.0, 0.0).astype(jnp.bfloat16)
    ones = jnp.ones((LANES, LANES), jnp.bfloat16)
    base = jnp.zeros((LANES, LANES), jnp.float32)
    table = jnp.zeros((LANES // 2, LANES), jnp.float32)
    for chunk in range(held // LANES):
        owner = owner_ref[chunk : chunk + 1, :]
        hot_f = jnp.where(jnp.broadcast_to(owner, (LANES, LANES)) == row_id, 1.0, 0.0)
        hot_b = hot_f.astype(jnp.bfloat16)
        earlier = jnp.dot(hot_b, before, preferred_element_type=jnp.float32)
        rank = jnp.sum(hot_f * (earlier + base), axis=0, keepdims=True).astype(jnp.int32)
        base = base + jnp.dot(hot_b, ones, preferred_element_type=jnp.float32)
        pair = lax.shift_right_logical(owner, 1)
        slot = (owner - 2 * pair) * capacity + rank
        in_pair = jnp.where(jnp.broadcast_to(pair, pair_id.shape) == pair_id, 1.0, 0.0)
        in_slot = jnp.where(jnp.broadcast_to(slot, row_id.shape) == row_id, 1.0, 0.0)
        found = lax.dot_general(
            jnp.concatenate([in_pair * place, in_pair], axis=0).astype(jnp.bfloat16),
            in_slot.astype(jnp.bfloat16),
            (((1,), (1,)), ((), ())),
            preferred_element_type=jnp.float32,
        )
        table = table + found[: LANES // 2] + found[LANES // 2 :] * (LANES * chunk + 1.0)
    return table.astype(jnp.int32)


def transport_front(lon_count, lat_count, hooks, a_hbm, c_hbm, m_hbm, front):
    (
        a_ref, c_ref, m_ref, vbuf, rbuf, send_n, send_s, send_e, send_w,
        from_s, from_n, from_w, from_e, rows_fix, merged, load_sem, send_sem, recv_sem,
    ) = front
    at_entry, before_rows, after_rows, after_columns, during_columns = hooks
    levels, tracers, band, tile = a_ref.shape
    lon, lat = lax.axis_index("lon"), lax.axis_index("lat")
    north = {"lon": lon, "lat": lax.rem(lat + 1, lat_count)}
    south = {"lon": lon, "lat": lax.rem(lat + lat_count - 1, lat_count)}
    east = {"lon": lax.rem(lon + 1, lon_count), "lat": lat}
    west = {"lon": lax.rem(lon + lon_count - 1, lon_count), "lat": lat}

    cuts = [levels * i // CHUNKS for i in range(CHUNKS)] + [levels]
    loads = []
    for i in range(CHUNKS):
        span, faces = slice(cuts[i], cuts[i + 1]), slice(cuts[i], min(cuts[i + 1], levels - 1))
        loads.append(pltpu.make_async_copy(m_hbm.at[faces], m_ref.at[faces], load_sem.at[2 * i]))
        loads.append(pltpu.make_async_copy(a_hbm.at[span], a_ref.at[span], load_sem.at[2 * i + 1]))
    loads.append(pltpu.make_async_copy(c_hbm, c_ref, load_sem.at[2 * CHUNKS]))
    for load in loads:
        load.start()
    at_entry()
    loads[0].wait()
    loads[1].wait()

    mix = m_ref[0]
    inverse = 1.0 / (1.0 + mix)
    ratio = mix * inverse
    solved = a_ref[0] * inverse[None]
    rbuf[0] = ratio
    vbuf[0] = solved

    def down(k, carry):
        mix_above, ratio, solved = carry
        mix = m_ref[k]
        inverse = 1.0 / (1.0 + mix_above + mix - mix_above * ratio)
        ratio = mix * inverse
        solved = (a_ref[k] + mix_above[None] * solved) * inverse[None]
        rbuf[k] = ratio
        vbuf[k] = solved
        return mix, ratio, solved

    carry = (mix, ratio, solved)
    for i in range(CHUNKS):
        if i > 0:
            loads[2 * i].wait()
            loads[2 * i + 1].wait()
        carry = lax.fori_loop(max(cuts[i], 1), min(cuts[i + 1], levels - 1), down, carry)
    mix, ratio, solved = carry
    inverse = 1.0 / (1.0 + mix - mix * ratio)
    solved = (a_ref[levels - 1] + mix[None] * solved) * inverse[None]

    def keep(k, solved):
        vbuf[k] = solved
        for t in range(tracers):
            send_s[pl.ds(t * levels + k, 1), :] = solved[t, 0:1, :]
            send_n[pl.ds(t * levels + k, 1), :] = solved[t, band - 1 : band, :]

    keep(levels - 1, solved)

    def up(i, solved):
        k = levels - 2 - i
        solved = vbuf[k] + rbuf[k][None] * solved
        keep(k, solved)
        return solved

    lax.fori_loop(0, levels - 1, up, solved)

    loads[2 * CHUNKS].wait()
    edge = jnp.where(lat == lat_count - 1, 0.0, 1.0)

    @pl.loop(0, levels // 8)
    def _(j):
        for i in range(8):
            k = j * 8 + i
            send_n[pl.ds(tracers * levels + k, 1), :] = c_ref[1, k, band - 1 : band, :] * edge

    def remote(index, src, dst, to):
        return pltpu.make_async_remote_copy(
            src_ref=src, dst_ref=dst, send_sem=send_sem.at[index], recv_sem=recv_sem.at[index],
            device_id=to, device_id_type=MESH,
        )

    to_north = remote(0, send_n, from_s, north)
    to_south = remote(1, send_s, from_n, south)
    before_rows()
    to_north.start()
    to_south.start()
    after_rows()

    top = lax.broadcasted_iota(jnp.int32, (band, tile), 0) == band - 1

    @pl.loop(0, levels // 2)
    def _(j):
        swept = []
        for i in range(2):
            face = c_ref[1, 2 * j + i]
            out_face, in_face = jnp.maximum(face, 0.0), jnp.minimum(face, 0.0)
            for t in range(tracers):
                cells = vbuf[2 * j + i, t]
                rise = jnp.where(top, 0.0, pltpu.roll(cells, band - 1, 0) - cells)
                swept.append(cells + out_face * rise + pltpu.roll(in_face * rise, 1, 0))
        for i in range(2):
            for t in range(tracers):
                vbuf[2 * j + i, t] = swept[tracers * i + t]

    lane = lane_iota((8, tile))
    zero = jnp.zeros((8, tile), jnp.float32)

    @pl.loop(0, band // 8)
    def _(g):
        span = pl.ds(pl.multiple_of(g * 8, 8), 8)
        last = zero
        for k in range(levels):
            last = jnp.where(lane == (k - 1) % tile, pltpu.roll(c_ref[0, k, span, :], k, 1), last)
        send_e[tracers, span, :] = last

    to_north.wait()
    to_south.wait()
    face_south = jnp.minimum(from_s[tracers * levels :, :], 0.0)
    face_north = jnp.maximum(send_n[tracers * levels :, :], 0.0)
    for t in range(tracers):
        part = slice(t * levels, (t + 1) * levels)
        rows_fix[part, :] = face_south * (send_s[part, :] - from_s[part, :])
        rows_fix[tracers * levels + t * levels : tracers * levels + (t + 1) * levels, :] = face_north * (
            from_n[part, :] - send_n[part, :]
        )

    row = lax.broadcasted_iota(jnp.int32, (8, tile), 0)

    def columns(g, fixed, at):
        span = pl.ds(pl.multiple_of(g * 8, 8), 8)
        for t in range(tracers):
            first, last = zero, zero
            for k in range(levels):
                cells = vbuf[k, t, span, :]
                if fixed is not None:
                    fix = rows_fix[fixed + t * levels + k : fixed + t * levels + k + 1, :]
                    cells = cells + jnp.where(row == at, jnp.broadcast_to(fix, (8, tile)), 0.0)
                    vbuf[k, t, span, :] = cells
                turned = pltpu.roll(cells, k, 1)
                first = jnp.where(lane == k, turned, first)
                last = jnp.where(lane == (k - 1) % tile, turned, last)
            send_w[t, span, :] = first
            send_e[t, span, :] = last

    columns(0, 0, 0)
    columns(band // 8 - 1, tracers * levels, 7)

    @pl.loop(1, band // 8 - 1)
    def _(g):
        columns(g, None, None)

    to_east = remote(2, send_e, from_w, east)
    to_west = remote(3, send_w, from_e, west)
    to_east.start()
    to_west.start()
    after_columns()
    during_columns()
    to_east.wait()
    to_west.wait()

    even = lax.rem(lane_iota((band, tile)), 2) == 0
    face_last = jnp.maximum(pltpu.roll(send_e[tracers], 1, 1), 0.0)
    face_first = jnp.minimum(pltpu.roll(from_w[tracers], 2, 1), 0.0)
    for t in range(tracers):
        at_last = face_last * (from_e[t] - pltpu.roll(send_e[t], 1, 1))
        at_first = face_first * (pltpu.roll(send_w[t], 1, 1) - pltpu.roll(from_w[t], 2, 1))
        merged[t, 0] = jnp.where(even, at_last, at_first)
        merged[t, 1] = jnp.where(even, at_first, at_last)


def front_scratch(levels, tracers, band, tile, merged=True):
    f32 = jnp.float32
    return [
        pltpu.VMEM((levels, tracers, band, tile), f32),
        pltpu.VMEM((2, levels, band, tile), f32),
        pltpu.VMEM((levels - 1, band, tile), f32),
        pltpu.VMEM((levels, tracers, band, tile), f32),
        pltpu.VMEM((levels - 1, band, tile), f32),
        pltpu.VMEM((levels * (tracers + 1), tile), f32),
        pltpu.VMEM((levels * tracers, tile), f32),
        pltpu.VMEM((tracers + 1, band, tile), f32),
        pltpu.VMEM((tracers, band, tile), f32),
        pltpu.VMEM((levels * (tracers + 1), tile), f32),
        pltpu.VMEM((levels * tracers, tile), f32),
        pltpu.VMEM((tracers + 1, band, tile), f32),
        pltpu.VMEM((tracers, band, tile), f32),
        pltpu.VMEM((2 * tracers * levels, tile), f32),
        pltpu.VMEM((tracers, 2, band, tile), f32),
        pltpu.SemaphoreType.DMA((2 * CHUNKS + 1,)),
        pltpu.SemaphoreType.DMA((4,)),
        pltpu.SemaphoreType.DMA((4,)),
    ]


FRONT = 18


def sweep_all(c_ref, vbuf, obuf, done):
    levels, tracers, band, tile = vbuf.shape
    lane = lane_iota((8, tile))

    @pl.loop(0, band // 8)
    def _(g):
        span = pl.ds(pl.multiple_of(g * 8, 8), 8)
        for k in range(levels):
            face = c_ref[0, k, span, :]
            out_face, in_face = jnp.maximum(face, 0.0), jnp.minimum(face, 0.0)
            for t in range(tracers):
                cells = vbuf[k, t, span, :]
                rise = jnp.where(lane == tile - 1, 0.0, pltpu.roll(cells, tile - 1, 1) - cells)
                obuf[k, t, span, :] = cells + out_face * rise + pltpu.roll(in_face * rise, 1, 1)
        done(g)


def add_sides(cells, merged, span, out):
    levels, tracers, band, tile = cells.shape
    lane = lane_iota((8, tile))
    ends = (lane == 0) | (lane == tile - 1)
    for t in range(tracers):
        sides = [merged[t, 0, span, :], merged[t, 1, span, :]]
        for k in range(levels):
            turned = pltpu.roll(sides[k % 2], tile - 1 - k, 1)
            out[k, t, span, :] = cells[k, t, span, :] + jnp.where(ends, turned, 0.0)


def chip_at(step):
    shift = lax.rem(step * 27, 64)
    lon, lat = lax.axis_index("lon"), lax.axis_index("lat")
    x = lax.rem(lon // 8 + shift // 16, 4)
    y = lax.rem(lax.rem(lon // 2, 4) + lax.rem(shift // 4, 4), 4)
    z = lax.rem((lat // 2) * 2 + lax.rem(lon, 2) + lax.rem(shift, 4), 4)
    return x * 8 + y * 2 + lax.rem(z, 2), (z // 2) * 2


def first_kernel(
    lon_count, lat_count, capacity, a_hbm, c_hbm, m_hbm, kernels_hbm, owner_ref, cell_ref, out_hbm, got_hbm, *scratch
):
    front, rest = scratch[:FRONT], scratch[FRONT:]
    (
        obuf, kernels, rows, table, table_smem, stage, blocks,
        store_sem, trade_send, trade_recv, own_sem, kernels_sem, table_sem,
    ) = rest
    c_ref, vbuf, merged = front[1], front[3], front[14]
    levels, tracers, band, tile = vbuf.shape
    held = kernels.shape[1]
    devices = lon_count * lat_count
    my_lon, my_lat = lax.axis_index("lon"), lax.axis_index("lat")
    me = my_lon * lat_count + my_lat
    used = pl.ds(0, HALF)
    low = lane_iota((HALF, LANES)) < capacity

    def send(lon, lat):
        pltpu.make_async_remote_copy(
            src_ref=blocks.at[lon * lat_count + lat, used], dst_ref=got_hbm.at[me, used],
            send_sem=trade_send, recv_sem=trade_recv,
            device_id={"lon": lon, "lat": lat}, device_id_type=MESH,
        ).start()

    def fill(places):
        wides = []
        for i, (lon, lat) in enumerate(places):
            first = ((lon * lat_count + lat) // 2) * LANES

            @pl.loop(0, LANES // 16)
            def _(part):
                for j in range(16):
                    at = part * 16 + j
                    source = jnp.minimum(jnp.maximum(table_smem[first + at], 0), held + 7)
                    stage[i, pl.ds(at, 1), :] = rows[pl.ds(source, 1), :]

        for i in range(len(places)):
            wides.append(stage[i].T)
        for (lon, lat), wide in zip(places, wides):
            first, second = wide[:HALF], wide[HALF : 2 * HALF]
            at = lon * lat_count + lat
            blocks[at, :HALF] = jnp.where(low, first, pltpu.roll(second, capacity, 1))
            blocks[at + 1, :HALF] = jnp.where(low, pltpu.roll(first, capacity, 1), second)

    def trade(begin, end):
        @pl.loop(begin, end)
        def _(part):
            places = [chip_at(part * 4 + i) for i in range(4)]
            fill(places)
            for lon, lat in places:
                send(lon, lat)
                send(lon, lat + 1)

    own = pltpu.make_async_copy(blocks.at[me, used], got_hbm.at[me, used], own_sem)

    def trade_first():
        @pl.loop(0, devices // 2)
        def _(pair):
            to_smem(pair).wait()

        places = [chip_at(i) for i in range(4)]
        fill(places)
        send(my_lon, my_lat + 1 - 2 * lax.rem(my_lat, 2))
        own.start()
        for lon, lat in places[1:]:
            send(lon, lat)
            send(lon, lat + 1)
        trade(1, 4)

    def to_smem(pair):
        return pltpu.make_async_copy(
            table.at[pair], table_smem.at[pl.ds(pair * LANES, LANES)], table_sem.at[pair]
        )

    def at_entry():
        load = pltpu.make_async_copy(kernels_hbm, kernels, kernels_sem)
        load.start()
        barrier = pltpu.get_barrier_semaphore()

        @pl.loop(1, devices)
        def _(i):
            peer = lax.rem(me + i, devices)
            pl.semaphore_signal(
                barrier, inc=1, device_id={"lon": peer // lat_count, "lat": lax.rem(peer, lat_count)},
                device_id_type=MESH,
            )

        table[...] = slot_table(owner_ref, capacity, held) + 7

        @pl.loop(0, devices // 2)
        def _(pair):
            to_smem(pair).start()

        load.wait()
        rows[0:8, :] = jnp.where(lane_iota((8, LANES)) == levels, -1.0, 0.0)
        for chunk in range(held // LANES):
            tall = jnp.concatenate(
                [
                    kernels[:, chunk * LANES : (chunk + 1) * LANES],
                    jnp.broadcast_to(cell_ref[chunk : chunk + 1, :].astype(jnp.float32), (8, LANES)),
                    jnp.zeros((LANES - levels - 8, LANES), jnp.float32),
                ],
                axis=0,
            )
            rows[8 + chunk * LANES : 8 + (chunk + 1) * LANES, :] = tall.T

    def before_rows():
        pl.semaphore_wait(pltpu.get_barrier_semaphore(), devices - 1)

    def main_sweep():
        sweep_all(c_ref, vbuf, obuf, lambda g: None)

    hooks = (at_entry, before_rows, trade_first, lambda: trade(4, devices // 8), main_sweep)
    transport_front(lon_count, lat_count, hooks, a_hbm, c_hbm, m_hbm, front)

    def stored(t, r):
        return pltpu.make_async_copy(obuf.at[:, t, r, :], out_hbm.at[t, r], store_sem.at[t * band + r])

    @pl.loop(0, band // 8)
    def _(g):
        add_sides(obuf, merged, pl.ds(pl.multiple_of(g * 8, 8), 8), obuf)
        for t in range(tracers):
            for r in range(8):
                stored(t, g * 8 + r).start()

    own.wait()
    most = pl.ds(0, devices - 1)
    pltpu.make_async_remote_copy(
        src_ref=blocks.at[most, used], dst_ref=got_hbm.at[most, used],
        send_sem=trade_send, recv_sem=trade_recv,
        device_id={"lon": my_lon, "lat": lax.rem(my_lat + 1, lat_count)},
        device_id_type=MESH,
    ).wait()

    @pl.loop(0, band)
    def _(r):
        for t in range(tracers):
            stored(t, r).wait()


def second_kernel(lon_count, lat_count, a_hbm, c_hbm, m_hbm, out_hbm, sides_ref, *scratch):
    front, (obuf, store_sem) = scratch[:FRONT], scratch[FRONT:]
    c_ref, vbuf, merged = front[1], front[3], front[14]
    band = vbuf.shape[2]

    def at_entry():
        lon, lat = lax.axis_index("lon"), lax.axis_index("lat")
        barrier = pltpu.get_barrier_semaphore()
        for d_lon, d_lat in ((1, 0), (lon_count - 1, 0), (0, 1), (0, lat_count - 1)):
            pl.semaphore_signal(
                barrier, inc=1,
                device_id={"lon": lax.rem(lon + d_lon, lon_count), "lat": lax.rem(lat + d_lat, lat_count)},
                device_id_type=MESH,
            )

    def before_rows():
        pl.semaphore_wait(pltpu.get_barrier_semaphore(), 4)

    def stored(g):
        span = pl.ds(pl.multiple_of(g * 8, 8), 8)
        return pltpu.make_async_copy(obuf.at[:, :, span, :], out_hbm.at[:, :, span, :], store_sem.at[g])

    def main_sweep():
        sweep_all(c_ref, vbuf, obuf, lambda g: stored(g).start())

    hooks = (at_entry, before_rows, lambda: None, lambda: None, main_sweep)
    transport_front(lon_count, lat_count, hooks, a_hbm, c_hbm, m_hbm, front)
    sides_ref[...] = merged[...]

    @pl.loop(0, band // 8)
    def _(g):
        stored(g).wait()


def first_step(state, courant, mixing, kernel_blocks, owner, cell, lon_count, lat_count, capacity):
    levels, tracers, band, tile = state.shape
    devices = lon_count * lat_count
    held = kernel_blocks.shape[1]
    f32 = jnp.float32
    small = pl.BlockSpec(memory_space=pltpu.VMEM)
    return pl.pallas_call(
        functools.partial(first_kernel, lon_count, lat_count, capacity),
        out_shape=(
            jax.ShapeDtypeStruct((tracers, band, levels, tile), f32),
            jax.ShapeDtypeStruct((devices, ROOM, LANES), f32),
        ),
        in_specs=[ANY] * 4 + [small] * 2,
        out_specs=(ANY, ANY),
        scratch_shapes=front_scratch(levels, tracers, band, tile)
        + [
            pltpu.VMEM((levels, tracers, band, tile), f32),
            pltpu.VMEM((levels, held), f32),
            pltpu.VMEM((held + 8, LANES), f32),
            pltpu.VMEM((devices // 2, LANES), jnp.int32),
            pltpu.SMEM((devices * capacity,), jnp.int32),
            pltpu.VMEM((4, LANES, LANES), f32),
            pltpu.VMEM((devices, ROOM, LANES), f32),
            pltpu.SemaphoreType.DMA((tracers * band,)),
            pltpu.SemaphoreType.DMA,
            pltpu.SemaphoreType.DMA,
            pltpu.SemaphoreType.DMA,
            pltpu.SemaphoreType.DMA,
            pltpu.SemaphoreType.DMA((devices // 2,)),
        ],
        compiler_params=pltpu.CompilerParams(
            collective_id=0, has_side_effects=True, vmem_limit_bytes=VMEM_LIMIT
        ),
        name="first_step",
    )(state, courant, mixing, kernel_blocks, owner, cell)


def second_front(state, courant, mixing, lon_count, lat_count):
    levels, tracers, band, tile = state.shape
    return pl.pallas_call(
        functools.partial(second_kernel, lon_count, lat_count),
        out_shape=(
            jax.ShapeDtypeStruct(state.shape, jnp.float32),
            jax.ShapeDtypeStruct((tracers, 2, band, tile), jnp.float32),
        ),
        in_specs=[ANY] * 3,
        out_specs=(ANY, pl.BlockSpec(memory_space=pltpu.VMEM)),
        scratch_shapes=front_scratch(levels, tracers, band, tile)
        + [pltpu.VMEM((levels, tracers, band, tile), jnp.float32), pltpu.SemaphoreType.DMA((band // 8,))],
        compiler_params=pltpu.CompilerParams(
            collective_id=1, has_side_effects=True, vmem_limit_bytes=VMEM_LIMIT
        ),
        name="second_front",
    )(state, courant, mixing)


def last_kernel(
    cells_hbm, sides_ref, first_hbm, out_hbm, flux_ref, cells, obuf, ground, cell_sem, store_sem, ground_sem
):
    band = cells.shape[2]

    def rows_of(g):
        return pl.ds(pl.multiple_of(g * 8, 8), 8)

    def load(g):
        return pltpu.make_async_copy(
            cells_hbm.at[:, :, rows_of(g), :], cells.at[:, :, rows_of(g), :], cell_sem.at[g]
        )

    def stored(g):
        return pltpu.make_async_copy(
            obuf.at[:, :, rows_of(g), :], out_hbm.at[:, :, rows_of(g), :], store_sem.at[g]
        )

    @pl.loop(0, band // 8)
    def _(g):
        load(g).start()

    load_ground = pltpu.make_async_copy(first_hbm.at[:, :, 0, :], ground, ground_sem)
    load_ground.start()

    @pl.loop(0, band // 8)
    def _(g):
        load(g).wait()
        add_sides(cells, sides_ref, rows_of(g), obuf)
        stored(g).start()

    load_ground.wait()
    flux_ref[...] = ground[...] + obuf[0]

    @pl.loop(0, band // 8)
    def _(g):
        stored(g).wait()


def last_part(cells, sides, after_first):
    levels, tracers, band, tile = cells.shape
    return pl.pallas_call(
        last_kernel,
        out_shape=(
            jax.ShapeDtypeStruct(cells.shape, jnp.float32),
            jax.ShapeDtypeStruct(cells.shape[1:], jnp.float32),
        ),
        in_specs=[ANY, pl.BlockSpec(memory_space=pltpu.VMEM), ANY],
        out_specs=(ANY, pl.BlockSpec(memory_space=pltpu.VMEM)),
        scratch_shapes=[
            pltpu.VMEM((levels, tracers, band, tile), jnp.float32),
            pltpu.VMEM((levels, tracers, band, tile), jnp.float32),
            pltpu.VMEM((tracers, band, tile), jnp.float32),
            pltpu.SemaphoreType.DMA((band // 8,)),
            pltpu.SemaphoreType.DMA((band // 8,)),
            pltpu.SemaphoreType.DMA,
        ],
        compiler_params=pltpu.CompilerParams(vmem_limit_bytes=VMEM_LIMIT),
        name="last_part",
    )(cells, sides, after_first)


def force_kernel(capacity, levels, lines, got_hbm, state_hbm, out_hbm, got_ref, rows, ids, ids_smem, state, total, *rest):
    sums, (got_sem, ids_sem, load_sem, store_sem) = rest[:STREAMS], rest[STREAMS:]
    devices = got_ref.shape[0]
    cells_all = lines * LANES
    load_got = pltpu.make_async_copy(got_hbm, got_ref, got_sem)
    load_got.start()
    load = pltpu.make_async_copy(state_hbm, state, load_sem)
    load.start()
    low = lane_iota((HALF, LANES)) < capacity
    group = 8
    zero = jnp.zeros((64, LANES), jnp.float32)

    @pl.loop(0, cells_all // 64)
    def _(i):
        for s in range(STREAMS):
            sums[s][pl.ds(pl.multiple_of(i * 64, 64), 64), :] = zero

    load_got.wait()

    def to_smem(pair):
        return pltpu.make_async_copy(
            ids.at[pair], ids_smem.at[pl.ds(pair * LANES, LANES)], ids_sem.at[pair]
        )

    @pl.loop(0, devices // (2 * group))
    def _(part):
        for i in range(group):
            pair = part * group + i
            one, two = got_ref[2 * pair, :HALF], got_ref[2 * pair + 1, :HALF]
            first = jnp.where(low, one, pltpu.roll(two, capacity, 1))
            second = jnp.where(low, pltpu.roll(one, capacity, 1), two)
            cell = second[levels - HALF : levels - HALF + 1, :].astype(jnp.int32)
            ids[pl.ds(pair, 1), :] = jnp.where(cell < 0, cells_all, cell)
            wide = jnp.concatenate([first, second, jnp.zeros((LANES - 2 * HALF, LANES), jnp.float32)], axis=0)
            rows[pl.ds(pl.multiple_of(pair * LANES, LANES), LANES), :] = wide.T
        for i in range(group):
            to_smem(part * group + i).start()

    @pl.loop(0, devices // 2)
    def _(pair):
        to_smem(pair).wait()

    @pl.loop(0, devices * capacity // (8 * STREAMS))
    def _(part):
        for i in range(8):
            at = [part * 8 * STREAMS + i * STREAMS + s for s in range(STREAMS)]
            cell = [ids_smem[at[s]] for s in range(STREAMS)]
            new = [sums[s][pl.ds(cell[s], 1), :] + rows[pl.ds(at[s], 1), :] for s in range(STREAMS)]
            for s in range(STREAMS):
                sums[s][pl.ds(cell[s], 1), :] = new[s]

    load.wait()

    def level_rows(line):
        return pl.ds(pl.multiple_of(line * levels, 8), levels)

    def stored(line):
        return pltpu.make_async_copy(total.at[level_rows(line)], out_hbm.at[:, line, :], store_sem.at[line])

    @pl.loop(0, lines // group)
    def _(part):
        turned = []
        for i in range(group):
            span = pl.ds(pl.multiple_of((part * group + i) * LANES, LANES), LANES)
            total_here = sums[0][span, :]
            for s in range(1, STREAMS):
                total_here = total_here + sums[s][span, :]
            turned.append(total_here.T[:levels])
        for i in range(group):
            at = level_rows(part * group + i)
            total[at, :] = state[at, :] + turned[i]
        for i in range(group):
            stored(part * group + i).start()

    @pl.loop(0, lines)
    def _(line):
        stored(line).wait()


def add_forcing(got, after_first, capacity):
    tracers, band, levels, tile = after_first.shape
    devices = got.shape[0]
    lines = tracers * band
    out = pl.pallas_call(
        functools.partial(force_kernel, capacity, levels, lines),
        out_shape=jax.ShapeDtypeStruct((levels, lines, tile), jnp.float32),
        in_specs=[ANY, ANY],
        out_specs=ANY,
        scratch_shapes=[
            pltpu.VMEM(got.shape, jnp.float32),
            pltpu.VMEM((devices * capacity, LANES), jnp.float32),
            pltpu.VMEM((devices // 2, LANES), jnp.int32),
            pltpu.SMEM((devices * capacity,), jnp.int32),
            pltpu.VMEM((levels * lines, tile), jnp.float32),
            pltpu.VMEM((levels * lines, tile), jnp.float32),
        ]
        + [pltpu.VMEM((lines * tile + 8, LANES), jnp.float32)] * STREAMS
        + [
            pltpu.SemaphoreType.DMA,
            pltpu.SemaphoreType.DMA((devices // 2,)),
            pltpu.SemaphoreType.DMA,
            pltpu.SemaphoreType.DMA((lines,)),
        ],
        compiler_params=pltpu.CompilerParams(vmem_limit_bytes=VMEM_LIMIT),
        name="add_forcing",
    )(got, after_first.reshape(levels * lines, tile))
    return out.reshape(levels, tracers, band, tile)


def on_device(adjoint_in, courant, mixing, kernel_blocks, sounding_dest, sounding_cell):
    lon_count = lax.axis_size("lon")
    lat_count = lax.axis_size("lat")
    devices = lon_count * lat_count
    held = kernel_blocks.shape[1]
    capacity = 4 * held // devices
    owner = sounding_dest.reshape(held // LANES, LANES)
    cell = sounding_cell.reshape(held // LANES, LANES)
    after_first, got = first_step(
        adjoint_in, courant, mixing, kernel_blocks, owner, cell, lon_count, lat_count, capacity
    )
    forced = add_forcing(got, after_first, capacity)
    swept, sides = second_front(forced, courant, mixing, lon_count, lat_count)
    return last_part(swept, sides, after_first)


def solution(mesh):
    placed = (
        P(None, None, "lat", "lon"),
        P(None, None, "lat", "lon"),
        P(None, "lat", "lon"),
        P(None, ("lon", "lat")),
        P(("lon", "lat"), None),
        P(("lon", "lat")),
    )
    return jax.shard_map(
        on_device,
        mesh=mesh,
        in_specs=placed,
        out_specs=(P(None, None, "lat", "lon"), P(None, "lat", "lon")),
        check_vma=False,
    )
```

```python
import functools
import jax
import jax.numpy as jnp
from jax import lax
from jax.experimental import pallas as pl
from jax.experimental.pallas import tpu as pltpu
from jax.sharding import PartitionSpec as P

MESH = pl.DeviceIdType.MESH
ANY = pl.BlockSpec(memory_space=pl.ANY)
LANES = 128
HALF = 37
ROOM = 40
STREAMS = 4
CHUNKS = 4
VMEM_LIMIT = 60 * 1024 * 1024


def lane_iota(shape):
    return lax.broadcasted_iota(jnp.int32, shape, len(shape) - 1)


def slot_table(owner_ref, capacity, held):
    row_id = lax.broadcasted_iota(jnp.int32, (LANES, LANES), 0)
    col_id = lax.broadcasted_iota(jnp.int32, (LANES, LANES), 1)
    pair_id = lax.broadcasted_iota(jnp.int32, (LANES // 2, LANES), 0)
    place = lane_iota((LANES // 2, LANES)).astype(jnp.float32)
    before = jnp.where(row_id < col_id, 1.0, 0.0).astype(jnp.bfloat16)
    ones = jnp.ones((LANES, LANES), jnp.bfloat16)
    base = jnp.zeros((LANES, LANES), jnp.float32)
    table = jnp.zeros((LANES // 2, LANES), jnp.float32)
    for chunk in range(held // LANES):
        owner = owner_ref[chunk : chunk + 1, :]
        hot_f = jnp.where(jnp.broadcast_to(owner, (LANES, LANES)) == row_id, 1.0, 0.0)
        hot_b = hot_f.astype(jnp.bfloat16)
        earlier = jnp.dot(hot_b, before, preferred_element_type=jnp.float32)
        rank = jnp.sum(hot_f * (earlier + base), axis=0, keepdims=True).astype(jnp.int32)
        base = base + jnp.dot(hot_b, ones, preferred_element_type=jnp.float32)
        pair = lax.shift_right_logical(owner, 1)
        slot = (owner - 2 * pair) * capacity + rank
        in_pair = jnp.where(jnp.broadcast_to(pair, pair_id.shape) == pair_id, 1.0, 0.0)
        in_slot = jnp.where(jnp.broadcast_to(slot, row_id.shape) == row_id, 1.0, 0.0)
        found = lax.dot_general(
            jnp.concatenate([in_pair * place, in_pair], axis=0).astype(jnp.bfloat16),
            in_slot.astype(jnp.bfloat16),
            (((1,), (1,)), ((), ())),
            preferred_element_type=jnp.float32,
        )
        table = table + found[: LANES // 2] + found[LANES // 2 :] * (LANES * chunk + 1.0)
    return table.astype(jnp.int32)


def transport_front(lon_count, lat_count, hooks, a_hbm, c_hbm, m_hbm, front):
    (
        a_ref, c_ref, m_ref, vbuf, rbuf, send_n, send_s, send_e, send_w,
        from_s, from_n, from_w, from_e, rows_fix, merged, load_sem, send_sem, recv_sem,
    ) = front
    at_entry, before_rows, after_rows, after_columns, during_columns = hooks
    levels, tracers, band, tile = a_ref.shape
    lon, lat = lax.axis_index("lon"), lax.axis_index("lat")
    north = {"lon": lon, "lat": lax.rem(lat + 1, lat_count)}
    south = {"lon": lon, "lat": lax.rem(lat + lat_count - 1, lat_count)}
    east = {"lon": lax.rem(lon + 1, lon_count), "lat": lat}
    west = {"lon": lax.rem(lon + lon_count - 1, lon_count), "lat": lat}

    cuts = [levels * i // CHUNKS for i in range(CHUNKS)] + [levels]
    loads = []
    for i in range(CHUNKS):
        span, faces = slice(cuts[i], cuts[i + 1]), slice(cuts[i], min(cuts[i + 1], levels - 1))
        loads.append(pltpu.make_async_copy(m_hbm.at[faces], m_ref.at[faces], load_sem.at[2 * i]))
        loads.append(pltpu.make_async_copy(a_hbm.at[span], a_ref.at[span], load_sem.at[2 * i + 1]))
    loads.append(pltpu.make_async_copy(c_hbm, c_ref, load_sem.at[2 * CHUNKS]))
    for load in loads:
        load.start()
    at_entry()
    loads[0].wait()
    loads[1].wait()

    mix = m_ref[0]
    inverse = 1.0 / (1.0 + mix)
    ratio = mix * inverse
    solved = a_ref[0] * inverse[None]
    rbuf[0] = ratio
    vbuf[0] = solved

    def down(k, carry):
        mix_above, ratio, solved = carry
        mix = m_ref[k]
        inverse = 1.0 / (1.0 + mix_above + mix - mix_above * ratio)
        ratio = mix * inverse
        solved = (a_ref[k] + mix_above[None] * solved) * inverse[None]
        rbuf[k] = ratio
        vbuf[k] = solved
        return mix, ratio, solved

    carry = (mix, ratio, solved)
    for i in range(CHUNKS):
        if i > 0:
            loads[2 * i].wait()
            loads[2 * i + 1].wait()
        carry = lax.fori_loop(max(cuts[i], 1), min(cuts[i + 1], levels - 1), down, carry)
    mix, ratio, solved = carry
    inverse = 1.0 / (1.0 + mix - mix * ratio)
    solved = (a_ref[levels - 1] + mix[None] * solved) * inverse[None]

    def keep(k, solved):
        vbuf[k] = solved
        for t in range(tracers):
            send_s[pl.ds(t * levels + k, 1), :] = solved[t, 0:1, :]
            send_n[pl.ds(t * levels + k, 1), :] = solved[t, band - 1 : band, :]

    keep(levels - 1, solved)

    def up(i, solved):
        k = levels - 2 - i
        solved = vbuf[k] + rbuf[k][None] * solved
        keep(k, solved)
        return solved

    lax.fori_loop(0, levels - 1, up, solved)

    loads[2 * CHUNKS].wait()
    edge = jnp.where(lat == lat_count - 1, 0.0, 1.0)

    @pl.loop(0, levels // 8)
    def _(j):
        for i in range(8):
            k = j * 8 + i
            send_n[pl.ds(tracers * levels + k, 1), :] = c_ref[1, k, band - 1 : band, :] * edge

    def remote(index, src, dst, to):
        return pltpu.make_async_remote_copy(
            src_ref=src, dst_ref=dst, send_sem=send_sem.at[index], recv_sem=recv_sem.at[index],
            device_id=to, device_id_type=MESH,
        )

    to_north = remote(0, send_n, from_s, north)
    to_south = remote(1, send_s, from_n, south)
    before_rows()
    to_north.start()
    to_south.start()
    after_rows()

    top = lax.broadcasted_iota(jnp.int32, (band, tile), 0) == band - 1

    @pl.loop(0, levels // 2)
    def _(j):
        swept = []
        for i in range(2):
            face = c_ref[1, 2 * j + i]
            out_face, in_face = jnp.maximum(face, 0.0), jnp.minimum(face, 0.0)
            for t in range(tracers):
                cells = vbuf[2 * j + i, t]
                rise = jnp.where(top, 0.0, pltpu.roll(cells, band - 1, 0) - cells)
                swept.append(cells + out_face * rise + pltpu.roll(in_face * rise, 1, 0))
        for i in range(2):
            for t in range(tracers):
                vbuf[2 * j + i, t] = swept[tracers * i + t]

    lane = lane_iota((8, tile))
    zero = jnp.zeros((8, tile), jnp.float32)

    @pl.loop(0, band // 8)
    def _(g):
        span = pl.ds(pl.multiple_of(g * 8, 8), 8)
        last = zero
        for k in range(levels):
            last = jnp.where(lane == (k - 1) % tile, pltpu.roll(c_ref[0, k, span, :], k, 1), last)
        send_e[tracers, span, :] = last

    to_north.wait()
    to_south.wait()
    face_south = jnp.minimum(from_s[tracers * levels :, :], 0.0)
    face_north = jnp.maximum(send_n[tracers * levels :, :], 0.0)
    for t in range(tracers):
        part = slice(t * levels, (t + 1) * levels)
        rows_fix[part, :] = face_south * (send_s[part, :] - from_s[part, :])
        rows_fix[tracers * levels + t * levels : tracers * levels + (t + 1) * levels, :] = face_north * (
            from_n[part, :] - send_n[part, :]
        )

    row = lax.broadcasted_iota(jnp.int32, (8, tile), 0)

    def columns(g, fixed, at):
        span = pl.ds(pl.multiple_of(g * 8, 8), 8)
        for t in range(tracers):
            first, last = zero, zero
            for k in range(levels):
                cells = vbuf[k, t, span, :]
                if fixed is not None:
                    fix = rows_fix[fixed + t * levels + k : fixed + t * levels + k + 1, :]
                    cells = cells + jnp.where(row == at, jnp.broadcast_to(fix, (8, tile)), 0.0)
                    vbuf[k, t, span, :] = cells
                turned = pltpu.roll(cells, k, 1)
                first = jnp.where(lane == k, turned, first)
                last = jnp.where(lane == (k - 1) % tile, turned, last)
            send_w[t, span, :] = first
            send_e[t, span, :] = last

    columns(0, 0, 0)
    columns(band // 8 - 1, tracers * levels, 7)

    @pl.loop(1, band // 8 - 1)
    def _(g):
        columns(g, None, None)

    to_east = remote(2, send_e, from_w, east)
    to_west = remote(3, send_w, from_e, west)
    to_east.start()
    to_west.start()
    after_columns()
    during_columns()
    to_east.wait()
    to_west.wait()

    even = lax.rem(lane_iota((band, tile)), 2) == 0
    face_last = jnp.maximum(pltpu.roll(send_e[tracers], 1, 1), 0.0)
    face_first = jnp.minimum(pltpu.roll(from_w[tracers], 2, 1), 0.0)
    for t in range(tracers):
        at_last = face_last * (from_e[t] - pltpu.roll(send_e[t], 1, 1))
        at_first = face_first * (pltpu.roll(send_w[t], 1, 1) - pltpu.roll(from_w[t], 2, 1))
        merged[t, 0] = jnp.where(even, at_last, at_first)
        merged[t, 1] = jnp.where(even, at_first, at_last)


def front_scratch(levels, tracers, band, tile, merged=True):
    f32 = jnp.float32
    return [
        pltpu.VMEM((levels, tracers, band, tile), f32),
        pltpu.VMEM((2, levels, band, tile), f32),
        pltpu.VMEM((levels - 1, band, tile), f32),
        pltpu.VMEM((levels, tracers, band, tile), f32),
        pltpu.VMEM((levels - 1, band, tile), f32),
        pltpu.VMEM((levels * (tracers + 1), tile), f32),
        pltpu.VMEM((levels * tracers, tile), f32),
        pltpu.VMEM((tracers + 1, band, tile), f32),
        pltpu.VMEM((tracers, band, tile), f32),
        pltpu.VMEM((levels * (tracers + 1), tile), f32),
        pltpu.VMEM((levels * tracers, tile), f32),
        pltpu.VMEM((tracers + 1, band, tile), f32),
        pltpu.VMEM((tracers, band, tile), f32),
        pltpu.VMEM((2 * tracers * levels, tile), f32),
        pltpu.VMEM((tracers, 2, band, tile), f32),
        pltpu.SemaphoreType.DMA((2 * CHUNKS + 1,)),
        pltpu.SemaphoreType.DMA((4,)),
        pltpu.SemaphoreType.DMA((4,)),
    ]


FRONT = 18


def sweep_all(c_ref, vbuf, obuf, done):
    levels, tracers, band, tile = vbuf.shape
    lane = lane_iota((8, tile))

    @pl.loop(0, band // 8)
    def _(g):
        span = pl.ds(pl.multiple_of(g * 8, 8), 8)
        for k in range(levels):
            face = c_ref[0, k, span, :]
            out_face, in_face = jnp.maximum(face, 0.0), jnp.minimum(face, 0.0)
            for t in range(tracers):
                cells = vbuf[k, t, span, :]
                rise = jnp.where(lane == tile - 1, 0.0, pltpu.roll(cells, tile - 1, 1) - cells)
                obuf[k, t, span, :] = cells + out_face * rise + pltpu.roll(in_face * rise, 1, 1)
        done(g)


def add_sides(cells, merged, span, out):
    levels, tracers, band, tile = cells.shape
    lane = lane_iota((8, tile))
    ends = (lane == 0) | (lane == tile - 1)
    for t in range(tracers):
        sides = [merged[t, 0, span, :], merged[t, 1, span, :]]
        for k in range(levels):
            turned = pltpu.roll(sides[k % 2], tile - 1 - k, 1)
            out[k, t, span, :] = cells[k, t, span, :] + jnp.where(ends, turned, 0.0)


def chip_at(step):
    shift = lax.rem(step * 27, 64)
    lon, lat = lax.axis_index("lon"), lax.axis_index("lat")
    x = lax.rem(lon // 8 + shift // 16, 4)
    y = lax.rem(lax.rem(lon // 2, 4) + lax.rem(shift // 4, 4), 4)
    z = lax.rem((lat // 2) * 2 + lax.rem(lon, 2) + lax.rem(shift, 4), 4)
    return x * 8 + y * 2 + lax.rem(z, 2), (z // 2) * 2


def first_kernel(
    lon_count, lat_count, capacity, a_hbm, c_hbm, m_hbm, kernels_hbm, owner_ref, cell_ref, out_hbm, got_hbm, *scratch
):
    front, rest = scratch[:FRONT], scratch[FRONT:]
    (
        obuf, kernels, rows, table, table_smem, stage, blocks,
        store_sem, trade_send, trade_recv, own_sem, kernels_sem, table_sem,
    ) = rest
    c_ref, vbuf, merged = front[1], front[3], front[14]
    levels, tracers, band, tile = vbuf.shape
    held = kernels.shape[1]
    devices = lon_count * lat_count
    my_lon, my_lat = lax.axis_index("lon"), lax.axis_index("lat")
    me = my_lon * lat_count + my_lat
    used = pl.ds(0, HALF)
    low = lane_iota((HALF, LANES)) < capacity

    def send(lon, lat):
        pltpu.make_async_remote_copy(
            src_ref=blocks.at[lon * lat_count + lat, used], dst_ref=got_hbm.at[me, used],
            send_sem=trade_send, recv_sem=trade_recv,
            device_id={"lon": lon, "lat": lat}, device_id_type=MESH,
        ).start()

    def fill(places):
        wides = []
        for i, (lon, lat) in enumerate(places):
            first = ((lon * lat_count + lat) // 2) * LANES

            @pl.loop(0, LANES // 64)
            def _(part):
                for j in range(64):
                    at = part * 64 + j
                    source = table_smem[first + at] & (2 * held - 1)
                    stage[i, pl.ds(at, 1), :] = rows[pl.ds(source, 1), :]

        for i in range(len(places)):
            wides.append(stage[i].T)
        for (lon, lat), wide in zip(places, wides):
            first, second = wide[:HALF], wide[HALF : 2 * HALF]
            at = lon * lat_count + lat
            blocks[at, :HALF] = jnp.where(low, first, pltpu.roll(second, capacity, 1))
            blocks[at + 1, :HALF] = jnp.where(low, pltpu.roll(first, capacity, 1), second)

    def trade(begin, end):
        @pl.loop(begin, end)
        def _(part):
            places = [chip_at(part * 4 + i) for i in range(4)]
            fill(places)
            for lon, lat in places:
                send(lon, lat)
                send(lon, lat + 1)

    own = pltpu.make_async_copy(blocks.at[me, used], got_hbm.at[me, used], own_sem)

    def trade_first():
        @pl.loop(0, devices // 2)
        def _(pair):
            to_smem(pair).wait()

        places = [chip_at(i) for i in range(4)]
        fill(places)
        send(my_lon, my_lat + 1 - 2 * lax.rem(my_lat, 2))
        own.start()
        for lon, lat in places[1:]:
            send(lon, lat)
            send(lon, lat + 1)
        trade(1, 4)

    def to_smem(pair):
        return pltpu.make_async_copy(
            table.at[pair], table_smem.at[pl.ds(pair * LANES, LANES)], table_sem.at[pair]
        )

    def at_entry():
        load = pltpu.make_async_copy(kernels_hbm, kernels, kernels_sem)
        load.start()
        barrier = pltpu.get_barrier_semaphore()

        @pl.loop(1, devices)
        def _(i):
            peer = lax.rem(me + i, devices)
            pl.semaphore_signal(
                barrier, inc=1, device_id={"lon": peer // lat_count, "lat": lax.rem(peer, lat_count)},
                device_id_type=MESH,
            )

        table[...] = jnp.clip(slot_table(owner_ref, capacity, held) + 7, 0, held + 7)

        @pl.loop(0, devices // 2)
        def _(pair):
            to_smem(pair).start()

        load.wait()
        rows[0:8, :] = jnp.where(lane_iota((8, LANES)) == levels, -1.0, 0.0)
        for chunk in range(held // LANES):
            tall = jnp.concatenate(
                [
                    kernels[:, chunk * LANES : (chunk + 1) * LANES],
                    jnp.broadcast_to(cell_ref[chunk : chunk + 1, :].astype(jnp.float32), (8, LANES)),
                    jnp.zeros((LANES - levels - 8, LANES), jnp.float32),
                ],
                axis=0,
            )
            rows[8 + chunk * LANES : 8 + (chunk + 1) * LANES, :] = tall.T

    def before_rows():
        pl.semaphore_wait(pltpu.get_barrier_semaphore(), devices - 1)

    def main_sweep():
        sweep_all(c_ref, vbuf, obuf, lambda g: None)

    hooks = (at_entry, before_rows, trade_first, lambda: trade(4, devices // 8), main_sweep)
    transport_front(lon_count, lat_count, hooks, a_hbm, c_hbm, m_hbm, front)

    def stored(t, r):
        return pltpu.make_async_copy(obuf.at[:, t, r, :], out_hbm.at[t, r], store_sem.at[t * band + r])

    @pl.loop(0, band // 8)
    def _(g):
        add_sides(obuf, merged, pl.ds(pl.multiple_of(g * 8, 8), 8), obuf)
        for t in range(tracers):
            for r in range(8):
                stored(t, g * 8 + r).start()

    own.wait()
    most = pl.ds(0, devices - 1)
    pltpu.make_async_remote_copy(
        src_ref=blocks.at[most, used], dst_ref=got_hbm.at[most, used],
        send_sem=trade_send, recv_sem=trade_recv,
        device_id={"lon": my_lon, "lat": lax.rem(my_lat + 1, lat_count)},
        device_id_type=MESH,
    ).wait()

    @pl.loop(0, band)
    def _(r):
        for t in range(tracers):
            stored(t, r).wait()


def second_kernel(lon_count, lat_count, a_hbm, c_hbm, m_hbm, out_hbm, sides_ref, *scratch):
    front, (obuf, store_sem) = scratch[:FRONT], scratch[FRONT:]
    c_ref, vbuf, merged = front[1], front[3], front[14]
    band = vbuf.shape[2]

    def at_entry():
        lon, lat = lax.axis_index("lon"), lax.axis_index("lat")
        barrier = pltpu.get_barrier_semaphore()
        for d_lon, d_lat in ((1, 0), (lon_count - 1, 0), (0, 1), (0, lat_count - 1)):
            pl.semaphore_signal(
                barrier, inc=1,
                device_id={"lon": lax.rem(lon + d_lon, lon_count), "lat": lax.rem(lat + d_lat, lat_count)},
                device_id_type=MESH,
            )

    def before_rows():
        pl.semaphore_wait(pltpu.get_barrier_semaphore(), 4)

    def stored(g):
        span = pl.ds(pl.multiple_of(g * 8, 8), 8)
        return pltpu.make_async_copy(obuf.at[:, :, span, :], out_hbm.at[:, :, span, :], store_sem.at[g])

    def main_sweep():
        sweep_all(c_ref, vbuf, obuf, lambda g: stored(g).start())

    hooks = (at_entry, before_rows, lambda: None, lambda: None, main_sweep)
    transport_front(lon_count, lat_count, hooks, a_hbm, c_hbm, m_hbm, front)
    sides_ref[...] = merged[...]

    @pl.loop(0, band // 8)
    def _(g):
        stored(g).wait()


def first_step(state, courant, mixing, kernel_blocks, owner, cell, lon_count, lat_count, capacity):
    levels, tracers, band, tile = state.shape
    devices = lon_count * lat_count
    held = kernel_blocks.shape[1]
    f32 = jnp.float32
    small = pl.BlockSpec(memory_space=pltpu.VMEM)
    return pl.pallas_call(
        functools.partial(first_kernel, lon_count, lat_count, capacity),
        out_shape=(
            jax.ShapeDtypeStruct((tracers, band, levels, tile), f32),
            jax.ShapeDtypeStruct((devices, ROOM, LANES), f32),
        ),
        in_specs=[ANY] * 4 + [small] * 2,
        out_specs=(ANY, ANY),
        scratch_shapes=front_scratch(levels, tracers, band, tile)
        + [
            pltpu.VMEM((levels, tracers, band, tile), f32),
            pltpu.VMEM((levels, held), f32),
            pltpu.VMEM((2 * held, LANES), f32),
            pltpu.VMEM((devices // 2, LANES), jnp.int32),
            pltpu.SMEM((devices * capacity,), jnp.int32),
            pltpu.VMEM((4, LANES, LANES), f32),
            pltpu.VMEM((devices, ROOM, LANES), f32),
            pltpu.SemaphoreType.DMA((tracers * band,)),
            pltpu.SemaphoreType.DMA,
            pltpu.SemaphoreType.DMA,
            pltpu.SemaphoreType.DMA,
            pltpu.SemaphoreType.DMA,
            pltpu.SemaphoreType.DMA((devices // 2,)),
        ],
        compiler_params=pltpu.CompilerParams(
            collective_id=0, has_side_effects=True, vmem_limit_bytes=VMEM_LIMIT
        ),
        name="first_step",
    )(state, courant, mixing, kernel_blocks, owner, cell)


def second_front(state, courant, mixing, lon_count, lat_count):
    levels, tracers, band, tile = state.shape
    return pl.pallas_call(
        functools.partial(second_kernel, lon_count, lat_count),
        out_shape=(
            jax.ShapeDtypeStruct(state.shape, jnp.float32),
            jax.ShapeDtypeStruct((tracers, 2, band, tile), jnp.float32),
        ),
        in_specs=[ANY] * 3,
        out_specs=(ANY, pl.BlockSpec(memory_space=pltpu.VMEM)),
        scratch_shapes=front_scratch(levels, tracers, band, tile)
        + [pltpu.VMEM((levels, tracers, band, tile), jnp.float32), pltpu.SemaphoreType.DMA((band // 8,))],
        compiler_params=pltpu.CompilerParams(
            collective_id=1, has_side_effects=True, vmem_limit_bytes=VMEM_LIMIT
        ),
        name="second_front",
    )(state, courant, mixing)


def last_kernel(
    cells_hbm, sides_ref, first_hbm, out_hbm, flux_ref, cells, obuf, ground, cell_sem, store_sem, ground_sem
):
    band = cells.shape[2]

    def rows_of(g):
        return pl.ds(pl.multiple_of(g * 8, 8), 8)

    def load(g):
        return pltpu.make_async_copy(
            cells_hbm.at[:, :, rows_of(g), :], cells.at[:, :, rows_of(g), :], cell_sem.at[g]
        )

    def stored(g):
        return pltpu.make_async_copy(
            obuf.at[:, :, rows_of(g), :], out_hbm.at[:, :, rows_of(g), :], store_sem.at[g]
        )

    @pl.loop(0, band // 8)
    def _(g):
        load(g).start()

    load_ground = pltpu.make_async_copy(first_hbm.at[:, :, 0, :], ground, ground_sem)
    load_ground.start()

    @pl.loop(0, band // 8)
    def _(g):
        load(g).wait()
        add_sides(cells, sides_ref, rows_of(g), obuf)
        stored(g).start()

    load_ground.wait()
    flux_ref[...] = ground[...] + obuf[0]

    @pl.loop(0, band // 8)
    def _(g):
        stored(g).wait()


def last_part(cells, sides, after_first):
    levels, tracers, band, tile = cells.shape
    return pl.pallas_call(
        last_kernel,
        out_shape=(
            jax.ShapeDtypeStruct(cells.shape, jnp.float32),
            jax.ShapeDtypeStruct(cells.shape[1:], jnp.float32),
        ),
        in_specs=[ANY, pl.BlockSpec(memory_space=pltpu.VMEM), ANY],
        out_specs=(ANY, pl.BlockSpec(memory_space=pltpu.VMEM)),
        scratch_shapes=[
            pltpu.VMEM((levels, tracers, band, tile), jnp.float32),
            pltpu.VMEM((levels, tracers, band, tile), jnp.float32),
            pltpu.VMEM((tracers, band, tile), jnp.float32),
            pltpu.SemaphoreType.DMA((band // 8,)),
            pltpu.SemaphoreType.DMA((band // 8,)),
            pltpu.SemaphoreType.DMA,
        ],
        compiler_params=pltpu.CompilerParams(vmem_limit_bytes=VMEM_LIMIT),
        name="last_part",
    )(cells, sides, after_first)


def force_kernel(capacity, levels, lines, got_hbm, state_hbm, out_hbm, got_ref, rows, ids, ids_smem, state, total, *rest):
    sums, (got_sem, ids_sem, load_sem, store_sem) = rest[:STREAMS], rest[STREAMS:]
    devices = got_ref.shape[0]
    cells_all = lines * LANES
    load_got = pltpu.make_async_copy(got_hbm, got_ref, got_sem)
    load_got.start()
    load = pltpu.make_async_copy(state_hbm, state, load_sem)
    load.start()
    low = lane_iota((HALF, LANES)) < capacity
    group = 8
    zero = jnp.zeros((64, LANES), jnp.float32)

    @pl.loop(0, cells_all // 64)
    def _(i):
        for s in range(STREAMS):
            sums[s][pl.ds(pl.multiple_of(i * 64, 64), 64), :] = zero

    load_got.wait()

    def to_smem(pair):
        return pltpu.make_async_copy(
            ids.at[pair], ids_smem.at[pl.ds(pair * LANES, LANES)], ids_sem.at[pair]
        )

    @pl.loop(0, devices // (2 * group))
    def _(part):
        for i in range(group):
            pair = part * group + i
            one, two = got_ref[2 * pair, :HALF], got_ref[2 * pair + 1, :HALF]
            first = jnp.where(low, one, pltpu.roll(two, capacity, 1))
            second = jnp.where(low, pltpu.roll(one, capacity, 1), two)
            cell = second[levels - HALF : levels - HALF + 1, :].astype(jnp.int32)
            ids[pl.ds(pair, 1), :] = jnp.where(cell < 0, cells_all, cell)
            wide = jnp.concatenate([first, second, jnp.zeros((LANES - 2 * HALF, LANES), jnp.float32)], axis=0)
            rows[pl.ds(pl.multiple_of(pair * LANES, LANES), LANES), :] = wide.T
        for i in range(group):
            to_smem(part * group + i).start()

    @pl.loop(0, devices // 2)
    def _(pair):
        to_smem(pair).wait()

    @pl.loop(0, devices * capacity // (8 * STREAMS))
    def _(part):
        for i in range(8):
            at = [part * 8 * STREAMS + i * STREAMS + s for s in range(STREAMS)]
            cell = [ids_smem[at[s]] for s in range(STREAMS)]
            new = [sums[s][pl.ds(cell[s], 1), :] + rows[pl.ds(at[s], 1), :] for s in range(STREAMS)]
            for s in range(STREAMS):
                sums[s][pl.ds(cell[s], 1), :] = new[s]

    load.wait()

    def level_rows(line):
        return pl.ds(pl.multiple_of(line * levels, 8), levels)

    def stored(line):
        return pltpu.make_async_copy(total.at[level_rows(line)], out_hbm.at[:, line, :], store_sem.at[line])

    group = 16

    @pl.loop(0, lines // group)
    def _(part):
        turned = []
        for i in range(group):
            span = pl.ds(pl.multiple_of((part * group + i) * LANES, LANES), LANES)
            total_here = sums[0][span, :]
            for s in range(1, STREAMS):
                total_here = total_here + sums[s][span, :]
            turned.append(total_here.T[:levels])
        for i in range(group):
            at = level_rows(part * group + i)
            total[at, :] = state[at, :] + turned[i]
        for i in range(group):
            stored(part * group + i).start()

    @pl.loop(0, lines)
    def _(line):
        stored(line).wait()


def add_forcing(got, after_first, capacity):
    tracers, band, levels, tile = after_first.shape
    devices = got.shape[0]
    lines = tracers * band
    out = pl.pallas_call(
        functools.partial(force_kernel, capacity, levels, lines),
        out_shape=jax.ShapeDtypeStruct((levels, lines, tile), jnp.float32),
        in_specs=[ANY, ANY],
        out_specs=ANY,
        scratch_shapes=[
            pltpu.VMEM(got.shape, jnp.float32),
            pltpu.VMEM((devices * capacity, LANES), jnp.float32),
            pltpu.VMEM((devices // 2, LANES), jnp.int32),
            pltpu.SMEM((devices * capacity,), jnp.int32),
            pltpu.VMEM((levels * lines, tile), jnp.float32),
            pltpu.VMEM((levels * lines, tile), jnp.float32),
        ]
        + [pltpu.VMEM((lines * tile + 8, LANES), jnp.float32)] * STREAMS
        + [
            pltpu.SemaphoreType.DMA,
            pltpu.SemaphoreType.DMA((devices // 2,)),
            pltpu.SemaphoreType.DMA,
            pltpu.SemaphoreType.DMA((lines,)),
        ],
        compiler_params=pltpu.CompilerParams(vmem_limit_bytes=VMEM_LIMIT),
        name="add_forcing",
    )(got, after_first.reshape(levels * lines, tile))
    return out.reshape(levels, tracers, band, tile)


def on_device(adjoint_in, courant, mixing, kernel_blocks, sounding_dest, sounding_cell):
    lon_count = lax.axis_size("lon")
    lat_count = lax.axis_size("lat")
    devices = lon_count * lat_count
    held = kernel_blocks.shape[1]
    capacity = 4 * held // devices
    owner = sounding_dest.reshape(held // LANES, LANES)
    cell = sounding_cell.reshape(held // LANES, LANES)
    after_first, got = first_step(
        adjoint_in, courant, mixing, kernel_blocks, owner, cell, lon_count, lat_count, capacity
    )
    forced = add_forcing(got, after_first, capacity)
    swept, sides = second_front(forced, courant, mixing, lon_count, lat_count)
    return last_part(swept, sides, after_first)


def solution(mesh):
    placed = (
        P(None, None, "lat", "lon"),
        P(None, None, "lat", "lon"),
        P(None, "lat", "lon"),
        P(None, ("lon", "lat")),
        P(("lon", "lat"), None),
        P(("lon", "lat")),
    )
    return jax.shard_map(
        on_device,
        mesh=mesh,
        in_specs=placed,
        out_specs=(P(None, None, "lat", "lon"), P(None, "lat", "lon")),
        check_vma=False,
    )
```

```python
import functools
import jax
import jax.numpy as jnp
from jax import lax
from jax.experimental import pallas as pl
from jax.experimental.pallas import tpu as pltpu
from jax.sharding import PartitionSpec as P

MESH = pl.DeviceIdType.MESH
ANY = pl.BlockSpec(memory_space=pl.ANY)
LANES = 128
HALF = 37
ROOM = 40
STREAMS = 4
CHUNKS = 4
VMEM_LIMIT = 60 * 1024 * 1024


def lane_iota(shape):
    return lax.broadcasted_iota(jnp.int32, shape, len(shape) - 1)


def slot_table(owner_ref, capacity, held):
    row_id = lax.broadcasted_iota(jnp.int32, (LANES, LANES), 0)
    col_id = lax.broadcasted_iota(jnp.int32, (LANES, LANES), 1)
    pair_id = lax.broadcasted_iota(jnp.int32, (LANES // 2, LANES), 0)
    place = lane_iota((LANES // 2, LANES)).astype(jnp.float32)
    before = jnp.where(row_id < col_id, 1.0, 0.0).astype(jnp.bfloat16)
    ones = jnp.ones((LANES, LANES), jnp.bfloat16)
    base = jnp.zeros((LANES, LANES), jnp.float32)
    table = jnp.zeros((LANES // 2, LANES), jnp.float32)
    for chunk in range(held // LANES):
        owner = owner_ref[chunk : chunk + 1, :]
        hot_f = jnp.where(jnp.broadcast_to(owner, (LANES, LANES)) == row_id, 1.0, 0.0)
        hot_b = hot_f.astype(jnp.bfloat16)
        earlier = jnp.dot(hot_b, before, preferred_element_type=jnp.float32)
        rank = jnp.sum(hot_f * (earlier + base), axis=0, keepdims=True).astype(jnp.int32)
        base = base + jnp.dot(hot_b, ones, preferred_element_type=jnp.float32)
        pair = lax.shift_right_logical(owner, 1)
        slot = (owner - 2 * pair) * capacity + rank
        in_pair = jnp.where(jnp.broadcast_to(pair, pair_id.shape) == pair_id, 1.0, 0.0)
        in_slot = jnp.where(jnp.broadcast_to(slot, row_id.shape) == row_id, 1.0, 0.0)
        found = lax.dot_general(
            jnp.concatenate([in_pair * place, in_pair], axis=0).astype(jnp.bfloat16),
            in_slot.astype(jnp.bfloat16),
            (((1,), (1,)), ((), ())),
            preferred_element_type=jnp.float32,
        )
        table = table + found[: LANES // 2] + found[LANES // 2 :] * (LANES * chunk + 1.0)
    return table.astype(jnp.int32)


def transport_front(lon_count, lat_count, hooks, a_hbm, c_hbm, m_hbm, front):
    (
        a_ref, c_ref, m_ref, vbuf, rbuf, send_n, send_s, send_e, send_w,
        from_s, from_n, from_w, from_e, rows_fix, merged, load_sem, send_sem, recv_sem,
    ) = front
    at_entry, before_rows, after_rows, after_columns, during_columns = hooks
    levels, tracers, band, tile = a_ref.shape
    lon, lat = lax.axis_index("lon"), lax.axis_index("lat")
    north = {"lon": lon, "lat": lax.rem(lat + 1, lat_count)}
    south = {"lon": lon, "lat": lax.rem(lat + lat_count - 1, lat_count)}
    east = {"lon": lax.rem(lon + 1, lon_count), "lat": lat}
    west = {"lon": lax.rem(lon + lon_count - 1, lon_count), "lat": lat}

    cuts = [levels * i // CHUNKS for i in range(CHUNKS)] + [levels]
    loads = []
    for i in range(CHUNKS):
        span, faces = slice(cuts[i], cuts[i + 1]), slice(cuts[i], min(cuts[i + 1], levels - 1))
        loads.append(pltpu.make_async_copy(m_hbm.at[faces], m_ref.at[faces], load_sem.at[2 * i]))
        loads.append(pltpu.make_async_copy(a_hbm.at[span], a_ref.at[span], load_sem.at[2 * i + 1]))
    loads.append(pltpu.make_async_copy(c_hbm, c_ref, load_sem.at[2 * CHUNKS]))
    for load in loads:
        load.start()
    at_entry()
    loads[0].wait()
    loads[1].wait()

    mix = m_ref[0]
    inverse = 1.0 / (1.0 + mix)
    ratio = mix * inverse
    solved = a_ref[0] * inverse[None]
    rbuf[0] = ratio
    vbuf[0] = solved

    def down(k, carry):
        mix_above, ratio, solved = carry
        mix = m_ref[k]
        inverse = 1.0 / (1.0 + mix_above + mix - mix_above * ratio)
        ratio = mix * inverse
        solved = (a_ref[k] + mix_above[None] * solved) * inverse[None]
        rbuf[k] = ratio
        vbuf[k] = solved
        return mix, ratio, solved

    carry = (mix, ratio, solved)
    for i in range(CHUNKS):
        if i > 0:
            loads[2 * i].wait()
            loads[2 * i + 1].wait()
        carry = lax.fori_loop(max(cuts[i], 1), min(cuts[i + 1], levels - 1), down, carry)
    mix, ratio, solved = carry
    inverse = 1.0 / (1.0 + mix - mix * ratio)
    solved = (a_ref[levels - 1] + mix[None] * solved) * inverse[None]

    def keep(k, solved):
        vbuf[k] = solved
        for t in range(tracers):
            send_s[pl.ds(t * levels + k, 1), :] = solved[t, 0:1, :]
            send_n[pl.ds(t * levels + k, 1), :] = solved[t, band - 1 : band, :]

    keep(levels - 1, solved)

    def up(i, solved):
        k = levels - 2 - i
        solved = vbuf[k] + rbuf[k][None] * solved
        keep(k, solved)
        return solved

    lax.fori_loop(0, levels - 1, up, solved)

    loads[2 * CHUNKS].wait()
    edge = jnp.where(lat == lat_count - 1, 0.0, 1.0)

    @pl.loop(0, levels // 8)
    def _(j):
        for i in range(8):
            k = j * 8 + i
            send_n[pl.ds(tracers * levels + k, 1), :] = c_ref[1, k, band - 1 : band, :] * edge

    def remote(index, src, dst, to):
        return pltpu.make_async_remote_copy(
            src_ref=src, dst_ref=dst, send_sem=send_sem.at[index], recv_sem=recv_sem.at[index],
            device_id=to, device_id_type=MESH,
        )

    to_north = remote(0, send_n, from_s, north)
    to_south = remote(1, send_s, from_n, south)
    before_rows()
    to_north.start()
    to_south.start()
    after_rows()

    top = lax.broadcasted_iota(jnp.int32, (band, tile), 0) == band - 1

    @pl.loop(0, levels // 2)
    def _(j):
        swept = []
        for i in range(2):
            face = c_ref[1, 2 * j + i]
            out_face, in_face = jnp.maximum(face, 0.0), jnp.minimum(face, 0.0)
            for t in range(tracers):
                cells = vbuf[2 * j + i, t]
                rise = jnp.where(top, 0.0, pltpu.roll(cells, band - 1, 0) - cells)
                swept.append(cells + out_face * rise + pltpu.roll(in_face * rise, 1, 0))
        for i in range(2):
            for t in range(tracers):
                vbuf[2 * j + i, t] = swept[tracers * i + t]

    lane = lane_iota((8, tile))
    zero = jnp.zeros((8, tile), jnp.float32)

    @pl.loop(0, band // 8)
    def _(g):
        span = pl.ds(pl.multiple_of(g * 8, 8), 8)
        last = zero
        for k in range(levels):
            last = jnp.where(lane == (k - 1) % tile, pltpu.roll(c_ref[0, k, span, :], k, 1), last)
        send_e[tracers, span, :] = last

    to_north.wait()
    to_south.wait()
    face_south = jnp.minimum(from_s[tracers * levels :, :], 0.0)
    face_north = jnp.maximum(send_n[tracers * levels :, :], 0.0)
    for t in range(tracers):
        part = slice(t * levels, (t + 1) * levels)
        rows_fix[part, :] = face_south * (send_s[part, :] - from_s[part, :])
        rows_fix[tracers * levels + t * levels : tracers * levels + (t + 1) * levels, :] = face_north * (
            from_n[part, :] - send_n[part, :]
        )

    row = lax.broadcasted_iota(jnp.int32, (8, tile), 0)

    def columns(g, fixed, at):
        span = pl.ds(pl.multiple_of(g * 8, 8), 8)
        for t in range(tracers):
            first, last = zero, zero
            for k in range(levels):
                cells = vbuf[k, t, span, :]
                if fixed is not None:
                    fix = rows_fix[fixed + t * levels + k : fixed + t * levels + k + 1, :]
                    cells = cells + jnp.where(row == at, jnp.broadcast_to(fix, (8, tile)), 0.0)
                    vbuf[k, t, span, :] = cells
                turned = pltpu.roll(cells, k, 1)
                first = jnp.where(lane == k, turned, first)
                last = jnp.where(lane == (k - 1) % tile, turned, last)
            send_w[t, span, :] = first
            send_e[t, span, :] = last

    columns(0, 0, 0)
    columns(band // 8 - 1, tracers * levels, 7)

    @pl.loop(1, band // 8 - 1)
    def _(g):
        columns(g, None, None)

    to_east = remote(2, send_e, from_w, east)
    to_west = remote(3, send_w, from_e, west)
    to_east.start()
    to_west.start()
    after_columns()
    during_columns()
    to_east.wait()
    to_west.wait()

    even = lax.rem(lane_iota((band, tile)), 2) == 0
    face_last = jnp.maximum(pltpu.roll(send_e[tracers], 1, 1), 0.0)
    face_first = jnp.minimum(pltpu.roll(from_w[tracers], 2, 1), 0.0)
    for t in range(tracers):
        at_last = face_last * (from_e[t] - pltpu.roll(send_e[t], 1, 1))
        at_first = face_first * (pltpu.roll(send_w[t], 1, 1) - pltpu.roll(from_w[t], 2, 1))
        merged[t, 0] = jnp.where(even, at_last, at_first)
        merged[t, 1] = jnp.where(even, at_first, at_last)


def front_scratch(levels, tracers, band, tile, merged=True):
    f32 = jnp.float32
    return [
        pltpu.VMEM((levels, tracers, band, tile), f32),
        pltpu.VMEM((2, levels, band, tile), f32),
        pltpu.VMEM((levels - 1, band, tile), f32),
        pltpu.VMEM((levels, tracers, band, tile), f32),
        pltpu.VMEM((levels - 1, band, tile), f32),
        pltpu.VMEM((levels * (tracers + 1), tile), f32),
        pltpu.VMEM((levels * tracers, tile), f32),
        pltpu.VMEM((tracers + 1, band, tile), f32),
        pltpu.VMEM((tracers, band, tile), f32),
        pltpu.VMEM((levels * (tracers + 1), tile), f32),
        pltpu.VMEM((levels * tracers, tile), f32),
        pltpu.VMEM((tracers + 1, band, tile), f32),
        pltpu.VMEM((tracers, band, tile), f32),
        pltpu.VMEM((2 * tracers * levels, tile), f32),
        pltpu.VMEM((tracers, 2, band, tile), f32),
        pltpu.SemaphoreType.DMA((2 * CHUNKS + 1,)),
        pltpu.SemaphoreType.DMA((4,)),
        pltpu.SemaphoreType.DMA((4,)),
    ]


FRONT = 18


def sweep_all(c_ref, vbuf, obuf, done):
    levels, tracers, band, tile = vbuf.shape
    lane = lane_iota((8, tile))

    @pl.loop(0, band // 8)
    def _(g):
        span = pl.ds(pl.multiple_of(g * 8, 8), 8)
        for k in range(levels):
            face = c_ref[0, k, span, :]
            out_face, in_face = jnp.maximum(face, 0.0), jnp.minimum(face, 0.0)
            for t in range(tracers):
                cells = vbuf[k, t, span, :]
                rise = jnp.where(lane == tile - 1, 0.0, pltpu.roll(cells, tile - 1, 1) - cells)
                obuf[k, t, span, :] = cells + out_face * rise + pltpu.roll(in_face * rise, 1, 1)
        done(g)


def add_sides(cells, merged, span, out):
    levels, tracers, band, tile = cells.shape
    lane = lane_iota((8, tile))
    ends = (lane == 0) | (lane == tile - 1)
    for t in range(tracers):
        sides = [merged[t, 0, span, :], merged[t, 1, span, :]]
        for k in range(levels):
            turned = pltpu.roll(sides[k % 2], tile - 1 - k, 1)
            out[k, t, span, :] = cells[k, t, span, :] + jnp.where(ends, turned, 0.0)


def chip_at(step):
    shift = lax.rem(step * 27, 64)
    lon, lat = lax.axis_index("lon"), lax.axis_index("lat")
    x = lax.rem(lon // 8 + shift // 16, 4)
    y = lax.rem(lax.rem(lon // 2, 4) + lax.rem(shift // 4, 4), 4)
    z = lax.rem((lat // 2) * 2 + lax.rem(lon, 2) + lax.rem(shift, 4), 4)
    return x * 8 + y * 2 + lax.rem(z, 2), (z // 2) * 2


def first_kernel(
    lon_count, lat_count, capacity, a_hbm, c_hbm, m_hbm, kernels_hbm, owner_ref, cell_ref, out_hbm, got_hbm, *scratch
):
    front, rest = scratch[:FRONT], scratch[FRONT:]
    (
        obuf, kernels, rows, table, table_smem, stage, blocks,
        store_sem, trade_send, trade_recv, own_sem, kernels_sem, table_sem,
    ) = rest
    c_ref, vbuf, merged = front[1], front[3], front[14]
    levels, tracers, band, tile = vbuf.shape
    held = kernels.shape[1]
    devices = lon_count * lat_count
    my_lon, my_lat = lax.axis_index("lon"), lax.axis_index("lat")
    me = my_lon * lat_count + my_lat
    used = pl.ds(0, HALF)
    low = lane_iota((HALF, LANES)) < capacity

    def send(lon, lat):
        pltpu.make_async_remote_copy(
            src_ref=blocks.at[lon * lat_count + lat, used], dst_ref=got_hbm.at[me, used],
            send_sem=trade_send, recv_sem=trade_recv,
            device_id={"lon": lon, "lat": lat}, device_id_type=MESH,
        ).start()

    def fill(places):
        wides = []
        for i, (lon, lat) in enumerate(places):
            first = ((lon * lat_count + lat) // 2) * LANES

            @pl.loop(0, LANES // 64)
            def _(part):
                for j in range(64):
                    at = part * 64 + j
                    source = table_smem[first + at] & (2 * held - 1)
                    stage[i, pl.ds(at, 1), :] = rows[pl.ds(source, 1), :]

        for i in range(len(places)):
            wides.append(stage[i].T)
        for (lon, lat), wide in zip(places, wides):
            first, second = wide[:HALF], wide[HALF : 2 * HALF]
            at = lon * lat_count + lat
            blocks[at, :HALF] = jnp.where(low, first, pltpu.roll(second, capacity, 1))
            blocks[at + 1, :HALF] = jnp.where(low, pltpu.roll(first, capacity, 1), second)

    def trade(begin, end):
        @pl.loop(begin, end)
        def _(part):
            places = [chip_at(part * 4 + i) for i in range(4)]
            fill(places)
            for lon, lat in places:
                send(lon, lat)
                send(lon, lat + 1)

    own = pltpu.make_async_copy(blocks.at[me, used], got_hbm.at[me, used], own_sem)

    def trade_first():
        @pl.loop(0, devices // 2)
        def _(pair):
            to_smem(pair).wait()

        places = [chip_at(i) for i in range(4)]
        fill(places)
        send(my_lon, my_lat + 1 - 2 * lax.rem(my_lat, 2))
        own.start()
        for lon, lat in places[1:]:
            send(lon, lat)
            send(lon, lat + 1)
        trade(1, 4)

    def to_smem(pair):
        return pltpu.make_async_copy(
            table.at[pair], table_smem.at[pl.ds(pair * LANES, LANES)], table_sem.at[pair]
        )

    def at_entry():
        load = pltpu.make_async_copy(kernels_hbm, kernels, kernels_sem)
        load.start()
        barrier = pltpu.get_barrier_semaphore()

        @pl.loop(1, devices)
        def _(i):
            peer = lax.rem(me + i, devices)
            pl.semaphore_signal(
                barrier, inc=1, device_id={"lon": peer // lat_count, "lat": lax.rem(peer, lat_count)},
                device_id_type=MESH,
            )

        table[...] = jnp.clip(slot_table(owner_ref, capacity, held) + 7, 0, held + 7)

        @pl.loop(0, devices // 2)
        def _(pair):
            to_smem(pair).start()

        load.wait()
        rows[0:8, :] = jnp.where(lane_iota((8, LANES)) == levels, -1.0, 0.0)
        for chunk in range(held // LANES):
            tall = jnp.concatenate(
                [
                    kernels[:, chunk * LANES : (chunk + 1) * LANES],
                    jnp.broadcast_to(cell_ref[chunk : chunk + 1, :].astype(jnp.float32), (8, LANES)),
                    jnp.zeros((LANES - levels - 8, LANES), jnp.float32),
                ],
                axis=0,
            )
            rows[8 + chunk * LANES : 8 + (chunk + 1) * LANES, :] = tall.T
        pl.semaphore_wait(barrier, devices - 1)
        trade_first()

    def main_sweep():
        sweep_all(c_ref, vbuf, obuf, lambda g: None)

    groups = devices // 8
    hooks = (at_entry, lambda: None, lambda: trade(4, 9), lambda: trade(9, groups), main_sweep)
    transport_front(lon_count, lat_count, hooks, a_hbm, c_hbm, m_hbm, front)

    def stored(t, r):
        return pltpu.make_async_copy(obuf.at[:, t, r, :], out_hbm.at[t, r], store_sem.at[t * band + r])

    @pl.loop(0, band // 8)
    def _(g):
        add_sides(obuf, merged, pl.ds(pl.multiple_of(g * 8, 8), 8), obuf)
        for t in range(tracers):
            for r in range(8):
                stored(t, g * 8 + r).start()

    own.wait()
    most = pl.ds(0, devices - 1)
    pltpu.make_async_remote_copy(
        src_ref=blocks.at[most, used], dst_ref=got_hbm.at[most, used],
        send_sem=trade_send, recv_sem=trade_recv,
        device_id={"lon": my_lon, "lat": lax.rem(my_lat + 1, lat_count)},
        device_id_type=MESH,
    ).wait()

    @pl.loop(0, band)
    def _(r):
        for t in range(tracers):
            stored(t, r).wait()


def second_kernel(lon_count, lat_count, a_hbm, c_hbm, m_hbm, out_hbm, sides_ref, *scratch):
    front, (obuf, store_sem) = scratch[:FRONT], scratch[FRONT:]
    c_ref, vbuf, merged = front[1], front[3], front[14]
    band = vbuf.shape[2]

    def at_entry():
        lon, lat = lax.axis_index("lon"), lax.axis_index("lat")
        barrier = pltpu.get_barrier_semaphore()
        for d_lon, d_lat in ((1, 0), (lon_count - 1, 0), (0, 1), (0, lat_count - 1)):
            pl.semaphore_signal(
                barrier, inc=1,
                device_id={"lon": lax.rem(lon + d_lon, lon_count), "lat": lax.rem(lat + d_lat, lat_count)},
                device_id_type=MESH,
            )

    def before_rows():
        pl.semaphore_wait(pltpu.get_barrier_semaphore(), 4)

    def stored(g):
        span = pl.ds(pl.multiple_of(g * 8, 8), 8)
        return pltpu.make_async_copy(obuf.at[:, :, span, :], out_hbm.at[:, :, span, :], store_sem.at[g])

    def main_sweep():
        sweep_all(c_ref, vbuf, obuf, lambda g: stored(g).start())

    hooks = (at_entry, before_rows, lambda: None, lambda: None, main_sweep)
    transport_front(lon_count, lat_count, hooks, a_hbm, c_hbm, m_hbm, front)
    sides_ref[...] = merged[...]

    @pl.loop(0, band // 8)
    def _(g):
        stored(g).wait()


def first_step(state, courant, mixing, kernel_blocks, owner, cell, lon_count, lat_count, capacity):
    levels, tracers, band, tile = state.shape
    devices = lon_count * lat_count
    held = kernel_blocks.shape[1]
    f32 = jnp.float32
    small = pl.BlockSpec(memory_space=pltpu.VMEM)
    return pl.pallas_call(
        functools.partial(first_kernel, lon_count, lat_count, capacity),
        out_shape=(
            jax.ShapeDtypeStruct((tracers, band, levels, tile), f32),
            jax.ShapeDtypeStruct((devices, ROOM, LANES), f32),
        ),
        in_specs=[ANY] * 4 + [small] * 2,
        out_specs=(ANY, ANY),
        scratch_shapes=front_scratch(levels, tracers, band, tile)
        + [
            pltpu.VMEM((levels, tracers, band, tile), f32),
            pltpu.VMEM((levels, held), f32),
            pltpu.VMEM((2 * held, LANES), f32),
            pltpu.VMEM((devices // 2, LANES), jnp.int32),
            pltpu.SMEM((devices * capacity,), jnp.int32),
            pltpu.VMEM((4, LANES, LANES), f32),
            pltpu.VMEM((devices, ROOM, LANES), f32),
            pltpu.SemaphoreType.DMA((tracers * band,)),
            pltpu.SemaphoreType.DMA,
            pltpu.SemaphoreType.DMA,
            pltpu.SemaphoreType.DMA,
            pltpu.SemaphoreType.DMA,
            pltpu.SemaphoreType.DMA((devices // 2,)),
        ],
        compiler_params=pltpu.CompilerParams(
            collective_id=0, has_side_effects=True, vmem_limit_bytes=VMEM_LIMIT
        ),
        name="first_step",
    )(state, courant, mixing, kernel_blocks, owner, cell)


def second_front(state, courant, mixing, lon_count, lat_count):
    levels, tracers, band, tile = state.shape
    return pl.pallas_call(
        functools.partial(second_kernel, lon_count, lat_count),
        out_shape=(
            jax.ShapeDtypeStruct(state.shape, jnp.float32),
            jax.ShapeDtypeStruct((tracers, 2, band, tile), jnp.float32),
        ),
        in_specs=[ANY] * 3,
        out_specs=(ANY, pl.BlockSpec(memory_space=pltpu.VMEM)),
        scratch_shapes=front_scratch(levels, tracers, band, tile)
        + [pltpu.VMEM((levels, tracers, band, tile), jnp.float32), pltpu.SemaphoreType.DMA((band // 8,))],
        compiler_params=pltpu.CompilerParams(
            collective_id=1, has_side_effects=True, vmem_limit_bytes=VMEM_LIMIT
        ),
        name="second_front",
    )(state, courant, mixing)


def last_kernel(
    cells_hbm, sides_ref, first_hbm, out_hbm, flux_ref, cells, obuf, ground, cell_sem, store_sem, ground_sem
):
    band = cells.shape[2]

    def rows_of(g):
        return pl.ds(pl.multiple_of(g * 8, 8), 8)

    def load(g):
        return pltpu.make_async_copy(
            cells_hbm.at[:, :, rows_of(g), :], cells.at[:, :, rows_of(g), :], cell_sem.at[g]
        )

    def stored(g):
        return pltpu.make_async_copy(
            obuf.at[:, :, rows_of(g), :], out_hbm.at[:, :, rows_of(g), :], store_sem.at[g]
        )

    @pl.loop(0, band // 8)
    def _(g):
        load(g).start()

    load_ground = pltpu.make_async_copy(first_hbm.at[:, :, 0, :], ground, ground_sem)
    load_ground.start()

    @pl.loop(0, band // 8)
    def _(g):
        load(g).wait()
        add_sides(cells, sides_ref, rows_of(g), obuf)
        stored(g).start()

    load_ground.wait()
    flux_ref[...] = ground[...] + obuf[0]

    @pl.loop(0, band // 8)
    def _(g):
        stored(g).wait()


def last_part(cells, sides, after_first):
    levels, tracers, band, tile = cells.shape
    return pl.pallas_call(
        last_kernel,
        out_shape=(
            jax.ShapeDtypeStruct(cells.shape, jnp.float32),
            jax.ShapeDtypeStruct(cells.shape[1:], jnp.float32),
        ),
        in_specs=[ANY, pl.BlockSpec(memory_space=pltpu.VMEM), ANY],
        out_specs=(ANY, pl.BlockSpec(memory_space=pltpu.VMEM)),
        scratch_shapes=[
            pltpu.VMEM((levels, tracers, band, tile), jnp.float32),
            pltpu.VMEM((levels, tracers, band, tile), jnp.float32),
            pltpu.VMEM((tracers, band, tile), jnp.float32),
            pltpu.SemaphoreType.DMA((band // 8,)),
            pltpu.SemaphoreType.DMA((band // 8,)),
            pltpu.SemaphoreType.DMA,
        ],
        compiler_params=pltpu.CompilerParams(vmem_limit_bytes=VMEM_LIMIT),
        name="last_part",
    )(cells, sides, after_first)


def force_kernel(capacity, levels, lines, got_hbm, state_hbm, out_hbm, got_ref, rows, ids, ids_smem, state, total, *rest):
    sums, (got_sem, ids_sem, load_sem, store_sem) = rest[:STREAMS], rest[STREAMS:]
    devices = got_ref.shape[0]
    cells_all = lines * LANES
    load_got = pltpu.make_async_copy(got_hbm, got_ref, got_sem)
    load_got.start()
    load = pltpu.make_async_copy(state_hbm, state, load_sem)
    load.start()
    low = lane_iota((HALF, LANES)) < capacity
    group = 8
    zero = jnp.zeros((64, LANES), jnp.float32)

    @pl.loop(0, cells_all // 64)
    def _(i):
        for s in range(STREAMS):
            sums[s][pl.ds(pl.multiple_of(i * 64, 64), 64), :] = zero

    load_got.wait()

    def to_smem(pair):
        return pltpu.make_async_copy(
            ids.at[pair], ids_smem.at[pl.ds(pair * LANES, LANES)], ids_sem.at[pair]
        )

    @pl.loop(0, devices // (2 * group))
    def _(part):
        for i in range(group):
            pair = part * group + i
            one, two = got_ref[2 * pair, :HALF], got_ref[2 * pair + 1, :HALF]
            first = jnp.where(low, one, pltpu.roll(two, capacity, 1))
            second = jnp.where(low, pltpu.roll(one, capacity, 1), two)
            cell = second[levels - HALF : levels - HALF + 1, :].astype(jnp.int32)
            ids[pl.ds(pair, 1), :] = jnp.where(cell < 0, cells_all, cell)
            wide = jnp.concatenate([first, second, jnp.zeros((LANES - 2 * HALF, LANES), jnp.float32)], axis=0)
            rows[pl.ds(pl.multiple_of(pair * LANES, LANES), LANES), :] = wide.T
        for i in range(group):
            to_smem(part * group + i).start()

    @pl.loop(0, devices // 2)
    def _(pair):
        to_smem(pair).wait()

    @pl.loop(0, devices * capacity // (8 * STREAMS))
    def _(part):
        for i in range(8):
            at = [part * 8 * STREAMS + i * STREAMS + s for s in range(STREAMS)]
            cell = [ids_smem[at[s]] for s in range(STREAMS)]
            new = [sums[s][pl.ds(cell[s], 1), :] + rows[pl.ds(at[s], 1), :] for s in range(STREAMS)]
            for s in range(STREAMS):
                sums[s][pl.ds(cell[s], 1), :] = new[s]

    load.wait()

    def level_rows(line):
        return pl.ds(pl.multiple_of(line * levels, 8), levels)

    def stored(line):
        return pltpu.make_async_copy(total.at[level_rows(line)], out_hbm.at[:, line, :], store_sem.at[line])

    group = 16

    @pl.loop(0, lines // group)
    def _(part):
        turned = []
        for i in range(group):
            span = pl.ds(pl.multiple_of((part * group + i) * LANES, LANES), LANES)
            total_here = sums[0][span, :]
            for s in range(1, STREAMS):
                total_here = total_here + sums[s][span, :]
            turned.append(total_here.T[:levels])
        for i in range(group):
            at = level_rows(part * group + i)
            total[at, :] = state[at, :] + turned[i]
        for i in range(group):
            stored(part * group + i).start()

    @pl.loop(0, lines)
    def _(line):
        stored(line).wait()


def add_forcing(got, after_first, capacity):
    tracers, band, levels, tile = after_first.shape
    devices = got.shape[0]
    lines = tracers * band
    out = pl.pallas_call(
        functools.partial(force_kernel, capacity, levels, lines),
        out_shape=jax.ShapeDtypeStruct((levels, lines, tile), jnp.float32),
        in_specs=[ANY, ANY],
        out_specs=ANY,
        scratch_shapes=[
            pltpu.VMEM(got.shape, jnp.float32),
            pltpu.VMEM((devices * capacity, LANES), jnp.float32),
            pltpu.VMEM((devices // 2, LANES), jnp.int32),
            pltpu.SMEM((devices * capacity,), jnp.int32),
            pltpu.VMEM((levels * lines, tile), jnp.float32),
            pltpu.VMEM((levels * lines, tile), jnp.float32),
        ]
        + [pltpu.VMEM((lines * tile + 8, LANES), jnp.float32)] * STREAMS
        + [
            pltpu.SemaphoreType.DMA,
            pltpu.SemaphoreType.DMA((devices // 2,)),
            pltpu.SemaphoreType.DMA,
            pltpu.SemaphoreType.DMA((lines,)),
        ],
        compiler_params=pltpu.CompilerParams(vmem_limit_bytes=VMEM_LIMIT),
        name="add_forcing",
    )(got, after_first.reshape(levels * lines, tile))
    return out.reshape(levels, tracers, band, tile)


def on_device(adjoint_in, courant, mixing, kernel_blocks, sounding_dest, sounding_cell):
    lon_count = lax.axis_size("lon")
    lat_count = lax.axis_size("lat")
    devices = lon_count * lat_count
    held = kernel_blocks.shape[1]
    capacity = 4 * held // devices
    owner = sounding_dest.reshape(held // LANES, LANES)
    cell = sounding_cell.reshape(held // LANES, LANES)
    after_first, got = first_step(
        adjoint_in, courant, mixing, kernel_blocks, owner, cell, lon_count, lat_count, capacity
    )
    forced = add_forcing(got, after_first, capacity)
    swept, sides = second_front(forced, courant, mixing, lon_count, lat_count)
    return last_part(swept, sides, after_first)


def solution(mesh):
    placed = (
        P(None, None, "lat", "lon"),
        P(None, None, "lat", "lon"),
        P(None, "lat", "lon"),
        P(None, ("lon", "lat")),
        P(("lon", "lat"), None),
        P(("lon", "lat")),
    )
    return jax.shard_map(
        on_device,
        mesh=mesh,
        in_specs=placed,
        out_specs=(P(None, None, "lat", "lon"), P(None, "lat", "lon")),
        check_vma=False,
    )
```
